256 devices in a mesh: wa: 128 (over y, x_lo, z, core), ha: 2 (over x_hi).
Axes of the slice: x: 4 (x_hi: 2, x_lo: 2; x = x_hi * 2 + x_lo), y: 4, z: 8, core: 2. Of those that a mesh axis runs over, the one named last changes fastest.
Arguments:
- tokens: bfloat16 [131072, 4096], P('wa'), may hold values from -6 to 6
- expert_ids: int32 [131072, 8], P('wa'), may hold values from 0 to 127, as said below
- keep_mask: int32 [131072, 8], P('wa'), may hold values from 0 to 1, as said below
- route_weight: float32 [131072, 8], P('wa'), may hold values from 0.2 to 1
- gate_weight: bfloat16 [4096, 1536], P('wa', 'ha'), may hold values from -0.09375 to 0.09375
- up_weight: bfloat16 [4096, 1536], P('wa', 'ha'), may hold values from -0.09375 to 0.09375
- down_weight: bfloat16 [4096, 1536], P('wa', 'ha'), may hold values from -0.15625 to 0.15625
Outputs:
- mixed: bfloat16 [131072, 4096], P('wa', 'ha')
The draws below stay inside these ranges and needn't reach their ends.
Inputs may be any that keep to these rules, and one draw needn't show every extreme that they name: `expert_ids`: each row names 8 different experts. keep_mask[t, k] is 1 exactly where fewer than 128 earlier tokens of the same block of 1024 rows name expert_ids[t, k]; in some block 128 tokens naming expert 0 are kept.
All inputs are finite; a program needn't handle non-finite values.
Results may differ from the reference program's by a relative error of at most 0.005.
Values may be sent and summed in bfloat16 or wider, within the bound.
No kernel may reach another device: no remote copies, remote signals or barrier semaphores. Data moves between devices by JAX's collectives and lax.ppermute only.
A program may use at most 128 MiB of HBM per device.

```python
import math
import jax
import jax.numpy as jnp
from jax import lax

D = 4096
HID = 1536
EXPERTS = 128
TOP = 8
TOK_DEV = 1024
CAP = 128
TOKENS = 131072
GLOBAL_CAP = 8192


def routing(key):
    block_count = TOKENS // TOK_DEV
    keys = jax.random.split(jax.random.fold_in(key, 11), 4)
    columns = jnp.arange(EXPERTS, dtype=jnp.int32)
    scores = jax.random.randint(keys[0], (TOKENS, EXPERTS), 0, 65536, dtype=jnp.int32) * EXPERTS + columns[None, :]
    boost_rate = jax.random.randint(keys[1], (block_count,), 1, 9, dtype=jnp.int32)
    forced = jax.random.randint(keys[2], (), 0, block_count, dtype=jnp.int32)
    boost_rate = jnp.where(jnp.arange(block_count, dtype=jnp.int32) == forced, 32, boost_rate)
    coin_flip = jax.random.randint(keys[3], (TOKENS,), 0, 32, dtype=jnp.int32)
    favoured = (coin_flip < jnp.repeat(boost_rate, TOK_DEV)).astype(jnp.int32)
    scores = scores.at[:, 0].add(favoured * 16777216)
    chosen_ids = lax.top_k(scores, TOP)[1].astype(jnp.int32)
    counts = jnp.zeros((TOKENS, EXPERTS), jnp.int32)
    for column in range(TOP):
        counts = counts + (chosen_ids[:, column:column + 1] == columns[None, :]).astype(jnp.int32)
    blocked = counts.reshape(block_count, TOK_DEV, EXPERTS)
    earlier = (jnp.cumsum(blocked, axis=1).astype(jnp.int32) - blocked).reshape(TOKENS, EXPERTS)
    position = jnp.take_along_axis(earlier, chosen_ids, axis=1)
    keeping = (position < CAP).astype(jnp.int32)
    return (chosen_ids, keeping)


def draw_expert_ids(key, part):
    return routing(key)[0]


def draw_keep_mask(key, part):
    return routing(key)[1]


def block_levels(own_key, dims, cuts, low, top_value):
    level, own = 1.0, jax.random.fold_in(own_key, 6)
    for axis_at, blocks in cuts:
        heights = jnp.exp(jax.random.uniform(jax.random.fold_in(own, axis_at), (blocks,), jnp.float32, low / len(cuts), top_value / len(cuts)))
        level = level * jnp.repeat(heights, dims[axis_at] // blocks).reshape([-1 if axis == axis_at else 1 for axis in range(len(dims))])
    return level


def normal_values(own_key, dims, spread, limit, cuts=(), kind=jnp.bfloat16):
    drawn = jax.random.normal(own_key, dims, jnp.float32) * spread
    if len(cuts) > 0:
        drawn = block_levels(own_key, dims, cuts, -0.22, 0.18) * drawn
    return jnp.clip(drawn, min=-limit, max=limit).astype(kind)


def setup_inputs(seed: int = 0) -> dict:
    splits = jax.random.split(jax.random.key(seed), 8)
    tokens = normal_values(splits[0], (TOKENS, D), 1.0, 6.0, ((0, 128),))
    expert_ids = draw_expert_ids(jax.random.fold_in(splits[7], 71), 0)
    keep_mask = draw_keep_mask(jax.random.fold_in(splits[7], 71), 0)
    route_weight = jnp.clip(jnp.exp(math.log(1.0) - 1.609438 * jax.random.uniform(splits[3], (TOKENS, TOP), jnp.float32) ** block_levels(splits[3], (TOKENS, TOP), ((0, 128),), -0.2, 0.2)), 0.2, 1.0)
    gate_weight = normal_values(splits[4], (D, HID), D ** -0.5, 0.09375, ((0, 128), (1, 2)))
    up_weight = normal_values(splits[5], (D, HID), D ** -0.5, 0.09375, ((0, 128), (1, 2)))
    down_weight = normal_values(splits[6], (D, HID), HID ** -0.5, 0.15625, ((0, 128), (1, 2)))
    return dict(tokens=tokens, expert_ids=expert_ids, keep_mask=keep_mask, route_weight=route_weight, gate_weight=gate_weight, up_weight=up_weight, down_weight=down_weight)


def reference(tokens, expert_ids, keep_mask, route_weight, gate_weight, up_weight, down_weight):
    block_count = TOKENS // TOK_DEV
    matches = (expert_ids == 0) & (keep_mask == 1)
    chosen = jnp.any(matches, axis=1).astype(jnp.int32).reshape(block_count, TOK_DEV)
    route_sum = jnp.sum(jnp.where(matches, route_weight, jnp.float32(0.0)), axis=1).astype(jnp.float32)
    route_sum = route_sum.reshape(block_count, TOK_DEV)
    position = (jnp.cumsum(chosen, axis=1).astype(jnp.int32) - chosen).astype(jnp.int32)
    counted = jnp.sum(chosen, axis=1).astype(jnp.int32)
    earlier = (jnp.cumsum(counted).astype(jnp.int32) - counted).astype(jnp.int32)
    admitted = chosen * ((earlier[:, None] + position) < GLOBAL_CAP).astype(jnp.int32)
    slot_ids = jnp.arange(CAP, dtype=jnp.int32)

    def one_block(packed):
        block_rows, block_pos, block_adm, block_route = packed
        dispatch = (block_pos[None, :] == slot_ids[:, None]) & (block_adm[None, :] == 1)
        slot_rows = jnp.dot(dispatch.astype(jnp.bfloat16), block_rows, preferred_element_type=jnp.float32).astype(jnp.bfloat16)
        gate_sum = jnp.dot(slot_rows, gate_weight, preferred_element_type=jnp.float32)
        up_sum = jnp.dot(slot_rows, up_weight, preferred_element_type=jnp.float32)
        hidden = (jax.nn.silu(gate_sum) * up_sum).astype(jnp.bfloat16)
        expert_out = jnp.dot(hidden, down_weight.T, preferred_element_type=jnp.float32)
        combine_map = jnp.where(dispatch.T, block_route[:, None], jnp.float32(0.0)).astype(jnp.float32)
        mixed_block = jnp.dot(combine_map, expert_out, precision=lax.Precision.HIGHEST, preferred_element_type=jnp.float32)
        return mixed_block.astype(jnp.bfloat16)

    mixed = lax.map(one_block, (tokens.reshape(block_count, TOK_DEV, D), position, admitted, route_sum))
    return mixed.reshape(TOKENS, D)
```

```python
import jax
import jax.numpy as jnp
from jax import lax
from jax.experimental import pallas as pl
from jax.experimental.pallas import tpu as pltpu
from jax.sharding import Mesh
from jax.sharding import PartitionSpec as P

CAP = 128
WA = ("y", "xl", "z", "c")
NY, NZ = 4, 8
F32, BF16, I32 = jnp.float32, jnp.bfloat16, jnp.int32
VMEM = pltpu.VMEM
LIMIT = 50 << 20


def whole(memory_space=VMEM):
    return pl.BlockSpec(memory_space=memory_space)


def ring(axis, n, k):
    return lambda a: lax.ppermute(a, axis, [(i, (i + k) % n) for i in range(n)])


def Z(k):
    return ring("z", NZ, k)


def Y(k):
    return ring("y", NY, k)


def C(a):
    return lax.ppermute(a, "c", [(0, 1), (1, 0)])


def XL(a):
    return lax.ppermute(a, "xl", [(0, 1), (1, 0)])


def HA(a):
    return lax.ppermute(a, "ha", [(0, 1), (1, 0)])


def X(k):
    def at(x):
        return (x % 2) * 2 + x // 2

    pairs = [(at(x), at((x + k) % 4)) for x in range(4)]
    return lambda a: lax.ppermute(a, ("xl", "ha"), pairs)


def route_body(ids, keep, rw, info, cnt):
    hit = (ids[...] == 0) & (keep[...] == 1)
    chosen = jnp.max(jnp.where(hit, 1.0, 0.0), axis=0, keepdims=True)
    route = jnp.sum(jnp.where(hit, rw[...], 0.0), axis=0, keepdims=True)
    n = chosen.shape[1]
    row = lax.broadcasted_iota(I32, (n, n), 0)
    col = lax.broadcasted_iota(I32, (n, n), 1)
    before = jnp.where(row < col, 1.0, 0.0).astype(BF16)
    ones = jnp.broadcast_to(chosen, (16, n)).astype(BF16)
    position = jnp.dot(ones, before, preferred_element_type=F32)[:1]
    info[0:1, :] = position
    info[1:2, :] = chosen
    info[2:3, :] = route
    info[3:8, :] = jnp.zeros((5, n), F32)
    total = jnp.sum(chosen, axis=1, keepdims=True)
    cnt[...] = jnp.broadcast_to(total, cnt.shape)


def routing(ids, keep, rw):
    n = ids.shape[1]
    return pl.pallas_call(
        route_body,
        out_shape=(jax.ShapeDtypeStruct((8, n), F32), jax.ShapeDtypeStruct((8, 384), F32)),
        in_specs=[whole()] * 3,
        out_specs=(whole(), whole()),
        cost_estimate=pl.CostEstimate(flops=2 * 16 * n * n, bytes_accessed=4 * 32 * n, transcendentals=0),
        name="routing",
    )(ids, keep, rw)


def table(info):
    slot = lax.broadcasted_iota(I32, (CAP, info.shape[1]), 0).astype(F32)
    return (info[0:1, :] == slot) & (info[1:2, :] > 0.5)


def gather_body(where, tokens, info, out, slot_route):
    block = pl.program_id(0)
    picked = table(info)
    rows = jnp.dot(picked.astype(BF16), tokens[...], preferred_element_type=F32).astype(BF16)
    ky = lax.rem(block - where[0] + NY, NY)
    yi = jnp.where(ky == 0, 0, jnp.where(ky == 3, 1, jnp.where(ky == 1, 2, 3)))
    for z in range(NZ):
        kz = lax.rem(z - where[1] + NZ, NZ)
        zi = jnp.where(kz == 0, 0, jnp.where(kz <= 3, 2 * kz, jnp.where(kz == 4, 7, 15 - 2 * kz)))
        piece = jnp.concatenate([rows[:, z * 64 : z * 64 + 64], rows[:, 512 + z * 64 : 576 + z * 64]], axis=1)
        out[:, pl.ds(pl.multiple_of((yi * NZ + zi) * 128, 128), 128)] = piece

    @pl.when(block == 0)
    def _():
        got = jnp.sum(jnp.where(picked, info[2:3, :], 0.0), axis=1, keepdims=True)
        slot_route[...] = jnp.broadcast_to(got, slot_route.shape)


def gather_rows(where, tokens, info):
    n, d = tokens.shape
    return pl.pallas_call(
        gather_body,
        out_shape=(jax.ShapeDtypeStruct((CAP, d), BF16), jax.ShapeDtypeStruct((CAP, 128), F32)),
        grid_spec=pltpu.PrefetchScalarGridSpec(
            num_scalar_prefetch=1,
            grid=(NY,),
            in_specs=[
                pl.BlockSpec((n, d // NY), lambda i, w: (0, i)),
                pl.BlockSpec((8, n), lambda i, w: (0, 0)),
            ],
            out_specs=(
                pl.BlockSpec((CAP, d), lambda i, w: (0, 0)),
                pl.BlockSpec((CAP, 128), lambda i, w: (0, 0)),
            ),
        ),
        compiler_params=pltpu.CompilerParams(vmem_limit_bytes=24 << 20),
        cost_estimate=pl.CostEstimate(flops=2 * CAP * n * d, bytes_accessed=2 * n * d, transcendentals=0),
        name="gather_rows",
    )(where, tokens, info)


def gate_up_body(n_weights, *refs):
    weights, rows = refs[:n_weights], refs[n_weights : n_weights + 6]
    own, other, x_all = refs[n_weights + 6 :]
    xo, xc, xa, xb, xac, xbc = rows
    x_all[0:128, :] = xo[...]
    x_all[128:256, :] = xc[...]
    x_all[256:320, :] = xb[...]
    x_all[320:384, :] = xa[...]
    x_all[384:448, :] = xbc[...]
    x_all[448:512, :] = xac[...]
    total = jnp.zeros((512, 384), F32)
    for ref, (start, size) in zip(weights, SPANS):
        total += jnp.dot(x_all[:, start : start + size], ref[0:size, :], preferred_element_type=F32)
    gate, up = total[:, :192], total[:, 192:]
    hidden = (gate * jax.nn.sigmoid(gate) * up).astype(BF16)
    own[...] = hidden[:256]
    other[...] = hidden[256:]


SPANS = []
for _i in range(3):
    SPANS += [(_i * 1024, 640), (_i * 1024 + 640, 384)]
SPANS += [(3072, 384), (3072 + 384, 256), (3072 + 640, 256), (3072 + 896, 128)]


def gate_up(weights, rows):
    half = jax.ShapeDtypeStruct((256, 192), BF16)
    return pl.pallas_call(
        lambda *refs: gate_up_body(len(weights), *refs),
        out_shape=(half, half),
        in_specs=[whole()] * (len(weights) + len(rows)),
        out_specs=(whole(), whole()),
        scratch_shapes=[VMEM((512, 4096), BF16)],
        compiler_params=pltpu.CompilerParams(vmem_limit_bytes=LIMIT),
        cost_estimate=pl.CostEstimate(flops=2 * 512 * 4096 * 384, bytes_accessed=8 << 20, transcendentals=512 * 192),
        name="gate_up",
    )(*weights, *rows)


def down_body(hidden, *refs):
    pieces, keep, send = refs[:-2], refs[-2], refs[-1]

    def dot(w):
        return lax.dot_general(hidden[...], w, (((1,), (1,)), ((), ())), preferred_element_type=F32)

    for r in range(NZ):
        at = slice(r * 128, r * 128 + 128)
        if r == 4:
            keep[:, at] = dot(pieces[4][...])
            send[:, at] = dot(pieces[8][...]).astype(BF16)
        else:
            both = dot(pieces[r][...])
            keep[:, at] = both[:, :128]
            send[:, at] = both[:, 128:].astype(BF16)


def down(hidden, pieces):
    return pl.pallas_call(
        down_body,
        out_shape=(jax.ShapeDtypeStruct((256, 1024), F32), jax.ShapeDtypeStruct((256, 1024), BF16)),
        in_specs=[whole()] * (1 + len(pieces)),
        out_specs=(whole(), whole()),
        compiler_params=pltpu.CompilerParams(vmem_limit_bytes=LIMIT),
        cost_estimate=pl.CostEstimate(flops=2 * 256 * 768 * 2048, bytes_accessed=5 << 20, transcendentals=0),
        name="down",
    )(hidden, *pieces)


def mix_body(where, mine, theirs, info, slot_route, out, slots):
    @pl.when(pl.program_id(0) == 0)
    def _():
        slot = lax.broadcasted_iota(I32, (CAP, 1), 0)
        scale = jnp.where(slot < where[2], slot_route[:, 0:1], 0.0)
        src = lax.broadcasted_iota(I32, (512, 512), 0)
        dst = lax.broadcasted_iota(I32, (512, 512), 1)
        moved = (src + where[1] * 64) & 511
        order = jnp.where(moved == dst, 1.0, 0.0).astype(BF16)
        for ref, column in ((mine, where[0]), (theirs, 1 - where[0])):
            scaled = (ref[...] * scale).astype(BF16)
            for y in range(2):
                part = jnp.concatenate(
                    [scaled[:, r * 128 + y * 64 : r * 128 + y * 64 + 64] for r in range(NZ)], axis=1
                )
                placed = jnp.dot(part, order, preferred_element_type=F32).astype(BF16)
                slots[:, pl.ds(pl.multiple_of(y * 1024 + column * 512, 512), 512)] = placed

    picked = table(info).astype(BF16)
    mixed = lax.dot_general(picked, slots[...], (((0,), (0,)), ((), ())), preferred_element_type=F32)
    out[...] = mixed.astype(BF16)


def mix(where, mine, theirs, info, slot_route):
    n, step = info.shape[1], 256
    return pl.pallas_call(
        mix_body,
        out_shape=jax.ShapeDtypeStruct((n, 2048), BF16),
        grid_spec=pltpu.PrefetchScalarGridSpec(
            num_scalar_prefetch=1,
            grid=(n // step,),
            in_specs=[
                pl.BlockSpec((CAP, 1024), lambda i, w: (0, 0)),
                pl.BlockSpec((CAP, 1024), lambda i, w: (0, 0)),
                pl.BlockSpec((8, step), lambda i, w: (0, i)),
                pl.BlockSpec((CAP, 128), lambda i, w: (0, 0)),
            ],
            out_specs=pl.BlockSpec((step, 2048), lambda i, w: (i, 0)),
            scratch_shapes=[VMEM((CAP, 2048), BF16)],
        ),
        compiler_params=pltpu.CompilerParams(vmem_limit_bytes=24 << 20),
        cost_estimate=pl.CostEstimate(flops=2 * n * CAP * 2048, bytes_accessed=6 << 20, transcendentals=0),
        name="mix",
    )(where, mine, theirs, info, slot_route)


def z_ring(u, cut):
    back, ahead, out = u, u, [u]
    for _ in range(3):
        back, ahead = Z(1)(back), Z(-1)(ahead)
        out += [back, ahead]
    return out, (Z(1)(back[:cut]), Z(-1)(ahead[cut:]))


def y_ring(u, cut):
    back, ahead = Y(1)(u), Y(-1)(u)
    return back, ahead, Y(1)(back[:cut]), Y(-1)(ahead[cut:])


def with_counts(units):
    return jnp.concatenate([u[:128] for u in units] + [u[128:] for u in units], axis=0)


def per_device(tokens, expert_ids, keep_mask, route_weight, gate_weight, up_weight, down_weight):
    y, xl, z, c, ha = (lax.axis_index(a) for a in ("y", "xl", "z", "c", "ha"))
    info, cnt = routing(expert_ids.T, keep_mask.T, route_weight.T)

    quarters = jnp.concatenate(
        [gate_weight.reshape(32, 4, 192).swapaxes(0, 1), up_weight.reshape(32, 4, 192).swapaxes(0, 1)], axis=2
    )
    counted = jnp.broadcast_to(cnt.astype(BF16)[None], (4, 8, 384))
    arrived = lax.all_to_all(
        jnp.concatenate([quarters, counted], axis=1), ("xl", "c"), split_axis=0, concat_axis=0, tiled=True
    )
    lane = lax.broadcasted_iota(I32, (8, 384), 1)
    tile = jnp.zeros((8, 384), BF16)
    for j in range(4):
        tile = jnp.where(lane == j, arrived[j, 32:40], tile)
    unit = jnp.concatenate([arrived[:, :32].reshape(128, 384), tile], axis=0)

    rows = lax.all_gather(down_weight, ("xl", "c"), axis=0, tiled=False)
    rows = lax.dynamic_slice_in_dim(rows, 2 * c, 2, axis=0).reshape(64, 768)
    d_back, d_ahead, d_far0, d_far1 = y_ring(rows, 32)
    turned = [rows, d_ahead, jnp.concatenate([d_far0, d_far1], axis=0), d_back]
    shift = lax.rem(2 * ha - y + NY, NY)
    ordered = []
    for j in range(4):
        pick = turned[j]
        for s in range(1, 4):
            pick = jnp.where(shift == s, turned[(j + s) % 4], pick)
        ordered.append(pick)
    d_near, d_last = z_ring(jnp.concatenate(ordered, axis=0), 128)
    pieces = [d_near[0], d_near[2], d_near[4], d_near[6], d_last[0], d_near[5], d_near[3], d_near[1], d_last[1]]

    g_near, g_last = z_ring(unit, 64)
    first = with_counts(g_near[:5])
    second = with_counts(g_near[5:] + [jnp.concatenate(g_last, axis=0)])
    f_back, f_ahead, f_far0, f_far1 = y_ring(first, 384)
    s_back, s_ahead, s_far0, s_far1 = y_ring(second, 256)

    slot_rows, slot_route = gather_rows(jnp.stack([y, z]), tokens, info)
    xa, xb = X(1)(slot_rows[64:]), X(-1)(slot_rows[:64])
    x_rows = [slot_rows, C(slot_rows), xa, xb, C(xa), C(xb)]
    weights = [first, second, f_back, s_back, f_ahead, s_ahead, f_far0, f_far1, s_far0, s_far1]
    h_own, h_other = gate_up(weights, x_rows)
    h_near = XL(h_other)
    swapped = C(
        jnp.concatenate(
            [jnp.concatenate([h_own[128:], h_own[:128]], 0), jnp.concatenate([h_near[128:], h_near[:128]], 0)], axis=1
        )
    )
    h_core, h_far = swapped[:, :192], swapped[:, 192:]
    c0, x0 = c == 0, xl == 0
    here = (jnp.where(c0, h_own, h_core), jnp.where(c0, h_core, h_own))
    there = (jnp.where(c0, h_near, h_far), jnp.where(c0, h_far, h_near))
    hidden = jnp.concatenate(
        [jnp.where(x0, a, b) for a, b in zip(here, there)] + [jnp.where(x0, b, a) for a, b in zip(here, there)], axis=1
    )
    keep, send = down(hidden, pieces)
    total = keep + HA(send).astype(F32)
    theirs = C(total[128:])

    counts = []
    for near, late in ((first[640:], second[384:]), (f_back[640:], s_back[384:]), (f_ahead[640:], s_ahead[384:]), (f_far1[256:], s_far1[128:])):
        counts += [near.reshape(5, 8, 384)[:, 0, :4], late.reshape(3, 8, 384)[:, 0, :4]]
    counts = jnp.concatenate(counts, axis=0).astype(I32)
    entry = lax.broadcasted_iota(I32, (32, 4), 0)
    quad = lax.broadcasted_iota(I32, (32, 4), 1)
    yi, zi = entry // 8, entry % 8
    ky = jnp.where(yi == 0, 0, jnp.where(yi == 1, 3, jnp.where(yi == 2, 1, 2)))
    kz = jnp.where(zi == 7, 4, jnp.where(zi % 2 == 0, zi // 2, 8 - (zi + 1) // 2))
    block = ((y + ky) % 4) * 32 + (quad // 2) * 16 + ((z + kz) % 8) * 2 + quad % 2
    me = y * 32 + xl * 16 + z * 2 + c
    earlier = jnp.sum(jnp.where(block < me, counts, 0))
    capacity = lax.axis_size(WA) * CAP // 2
    return mix(jnp.stack([c, z, capacity - earlier]), total[:128], theirs, info, slot_route)


def solution(mesh):
    finer = Mesh(mesh.devices.reshape(NY, 2, NZ, 2, mesh.shape["ha"]), ("y", "xl", "z", "c", "ha"))
    placed = (P(WA, None),) * 4 + (P(WA, "ha"),) * 3
    return jax.shard_map(per_device, mesh=finer, in_specs=placed, out_specs=P(WA, "ha"), check_vma=False)
```

```python
import jax
import jax.numpy as jnp
from jax import lax
from jax.experimental import pallas as pl
from jax.experimental.pallas import tpu as pltpu
from jax.sharding import Mesh
from jax.sharding import PartitionSpec as P

CAP = 128
WA = ("y", "xl", "z", "c")
NY, NZ = 4, 8
F32, BF16, I32 = jnp.float32, jnp.bfloat16, jnp.int32
VMEM = pltpu.VMEM


def whole(memory_space=VMEM):
    return pl.BlockSpec(memory_space=memory_space)


def ring(axis, n, k):
    return lambda a: lax.ppermute(a, axis, [(i, (i + k) % n) for i in range(n)])


def Z(k):
    return ring("z", NZ, k)


def Y(k):
    return ring("y", NY, k)


def C(a):
    return lax.ppermute(a, "c", [(0, 1), (1, 0)])


def XL(a):
    return lax.ppermute(a, "xl", [(0, 1), (1, 0)])


def HA(a):
    return lax.ppermute(a, "ha", [(0, 1), (1, 0)])


def X(k):
    def at(x):
        return (x % 2) * 2 + x // 2

    pairs = [(at(x), at((x + k) % 4)) for x in range(4)]
    return lambda a: lax.ppermute(a, ("xl", "ha"), pairs)


def prep_body(ids, keep, rw, gate, up, down_rows, info, packed):
    hit = (ids[...] == 0) & (keep[...] == 1)
    chosen = jnp.max(jnp.where(hit, 1.0, 0.0), axis=0, keepdims=True)
    route = jnp.sum(jnp.where(hit, rw[...], 0.0), axis=0, keepdims=True)
    n = chosen.shape[1]
    row = lax.broadcasted_iota(I32, (n, n), 0)
    col = lax.broadcasted_iota(I32, (n, n), 1)
    before = jnp.where(row < col, 1.0, 0.0).astype(BF16)
    ones = jnp.broadcast_to(chosen, (16, n)).astype(BF16)
    position = jnp.dot(ones, before, preferred_element_type=F32)[:1]
    info[0:1, :] = position
    info[1:2, :] = chosen
    info[2:3, :] = route
    info[3:8, :] = jnp.zeros((5, n), F32)
    total = jnp.sum(chosen, axis=1, keepdims=True)
    for q in range(4):
        at = slice(q * 192, q * 192 + 192)
        packed[q, 0:32, :] = jnp.concatenate([gate[:, at], up[:, at]], axis=1)
        packed[q, 32:40, :] = jnp.broadcast_to(total, (8, 384)).astype(BF16)
        packed[q, 40:72, :] = down_rows[:, :384]
        packed[q, 72:104, :] = down_rows[:, 384:]


def prep(ids, keep, rw, gate, up, down_rows):
    n = ids.shape[1]
    return pl.pallas_call(
        prep_body,
        out_shape=(jax.ShapeDtypeStruct((8, n), F32), jax.ShapeDtypeStruct((4, 104, 384), BF16)),
        in_specs=[whole()] * 6,
        out_specs=(whole(), whole()),
        compiler_params=pltpu.CompilerParams(vmem_limit_bytes=12 << 20),
        cost_estimate=pl.CostEstimate(flops=2 * 16 * n * n, bytes_accessed=4 * 32 * n, transcendentals=0),
        name="prep",
    )(ids, keep, rw, gate, up, down_rows)


def table(info):
    slot = lax.broadcasted_iota(I32, (CAP, info.shape[1]), 0).astype(F32)
    return (info[0:1, :] == slot) & (info[1:2, :] > 0.5)


def gather_body(where, tokens, info, out, slot_route):
    block = pl.program_id(0)
    picked = table(info)
    rows = jnp.dot(picked.astype(BF16), tokens[...], preferred_element_type=F32).astype(BF16)
    ky = lax.rem(block - where[0] + NY, NY)
    yi = jnp.where(ky == 0, 0, jnp.where(ky == 3, 1, jnp.where(ky == 1, 2, 3)))
    for z in range(NZ):
        kz = lax.rem(z - where[1] + NZ, NZ)
        zi = jnp.where(kz == 0, 0, jnp.where(kz <= 3, 2 * kz, jnp.where(kz == 4, 7, 15 - 2 * kz)))
        piece = jnp.concatenate([rows[:, z * 64 : z * 64 + 64], rows[:, 512 + z * 64 : 576 + z * 64]], axis=1)
        out[:, pl.ds(pl.multiple_of((yi * NZ + zi) * 128, 128), 128)] = piece

    @pl.when(block == 0)
    def _():
        got = jnp.sum(jnp.where(picked, info[2:3, :], 0.0), axis=1, keepdims=True)
        slot_route[...] = jnp.broadcast_to(got, slot_route.shape)


def gather_rows(where, tokens, info):
    n, d = tokens.shape
    return pl.pallas_call(
        gather_body,
        out_shape=(jax.ShapeDtypeStruct((CAP, d), BF16), jax.ShapeDtypeStruct((CAP, 128), F32)),
        grid_spec=pltpu.PrefetchScalarGridSpec(
            num_scalar_prefetch=1,
            grid=(NY,),
            in_specs=[
                pl.BlockSpec((n, d // NY), lambda i, w: (0, i)),
                pl.BlockSpec((8, n), lambda i, w: (0, 0)),
            ],
            out_specs=(
                pl.BlockSpec((CAP, d), lambda i, w: (0, 0)),
                pl.BlockSpec((CAP, 128), lambda i, w: (0, 0)),
            ),
        ),
        compiler_params=pltpu.CompilerParams(vmem_limit_bytes=24 << 20),
        cost_estimate=pl.CostEstimate(flops=2 * CAP * n * d, bytes_accessed=2 * n * d, transcendentals=0),
        name="gather_rows",
    )(where, tokens, info)


def gate_up_body(n_weights, *refs):
    weights, rows = refs[:n_weights], refs[n_weights : n_weights + 6]
    own, other, x_all = refs[n_weights + 6 :]
    xo, xc, xa, xb, xac, xbc = rows
    x_all[0:128, :] = xo[...]
    x_all[128:256, :] = xc[...]
    x_all[256:320, :] = xb[...]
    x_all[320:384, :] = xa[...]
    x_all[384:448, :] = xbc[...]
    x_all[448:512, :] = xac[...]
    total = jnp.zeros((512, 384), F32)
    for ref, (start, size) in zip(weights, SPANS):
        total += jnp.dot(x_all[:, start : start + size], ref[0:size, :], preferred_element_type=F32)
    gate, up = total[:, :192], total[:, 192:]
    hidden = (gate * jax.nn.sigmoid(gate) * up).astype(BF16)
    own[...] = hidden[:256]
    other[...] = hidden[256:]


SPANS = []
for _i in range(3):
    SPANS += [(_i * 1024, 640), (_i * 1024 + 640, 384)]
SPANS += [(3072, 384), (3072 + 384, 256), (3072 + 640, 256), (3072 + 896, 128)]


def gate_up(weights, rows):
    half = jax.ShapeDtypeStruct((256, 192), BF16)
    return pl.pallas_call(
        lambda *refs: gate_up_body(len(weights), *refs),
        out_shape=(half, half),
        in_specs=[whole()] * (len(weights) + len(rows)),
        out_specs=(whole(), whole()),
        scratch_shapes=[VMEM((512, 4096), BF16)],
        compiler_params=pltpu.CompilerParams(vmem_limit_bytes=20 << 20),
        cost_estimate=pl.CostEstimate(flops=2 * 512 * 4096 * 384, bytes_accessed=8 << 20, transcendentals=512 * 192),
        name="gate_up",
    )(*weights, *rows)


def down_body(hidden, *refs):
    pieces, out = refs[:-1], refs[-1]

    def dot(k, w):
        return lax.dot_general(
            hidden[:, k * 384 : k * 384 + 384], w, (((1,), (1,)), ((), ())), preferred_element_type=F32
        )

    for r in range(NZ):
        near, far = (pieces[4], pieces[8]) if r == 4 else (pieces[r], pieces[r])
        base = 0 if r == 4 else 256
        total = dot(0, near[0:128]) + dot(1, near[128:256])
        total += dot(2, far[base : base + 128]) + dot(3, far[base + 128 : base + 256])
        out[:, r * 128 : r * 128 + 128] = total


def down(hidden, pieces):
    return pl.pallas_call(
        down_body,
        out_shape=jax.ShapeDtypeStruct((256, 1024), F32),
        in_specs=[whole()] * (1 + len(pieces)),
        out_specs=whole(),
        compiler_params=pltpu.CompilerParams(vmem_limit_bytes=12 << 20),
        cost_estimate=pl.CostEstimate(flops=2 * 256 * 1536 * 1024, bytes_accessed=5 << 20, transcendentals=0),
        name="down",
    )(hidden, *pieces)


def mix_body(where, mine, theirs, info, slot_route, out, slots):
    @pl.when(pl.program_id(0) == 0)
    def _():
        slot = lax.broadcasted_iota(I32, (CAP, 1), 0)
        scale = jnp.where(slot < where[2], slot_route[:, 0:1], 0.0)
        src = lax.broadcasted_iota(I32, (512, 512), 0)
        dst = lax.broadcasted_iota(I32, (512, 512), 1)
        moved = (src + where[1] * 64) & 511
        order = jnp.where(moved == dst, 1.0, 0.0).astype(BF16)
        for ref, column in ((mine, where[0]), (theirs, 1 - where[0])):
            scaled = (ref[...] * scale).astype(BF16)
            for y in range(2):
                part = jnp.concatenate(
                    [scaled[:, r * 128 + y * 64 : r * 128 + y * 64 + 64] for r in range(NZ)], axis=1
                )
                placed = jnp.dot(part, order, preferred_element_type=F32).astype(BF16)
                slots[:, pl.ds(pl.multiple_of(y * 1024 + column * 512, 512), 512)] = placed

    picked = table(info).astype(BF16)
    mixed = lax.dot_general(picked, slots[...], (((0,), (0,)), ((), ())), preferred_element_type=F32)
    out[...] = mixed.astype(BF16)


def mix(where, mine, theirs, info, slot_route):
    n, step = info.shape[1], 256
    return pl.pallas_call(
        mix_body,
        out_shape=jax.ShapeDtypeStruct((n, 2048), BF16),
        grid_spec=pltpu.PrefetchScalarGridSpec(
            num_scalar_prefetch=1,
            grid=(n // step,),
            in_specs=[
                pl.BlockSpec((CAP, 1024), lambda i, w: (0, 0)),
                pl.BlockSpec((CAP, 1024), lambda i, w: (0, 0)),
                pl.BlockSpec((8, step), lambda i, w: (0, i)),
                pl.BlockSpec((CAP, 128), lambda i, w: (0, 0)),
            ],
            out_specs=pl.BlockSpec((step, 2048), lambda i, w: (i, 0)),
            scratch_shapes=[VMEM((CAP, 2048), BF16)],
        ),
        compiler_params=pltpu.CompilerParams(vmem_limit_bytes=24 << 20),
        cost_estimate=pl.CostEstimate(flops=2 * n * CAP * 2048, bytes_accessed=6 << 20, transcendentals=0),
        name="mix",
    )(where, mine, theirs, info, slot_route)


def with_counts(units):
    return jnp.concatenate([u[:128] for u in units] + [u[128:] for u in units], axis=0)


def together(*arrays):
    return lax.optimization_barrier(arrays)


def flipped(a):
    return jnp.concatenate([a[128:], a[:128]], axis=0)


def HIDDEN_FAR(a):
    pairs = [(k, 3 - k) for k in range(4)]
    return lax.ppermute(a, ("xl", "ha"), pairs)


def per_device(tokens, expert_ids, keep_mask, route_weight, gate_weight, up_weight, down_weight):
    y, xl, z, c, ha = (lax.axis_index(a) for a in ("y", "xl", "z", "c", "ha"))
    info, packed = prep(expert_ids.T, keep_mask.T, route_weight.T, gate_weight, up_weight, down_weight)
    arrived = lax.all_to_all(packed, ("xl", "c"), split_axis=0, concat_axis=0, tiled=True)
    slot_rows, slot_route = gather_rows(jnp.stack([y, z]), tokens, info)

    lane = lax.broadcasted_iota(I32, (8, 384), 1)
    tile = jnp.zeros((8, 384), BF16)
    for j in range(4):
        tile = jnp.where(lane == j, arrived[j, 32:40], tile)
    unit = jnp.concatenate([arrived[:, :32].reshape(128, 384), tile], axis=0)
    picked = lax.dynamic_slice_in_dim(arrived, 2 * c, 2, axis=0)[:, 40:]
    rows = jnp.concatenate([picked[0, :32], picked[1, :32], picked[0, 32:], picked[1, 32:]], axis=0)

    b1, a1 = Z(1)(unit), Z(-1)(unit)
    d_back, d_ahead = Y(1)(rows), Y(-1)(rows)
    b1, a1, d_back, d_ahead = together(b1, a1, d_back, d_ahead)
    b2, a2 = Z(1)(b1), Z(-1)(a1)
    d_far = Y(1)(d_back[:64]), Y(-1)(d_ahead[64:])
    b2, a2, d_far0, d_far1 = together(b2, a2, *d_far)

    turned = [rows, d_ahead, jnp.concatenate([d_far0, d_far1], axis=0), d_back]
    shift = lax.rem(2 * ha - y + NY, NY)
    ordered = []
    for j in range(4):
        pick = turned[j]
        for s in range(1, 4):
            pick = jnp.where(shift == s, turned[(j + s) % 4], pick)
        ordered.append(pick)

    def halves(p, q):
        return jnp.concatenate([p[:64], q[:64], p[64:], q[64:]], axis=0)

    d_swap = HA(halves(ordered[2], ordered[3]))
    b3, a3 = Z(1)(b2), Z(-1)(a2)
    first = with_counts([unit, b1, a1, b2, a2])
    f_back, f_ahead = Y(1)(first), Y(-1)(first)
    b3, a3, d_swap = together(b3, a3, d_swap)

    d0 = jnp.concatenate([halves(ordered[0], ordered[1]), d_swap], axis=0)
    e0, e1 = Z(1)(b3[:64]), Z(-1)(a3[64:])
    db1, da1 = Z(1)(d0), Z(-1)(d0)
    e0, e1, f_back, f_ahead = together(e0, e1, f_back, f_ahead)
    second = with_counts([b3, a3, jnp.concatenate([e0, e1], axis=0)])
    f_far0, f_far1 = Y(1)(f_back[:384]), Y(-1)(f_ahead[384:])
    s_back, s_ahead = Y(1)(second), Y(-1)(second)
    s_back, s_ahead, db1, da1 = together(s_back, s_ahead, db1, da1)
    s_far0, s_far1 = Y(1)(s_back[:256]), Y(-1)(s_ahead[256:])
    db2, da2 = Z(1)(db1), Z(-1)(da1)

    xa, xb = X(1)(slot_rows[64:]), X(-1)(slot_rows[:64])
    x_rows = [slot_rows, C(slot_rows), xa, xb, C(xa), C(xb)]
    weights = [first, second, f_back, s_back, f_ahead, s_ahead, f_far0, f_far1, s_far0, s_far1]
    h_own, h_other = gate_up(weights, x_rows)
    db3, da3 = Z(1)(db2), Z(-1)(da2)
    h_near, h_ha, h_far = XL(h_other), HA(h_own), HIDDEN_FAR(h_other)
    de0, de1 = Z(1)(db3[:256]), Z(-1)(da3[256:])
    mine = (h_own, h_near, h_ha, h_far)
    core = C(jnp.concatenate([flipped(h) for h in mine], axis=1))
    theirs = [core[:, k * 192 : k * 192 + 192] for k in range(4)]
    c0, x0 = c == 0, xl == 0
    hidden = []
    for k in (0, 2):
        here = (jnp.where(c0, mine[k], theirs[k]), jnp.where(c0, theirs[k], mine[k]))
        there = (jnp.where(c0, mine[k + 1], theirs[k + 1]), jnp.where(c0, theirs[k + 1], mine[k + 1]))
        hidden += [jnp.where(x0, p, q) for p, q in zip(here, there)]
        hidden += [jnp.where(x0, q, p) for p, q in zip(here, there)]
    pieces = [d0, da1, da2, da3, de0, db3, db2, db1, de1]
    total = down(jnp.concatenate(hidden, axis=1), pieces)
    other = C(total[128:])

    counts = []
    for near, late in (
        (first[640:], second[384:]),
        (f_back[640:], s_back[384:]),
        (f_ahead[640:], s_ahead[384:]),
        (f_far1[256:], s_far1[128:]),
    ):
        counts += [near.reshape(5, 8, 384)[:, 0, :4], late.reshape(3, 8, 384)[:, 0, :4]]
    counts = jnp.concatenate(counts, axis=0).astype(I32)
    entry = lax.broadcasted_iota(I32, (32, 4), 0)
    quad = lax.broadcasted_iota(I32, (32, 4), 1)
    yi, zi = entry // 8, entry % 8
    ky = jnp.where(yi == 0, 0, jnp.where(yi == 1, 3, jnp.where(yi == 2, 1, 2)))
    kz = jnp.where(zi == 7, 4, jnp.where(zi % 2 == 0, zi // 2, 8 - (zi + 1) // 2))
    block = ((y + ky) % 4) * 32 + (quad // 2) * 16 + ((z + kz) % 8) * 2 + quad % 2
    me = y * 32 + xl * 16 + z * 2 + c
    earlier = jnp.sum(jnp.where(block < me, counts, 0))
    capacity = lax.axis_size(WA) * CAP // 2
    return mix(jnp.stack([c, z, capacity - earlier]), total[:128], other, info, slot_route)


def solution(mesh):
    finer = Mesh(mesh.devices.reshape(NY, 2, NZ, 2, mesh.shape["ha"]), ("y", "xl", "z", "c", "ha"))
    placed = (P(WA, None),) * 4 + (P(WA, "ha"),) * 3
    return jax.shard_map(per_device, mesh=finer, in_specs=placed, out_specs=P(WA, "ha"), check_vma=False)
```

```python
import jax
import jax.numpy as jnp
from jax import lax
from jax.experimental import pallas as pl
from jax.experimental.pallas import tpu as pltpu
from jax.sharding import Mesh
from jax.sharding import PartitionSpec as P

CAP = 128
WA = ("y", "xl", "z", "c")
NY, NZ = 4, 8
F32, BF16, I32 = jnp.float32, jnp.bfloat16, jnp.int32
VMEM = pltpu.VMEM


def whole(memory_space=VMEM):
    return pl.BlockSpec(memory_space=memory_space)


def ring(axis, n, k):
    return lambda a: lax.ppermute(a, axis, [(i, (i + k) % n) for i in range(n)])


def Z(k):
    return ring("z", NZ, k)


def Y(k):
    return ring("y", NY, k)


def C(a):
    return lax.ppermute(a, "c", [(0, 1), (1, 0)])


def XL(a):
    return lax.ppermute(a, "xl", [(0, 1), (1, 0)])


def HA(a):
    return lax.ppermute(a, "ha", [(0, 1), (1, 0)])


def across_x(a):
    def at(x, c):
        return (x % 2) * 4 + c * 2 + x // 2

    pairs = [(at(x, c), at((x + 1 - 2 * c) % 4, c)) for x in range(4) for c in range(2)]
    return lax.ppermute(a, ("xl", "c", "ha"), pairs)


def prep_body(*refs):
    far, (info, packed), near, arrive = refs[:6], refs[6:8], refs[8:14], refs[14]
    copies = [pltpu.make_async_copy(f, n, arrive.at[i]) for i, (f, n) in enumerate(zip(far, near))]
    for copy in copies:
        copy.start()
    for copy in copies:
        copy.wait()
    ids, keep, rw, gate, up, down_rows = near
    hit = (ids[...] == 0) & (keep[...] == 1)
    chosen = jnp.max(jnp.where(hit, 1.0, 0.0), axis=0, keepdims=True)
    route = jnp.sum(jnp.where(hit, rw[...], 0.0), axis=0, keepdims=True)
    n = chosen.shape[1]
    row = lax.broadcasted_iota(I32, (n, n), 0)
    col = lax.broadcasted_iota(I32, (n, n), 1)
    before = jnp.where(row < col, 1.0, 0.0).astype(BF16)
    ones = jnp.broadcast_to(chosen, (16, n)).astype(BF16)
    position = jnp.dot(ones, before, preferred_element_type=F32)[:1]
    info[0:1, :] = position
    info[1:2, :] = chosen
    info[2:3, :] = route
    info[3:8, :] = jnp.zeros((5, n), F32)
    total = jnp.sum(chosen, axis=1, keepdims=True)
    for q in range(4):
        at = slice(q * 192, q * 192 + 192)
        packed[q, 0:32, :] = jnp.concatenate([gate[:, at], up[:, at]], axis=1)
        packed[q, 32:40, :] = jnp.broadcast_to(total, (8, 384)).astype(BF16)
        packed[q, 40:72, :] = down_rows[:, :384]
        packed[q, 72:104, :] = down_rows[:, 384:]


def prep(ids, keep, rw, gate, up, down_rows):
    n = ids.shape[1]
    return pl.pallas_call(
        prep_body,
        out_shape=(jax.ShapeDtypeStruct((8, n), F32), jax.ShapeDtypeStruct((4, 104, 384), BF16)),
        in_specs=[whole(pltpu.HBM)] * 6,
        out_specs=(whole(), whole()),
        scratch_shapes=[VMEM(a.shape, a.dtype) for a in (ids, keep, rw, gate, up, down_rows)]
        + [pltpu.SemaphoreType.DMA((6,))],
        compiler_params=pltpu.CompilerParams(vmem_limit_bytes=12 << 20),
        cost_estimate=pl.CostEstimate(flops=2 * 16 * n * n, bytes_accessed=4 * 32 * n, transcendentals=0),
        name="prep",
    )(ids, keep, rw, gate, up, down_rows)


def table(info):
    slot = lax.broadcasted_iota(I32, (CAP, info.shape[1]), 0).astype(F32)
    return (info[0:1, :] == slot) & (info[1:2, :] > 0.5)


def gather_body(where, tokens, info, out, slot_route, near, arrive):
    n, width = near.shape[1:]
    copies = [
        pltpu.make_async_copy(tokens.at[:, i * width : (i + 1) * width], near.at[i], arrive.at[i]) for i in range(NY)
    ]
    for copy in copies:
        copy.start()
    picked = table(info)
    got = jnp.sum(jnp.where(picked, info[2:3, :], 0.0), axis=1, keepdims=True)
    slot_route[...] = jnp.broadcast_to(got, slot_route.shape)
    one_hot = picked.astype(BF16)
    for block in range(NY):
        copies[block].wait()
        rows = jnp.dot(one_hot, near[block], preferred_element_type=F32).astype(BF16)
        ky = lax.rem(block - where[0] + NY, NY)
        yi = jnp.where(ky == 0, 0, jnp.where(ky == 3, 1, jnp.where(ky == 1, 2, 3)))
        for z in range(NZ):
            kz = lax.rem(z - where[1] + NZ, NZ)
            zi = jnp.where(kz == 0, 0, jnp.where(kz <= 3, 2 * kz, jnp.where(kz == 4, 7, 15 - 2 * kz)))
            piece = jnp.concatenate([rows[:, z * 64 : z * 64 + 64], rows[:, 512 + z * 64 : 576 + z * 64]], axis=1)
            out[:, pl.ds(pl.multiple_of((yi * NZ + zi) * 128, 128), 128)] = piece


def gather_rows(where, tokens, info):
    n, d = tokens.shape
    return pl.pallas_call(
        gather_body,
        out_shape=(jax.ShapeDtypeStruct((CAP, d), BF16), jax.ShapeDtypeStruct((CAP, 128), F32)),
        in_specs=[whole(pltpu.SMEM), whole(pltpu.HBM), whole()],
        out_specs=(whole(), whole()),
        scratch_shapes=[VMEM((NY, n, d // NY), tokens.dtype), pltpu.SemaphoreType.DMA((NY,))],
        compiler_params=pltpu.CompilerParams(vmem_limit_bytes=16 << 20),
        cost_estimate=pl.CostEstimate(flops=2 * CAP * n * d, bytes_accessed=2 * n * d, transcendentals=0),
        name="gather_rows",
    )(where, tokens, info)


def near_body(first, second, f_back, s_back, f_ahead, s_ahead, xo, xc, xn, xnc, total, x_far, x_all):
    for i, ref in enumerate((xo, xc, xn, xnc)):
        x_all[i * 128 : i * 128 + 128, :] = ref[:, :3072]
        x_far[i * 128 : i * 128 + 128, :] = ref[:, 3072:]
    acc = jnp.zeros((512, 384), F32)
    for i, (f, s) in enumerate(((first, second), (f_back, s_back), (f_ahead, s_ahead))):
        acc += jnp.dot(x_all[:, i * 1024 : i * 1024 + 640], f[0:640, :], preferred_element_type=F32)
        acc += jnp.dot(x_all[:, i * 1024 + 640 : i * 1024 + 1024], s[0:384, :], preferred_element_type=F32)
    total[...] = acc


def gate_up_near(*arrays):
    return pl.pallas_call(
        near_body,
        out_shape=(jax.ShapeDtypeStruct((512, 384), F32), jax.ShapeDtypeStruct((512, 1024), BF16)),
        in_specs=[whole()] * len(arrays),
        out_specs=(whole(), whole()),
        scratch_shapes=[VMEM((512, 3072), BF16)],
        compiler_params=pltpu.CompilerParams(vmem_limit_bytes=16 << 20),
        cost_estimate=pl.CostEstimate(flops=2 * 512 * 3072 * 384, bytes_accessed=8 << 20, transcendentals=0),
        name="gate_up_near",
    )(*arrays)


def far_body(where, total, x_far, far0, far1, first, second, f_back, s_back, f_ahead, s_ahead, own, other, limit):
    acc = total[...]
    acc += jnp.dot(x_far[:, 0:384], far0[0:384, :], preferred_element_type=F32)
    acc += jnp.dot(x_far[:, 384:640], far1[0:256, :], preferred_element_type=F32)
    acc += jnp.dot(x_far[:, 640:768], far0[384:512, :], preferred_element_type=F32)
    acc += jnp.dot(x_far[:, 768:1024], far1[256:512, :], preferred_element_type=F32)
    gate, up = acc[:, :192], acc[:, 192:]
    hidden = (gate * jax.nn.sigmoid(gate) * up).astype(BF16)
    own[...] = hidden[:256]
    other[...] = hidden[256:]

    lane = lax.broadcasted_iota(I32, (8, 128), 1)
    quad = lax.shift_right_logical(lane, 1) * 16 + (lane & 1)
    earlier = jnp.zeros((8, 128), F32)
    groups = (
        (0, first[640:680, 0:128], second[384:408, 0:128]),
        (3, f_back[640:680, 0:128], s_back[384:408, 0:128]),
        (1, f_ahead[640:680, 0:128], s_ahead[384:408, 0:128]),
        (2, far1[512:552, 0:128], far1[552:576, 0:128]),
    )
    for ky, near, late in groups:
        tiles = jnp.concatenate([near.astype(F32), late.astype(F32)], axis=0)
        for zi, kz in enumerate((0, 7, 1, 6, 2, 5, 3, 4)):
            block = ((where[0] + ky) & 3) * 32 + ((where[1] + kz) & 7) * 2 + quad
            counted = (block < where[2]) & (lane < 4)
            earlier += jnp.where(counted, tiles[zi * 8 : zi * 8 + 8], 0.0)
    before = jnp.sum(earlier[0:1], axis=1, keepdims=True)
    limit[...] = jnp.broadcast_to(where[3].astype(F32) - before, limit.shape)


def gate_up_far(*arrays):
    half = jax.ShapeDtypeStruct((256, 192), BF16)
    return pl.pallas_call(
        far_body,
        out_shape=(half, half, jax.ShapeDtypeStruct((8, 128), F32)),
        in_specs=[whole(pltpu.SMEM)] + [whole()] * (len(arrays) - 1),
        out_specs=(whole(), whole(), whole()),
        compiler_params=pltpu.CompilerParams(vmem_limit_bytes=16 << 20),
        cost_estimate=pl.CostEstimate(flops=2 * 512 * 1024 * 384, bytes_accessed=4 << 20, transcendentals=512 * 192),
        name="gate_up_far",
    )(*arrays)


def down_body(hidden, *refs):
    pieces, out = refs[:-1], refs[-1]

    def dot(k, w):
        return lax.dot_general(
            hidden[:, k * 384 : k * 384 + 384], w, (((1,), (1,)), ((), ())), preferred_element_type=F32
        )

    for r in range(NZ):
        near, far = (pieces[4], pieces[8]) if r == 4 else (pieces[r], pieces[r])
        base = 0 if r == 4 else 256
        total = dot(0, near[0:128]) + dot(1, near[128:256])
        total += dot(2, far[base : base + 128]) + dot(3, far[base + 128 : base + 256])
        out[:, r * 128 : r * 128 + 128] = total


def down(hidden, pieces):
    return pl.pallas_call(
        down_body,
        out_shape=jax.ShapeDtypeStruct((256, 1024), F32),
        in_specs=[whole()] * (1 + len(pieces)),
        out_specs=whole(),
        compiler_params=pltpu.CompilerParams(vmem_limit_bytes=12 << 20),
        cost_estimate=pl.CostEstimate(flops=2 * 256 * 1536 * 1024, bytes_accessed=5 << 20, transcendentals=0),
        name="down",
    )(hidden, *pieces)


def mix_body(where, mine, theirs, info, slot_route, limit, out, slots):
    @pl.when(pl.program_id(0) == 0)
    def _():
        slot = lax.broadcasted_iota(I32, (CAP, 1), 0).astype(F32)
        scale = jnp.where(slot < limit[0:1, 0:1], slot_route[:, 0:1], 0.0)
        src = lax.broadcasted_iota(I32, (512, 512), 0)
        dst = lax.broadcasted_iota(I32, (512, 512), 1)
        moved = (src + where[1] * 64) & 511
        order = jnp.where(moved == dst, 1.0, 0.0).astype(BF16)
        for ref, column in ((mine, where[0]), (theirs, 1 - where[0])):
            scaled = (ref[...] * scale).astype(BF16)
            for y in range(2):
                part = jnp.concatenate(
                    [scaled[:, r * 128 + y * 64 : r * 128 + y * 64 + 64] for r in range(NZ)], axis=1
                )
                placed = jnp.dot(part, order, preferred_element_type=F32).astype(BF16)
                slots[:, pl.ds(pl.multiple_of(y * 1024 + column * 512, 512), 512)] = placed

    picked = table(info).astype(BF16)
    mixed = lax.dot_general(picked, slots[...], (((0,), (0,)), ((), ())), preferred_element_type=F32)
    out[...] = mixed.astype(BF16)


def mix(where, mine, theirs, info, slot_route, limit):
    n, step = info.shape[1], 256
    return pl.pallas_call(
        mix_body,
        out_shape=jax.ShapeDtypeStruct((n, 2048), BF16),
        grid_spec=pltpu.PrefetchScalarGridSpec(
            num_scalar_prefetch=1,
            grid=(n // step,),
            in_specs=[
                pl.BlockSpec((CAP, 1024), lambda i, w: (0, 0)),
                pl.BlockSpec((CAP, 1024), lambda i, w: (0, 0)),
                pl.BlockSpec((8, step), lambda i, w: (0, i)),
                pl.BlockSpec((CAP, 128), lambda i, w: (0, 0)),
                pl.BlockSpec((8, 128), lambda i, w: (0, 0)),
            ],
            out_specs=pl.BlockSpec((step, 2048), lambda i, w: (i, 0)),
            scratch_shapes=[VMEM((CAP, 2048), BF16)],
        ),
        compiler_params=pltpu.CompilerParams(vmem_limit_bytes=16 << 20),
        cost_estimate=pl.CostEstimate(flops=2 * n * CAP * 2048, bytes_accessed=6 << 20, transcendentals=0),
        name="mix",
    )(where, mine, theirs, info, slot_route, limit)


def with_counts(units):
    return jnp.concatenate([u[:128] for u in units] + [u[128:] for u in units], axis=0)


def together(*arrays):
    return lax.optimization_barrier(arrays)


def flipped(a):
    return jnp.concatenate([a[128:], a[:128]], axis=0)


def HIDDEN_FAR(a):
    pairs = [(k, 3 - k) for k in range(4)]
    return lax.ppermute(a, ("xl", "ha"), pairs)


def per_device(tokens, expert_ids, keep_mask, route_weight, gate_weight, up_weight, down_weight):
    y, xl, z, c, ha = (lax.axis_index(a) for a in ("y", "xl", "z", "c", "ha"))
    sources = (expert_ids.T, keep_mask.T, route_weight.T, gate_weight, up_weight, down_weight)
    info, packed = prep(*(pltpu.with_memory_space_constraint(a, pltpu.HBM) for a in sources))
    arrived = lax.all_to_all(packed, ("xl", "c"), split_axis=0, concat_axis=0, tiled=True)
    slot_rows, slot_route = gather_rows(
        jnp.stack([y, z]), pltpu.with_memory_space_constraint(tokens, pltpu.HBM), info
    )

    lane = lax.broadcasted_iota(I32, (8, 384), 1)
    tile = jnp.zeros((8, 384), BF16)
    for j in range(4):
        tile = jnp.where(lane == j, arrived[j, 32:40], tile)
    unit = jnp.concatenate([arrived[:, :32].reshape(128, 384), tile], axis=0)
    picked = lax.dynamic_slice_in_dim(arrived, 2 * c, 2, axis=0)[:, 40:]
    rows = jnp.concatenate([picked[0, :32], picked[1, :32], picked[0, 32:], picked[1, 32:]], axis=0)

    neighbour_rows = across_x(slot_rows)
    b1, a1 = Z(1)(unit), Z(-1)(unit)
    d_back, d_ahead = Y(1)(rows), Y(-1)(rows)
    b1, a1, d_back, d_ahead = together(b1, a1, d_back, d_ahead)
    b2, a2 = Z(1)(b1), Z(-1)(a1)
    d_far = Y(1)(d_back[:64]), Y(-1)(d_ahead[64:])
    b2, a2, d_far0, d_far1, neighbour_rows = together(b2, a2, *d_far, neighbour_rows)

    turned = [rows, d_ahead, jnp.concatenate([d_far0, d_far1], axis=0), d_back]
    shift = lax.rem(2 * ha - y + NY, NY)
    ordered = []
    for j in range(4):
        pick = turned[j]
        for s in range(1, 4):
            pick = jnp.where(shift == s, turned[(j + s) % 4], pick)
        ordered.append(pick)

    def halves(p, q):
        return jnp.concatenate([p[:64], q[:64], p[64:], q[64:]], axis=0)

    d_swap = HA(halves(ordered[2], ordered[3]))
    b3, a3 = Z(1)(b2), Z(-1)(a2)
    first = with_counts([unit, b1, a1, b2, a2])
    f_back, f_ahead = Y(1)(first), Y(-1)(first)
    b3, a3, d_swap = together(b3, a3, d_swap)

    d0 = jnp.concatenate([halves(ordered[0], ordered[1]), d_swap], axis=0)
    e = Z(1)(b3)
    db1, da1 = Z(1)(d0), Z(-1)(d0)
    e, f_back, f_ahead = together(e, f_back, f_ahead)
    second = with_counts([b3, a3, e])
    s_back, s_ahead = Y(1)(second), Y(-1)(second)
    x_rows = [slot_rows, C(slot_rows), neighbour_rows, C(neighbour_rows)]
    s_back, s_ahead, db1, da1 = together(s_back, s_ahead, db1, da1)
    far0 = Y(1)(jnp.concatenate([f_back[:384], s_back[:128]], axis=0))
    far1 = Y(-1)(jnp.concatenate([f_ahead[384:640], s_ahead[128:384], f_ahead[640:], s_ahead[384:]], axis=0))
    db2, da2 = Z(1)(db1), Z(-1)(da1)
    near = (first, second, f_back, s_back, f_ahead, s_ahead)
    partial, x_far = gate_up_near(*near, *x_rows)
    partial, x_far, far0, far1, db2, da2 = together(partial, x_far, far0, far1, db2, da2)

    db3, da3 = Z(1)(db2), Z(-1)(da2)
    me = y * 32 + xl * 16 + z * 2 + c
    capacity = lax.axis_size(WA) * CAP // 2
    h_own, h_other, limit = gate_up_far(jnp.stack([y, z, me, capacity]), partial, x_far, far0, far1, *near)
    h_near, h_ha, h_far = XL(h_other), HA(h_own), HIDDEN_FAR(h_other)
    de0, de1 = Z(1)(db3[:256]), Z(-1)(da3[256:])
    mine = (h_own, h_near, h_ha, h_far)
    core = C(jnp.concatenate([flipped(h) for h in mine], axis=1))
    theirs = [core[:, k * 192 : k * 192 + 192] for k in range(4)]
    c0, x0 = c == 0, xl == 0
    hidden = []
    for k in (0, 2):
        here = (jnp.where(c0, mine[k], theirs[k]), jnp.where(c0, theirs[k], mine[k]))
        there = (jnp.where(c0, mine[k + 1], theirs[k + 1]), jnp.where(c0, theirs[k + 1], mine[k + 1]))
        hidden += [jnp.where(x0, p, q) for p, q in zip(here, there)]
        hidden += [jnp.where(x0, q, p) for p, q in zip(here, there)]
    pieces = [d0, da1, da2, da3, de0, db3, db2, db1, de1]
    total = down(jnp.concatenate(hidden, axis=1), pieces)
    other = C(total[128:])

    return mix(jnp.stack([c, z]), total[:128], other, info, slot_route, limit)


def solution(mesh):
    finer = Mesh(mesh.devices.reshape(NY, 2, NZ, 2, mesh.shape["ha"]), ("y", "xl", "z", "c", "ha"))
    placed = (P(WA, None),) * 4 + (P(WA, "ha"),) * 3
    return jax.shard_map(per_device, mesh=finer, in_specs=placed, out_specs=P(WA, "ha"), check_vma=False)
```

```python
import jax
import jax.numpy as jnp
from jax import lax
from jax.experimental import pallas as pl
from jax.experimental.pallas import tpu as pltpu
from jax.sharding import Mesh
from jax.sharding import PartitionSpec as P

CAP = 128
WA = ("y", "xl", "z", "c")
NY, NZ = 4, 8
F32, BF16, I32 = jnp.float32, jnp.bfloat16, jnp.int32
VMEM = pltpu.VMEM


def whole(memory_space=VMEM):
    return pl.BlockSpec(memory_space=memory_space)


def ring(axis, n, k):
    return lambda a: lax.ppermute(a, axis, [(i, (i + k) % n) for i in range(n)])


def Z(k):
    return ring("z", NZ, k)


def Y(k):
    return ring("y", NY, k)


def C(a):
    return lax.ppermute(a, "c", [(0, 1), (1, 0)])


def XL(a):
    return lax.ppermute(a, "xl", [(0, 1), (1, 0)])


def HA(a):
    return lax.ppermute(a, "ha", [(0, 1), (1, 0)])


def across_x(a):
    def at(x, c):
        return (x % 2) * 4 + c * 2 + x // 2

    pairs = [(at(x, c), at((x + 1 - 2 * c) % 4, c)) for x in range(4) for c in range(2)]
    return lax.ppermute(a, ("xl", "c", "ha"), pairs)


def prep_body(*refs):
    far, (info, packed), near, arrive = refs[:6], refs[6:8], refs[8:14], refs[14]
    copies = [pltpu.make_async_copy(f, n, arrive.at[i]) for i, (f, n) in enumerate(zip(far, near))]
    for copy in copies:
        copy.start()
    for copy in copies:
        copy.wait()
    ids, keep, rw, gate, up, down_rows = near
    hit = (ids[...] == 0) & (keep[...] == 1)
    chosen = jnp.max(jnp.where(hit, 1.0, 0.0), axis=0, keepdims=True)
    route = jnp.sum(jnp.where(hit, rw[...], 0.0), axis=0, keepdims=True)
    n = chosen.shape[1]
    row = lax.broadcasted_iota(I32, (n, n), 0)
    col = lax.broadcasted_iota(I32, (n, n), 1)
    before = jnp.where(row < col, 1.0, 0.0).astype(BF16)
    ones = jnp.broadcast_to(chosen, (16, n)).astype(BF16)
    position = jnp.dot(ones, before, preferred_element_type=F32)[:1]
    info[0:1, :] = position
    info[1:2, :] = chosen
    info[2:3, :] = route
    info[3:8, :] = jnp.zeros((5, n), F32)
    total = jnp.sum(chosen, axis=1, keepdims=True)
    for q in range(4):
        at = slice(q * 192, q * 192 + 192)
        packed[q, 0:32, :] = jnp.concatenate([gate[:, at], up[:, at]], axis=1)
        packed[q, 32:40, :] = jnp.broadcast_to(total, (8, 384)).astype(BF16)
        packed[q, 40:72, :] = down_rows[:, :384]
        packed[q, 72:104, :] = down_rows[:, 384:]


def prep(ids, keep, rw, gate, up, down_rows):
    n = ids.shape[1]
    return pl.pallas_call(
        prep_body,
        out_shape=(jax.ShapeDtypeStruct((8, n), F32), jax.ShapeDtypeStruct((4, 104, 384), BF16)),
        in_specs=[whole(pltpu.HBM)] * 6,
        out_specs=(whole(), whole()),
        scratch_shapes=[VMEM(a.shape, a.dtype) for a in (ids, keep, rw, gate, up, down_rows)]
        + [pltpu.SemaphoreType.DMA((6,))],
        compiler_params=pltpu.CompilerParams(vmem_limit_bytes=12 << 20),
        cost_estimate=pl.CostEstimate(flops=2 * 16 * n * n, bytes_accessed=4 * 32 * n, transcendentals=0),
        name="prep",
    )(ids, keep, rw, gate, up, down_rows)


def table(info):
    slot = lax.broadcasted_iota(I32, (CAP, info.shape[1]), 0).astype(F32)
    return (info[0:1, :] == slot) & (info[1:2, :] > 0.5)


def gather_body(where, tokens, info, out, slot_route, near, arrive):
    n, width = near.shape[1:]
    copies = [
        pltpu.make_async_copy(tokens.at[:, i * width : (i + 1) * width], near.at[i], arrive.at[i]) for i in range(NY)
    ]
    for copy in copies:
        copy.start()
    picked = table(info)
    got = jnp.sum(jnp.where(picked, info[2:3, :], 0.0), axis=1, keepdims=True)
    slot_route[...] = jnp.broadcast_to(got, slot_route.shape)
    one_hot = picked.astype(BF16)
    for block in range(NY):
        copies[block].wait()
        rows = jnp.dot(one_hot, near[block], preferred_element_type=F32).astype(BF16)
        ky = lax.rem(block - where[0] + NY, NY)
        yi = jnp.where(ky == 0, 0, jnp.where(ky == 3, 1, jnp.where(ky == 1, 2, 3)))
        for z in range(NZ):
            kz = lax.rem(z - where[1] + NZ, NZ)
            zi = jnp.where(kz == 0, 0, jnp.where(kz <= 3, 2 * kz, jnp.where(kz == 4, 7, 15 - 2 * kz)))
            piece = jnp.concatenate([rows[:, z * 64 : z * 64 + 64], rows[:, 512 + z * 64 : 576 + z * 64]], axis=1)
            out[:, pl.ds(pl.multiple_of((yi * NZ + zi) * 128, 128), 128)] = piece


def gather_rows(where, tokens, info):
    n, d = tokens.shape
    return pl.pallas_call(
        gather_body,
        out_shape=(jax.ShapeDtypeStruct((CAP, d), BF16), jax.ShapeDtypeStruct((CAP, 128), F32)),
        in_specs=[whole(pltpu.SMEM), whole(pltpu.HBM), whole()],
        out_specs=(whole(), whole()),
        scratch_shapes=[VMEM((NY, n, d // NY), tokens.dtype), pltpu.SemaphoreType.DMA((NY,))],
        compiler_params=pltpu.CompilerParams(vmem_limit_bytes=16 << 20),
        cost_estimate=pl.CostEstimate(flops=2 * CAP * n * d, bytes_accessed=2 * n * d, transcendentals=0),
        name="gather_rows",
    )(where, tokens, info)


def near_body(first, second, f_back, s_back, f_ahead, s_ahead, xo, xc, xn, xnc, total, x_far, x_all):
    for i, ref in enumerate((xo, xc, xn, xnc)):
        x_all[i * 128 : i * 128 + 128, :] = ref[:, :3072]
        x_far[i * 128 : i * 128 + 128, :] = ref[:, 3072:]
    acc = jnp.zeros((512, 384), F32)
    for i, (f, s) in enumerate(((first, second), (f_back, s_back), (f_ahead, s_ahead))):
        acc += jnp.dot(x_all[:, i * 1024 : i * 1024 + 640], f[0:640, :], preferred_element_type=F32)
        acc += jnp.dot(x_all[:, i * 1024 + 640 : i * 1024 + 1024], s[0:384, :], preferred_element_type=F32)
    total[...] = acc


def gate_up_near(*arrays):
    return pl.pallas_call(
        near_body,
        out_shape=(jax.ShapeDtypeStruct((512, 384), F32), jax.ShapeDtypeStruct((512, 1024), BF16)),
        in_specs=[whole()] * len(arrays),
        out_specs=(whole(), whole()),
        scratch_shapes=[VMEM((512, 3072), BF16)],
        compiler_params=pltpu.CompilerParams(vmem_limit_bytes=16 << 20),
        cost_estimate=pl.CostEstimate(flops=2 * 512 * 3072 * 384, bytes_accessed=8 << 20, transcendentals=0),
        name="gate_up_near",
    )(*arrays)


def far_body(where, total, x_far, far0, far1, first, second, f_back, s_back, f_ahead, s_ahead, own, other, limit):
    acc = total[...]
    acc += jnp.dot(x_far[:, 0:384], far0[0:384, :], preferred_element_type=F32)
    acc += jnp.dot(x_far[:, 384:640], far1[0:256, :], preferred_element_type=F32)
    acc += jnp.dot(x_far[:, 640:768], far0[384:512, :], preferred_element_type=F32)
    acc += jnp.dot(x_far[:, 768:1024], far1[256:512, :], preferred_element_type=F32)
    gate, up = acc[:, :192], acc[:, 192:]
    hidden = (gate * jax.nn.sigmoid(gate) * up).astype(BF16)
    own[...] = hidden[:256]
    other[...] = hidden[256:]

    lane = lax.broadcasted_iota(I32, (8, 128), 1)
    quad = lax.shift_right_logical(lane, 1) * 16 + (lane & 1)
    earlier = jnp.zeros((8, 128), F32)
    groups = (
        (0, first[640:680, 0:128], second[384:408, 0:128]),
        (3, f_back[640:680, 0:128], s_back[384:408, 0:128]),
        (1, f_ahead[640:680, 0:128], s_ahead[384:408, 0:128]),
        (2, far1[512:552, 0:128], far1[552:576, 0:128]),
    )
    for ky, near, late in groups:
        tiles = jnp.concatenate([near.astype(F32), late.astype(F32)], axis=0)
        for zi, kz in enumerate((0, 7, 1, 6, 2, 5, 3, 4)):
            block = ((where[0] + ky) & 3) * 32 + ((where[1] + kz) & 7) * 2 + quad
            counted = (block < where[2]) & (lane < 4)
            earlier += jnp.where(counted, tiles[zi * 8 : zi * 8 + 8], 0.0)
    before = jnp.sum(earlier[0:1], axis=1, keepdims=True)
    limit[...] = jnp.broadcast_to(where[3].astype(F32) - before, limit.shape)


def gate_up_far(*arrays):
    half = jax.ShapeDtypeStruct((256, 192), BF16)
    return pl.pallas_call(
        far_body,
        out_shape=(half, half, jax.ShapeDtypeStruct((8, 128), F32)),
        in_specs=[whole(pltpu.SMEM)] + [whole()] * (len(arrays) - 1),
        out_specs=(whole(), whole(), whole()),
        compiler_params=pltpu.CompilerParams(vmem_limit_bytes=16 << 20),
        cost_estimate=pl.CostEstimate(flops=2 * 512 * 1024 * 384, bytes_accessed=4 << 20, transcendentals=512 * 192),
        name="gate_up_far",
    )(*arrays)


def down_body(where, own, near, ha, far, core, *refs):
    pieces, (out, hidden) = refs[:-2], refs[-2:]

    for xl in range(2):
        for c in range(2):

            @pl.when((where[0] == xl) & (where[1] == c))
            def _():
                for k, ref in enumerate((own, near, ha, far)):
                    pair = xl if k % 2 == 0 else 1 - xl
                    base = (k // 2) * 768 + pair * 384
                    hidden[:, base + c * 192 : base + c * 192 + 192] = ref[...]
                    got = core[:, k * 192 : k * 192 + 192]
                    hidden[:, base + (1 - c) * 192 : base + (1 - c) * 192 + 192] = jnp.concatenate(
                        [got[128:], got[:128]], axis=0
                    )

    def dot(k, w):
        return lax.dot_general(
            hidden[:, k * 384 : k * 384 + 384], w, (((1,), (1,)), ((), ())), preferred_element_type=F32
        )

    blocks = []
    for r in range(NZ):
        front, rear = (pieces[4], pieces[8]) if r == 4 else (pieces[r], pieces[r])
        base = 0 if r == 4 else 256
        total = dot(0, front[0:128]) + dot(1, front[128:256])
        blocks.append(total + dot(2, rear[base : base + 128]) + dot(3, rear[base + 128 : base + 256]))
    for y in range(2):
        part = jnp.concatenate([b[:, y * 64 : y * 64 + 64] for b in blocks], axis=1)
        out[:, y * 512 : y * 512 + 512] = pltpu.roll(part, where[2] * 64, 1)


def down(where, hidden, pieces):
    return pl.pallas_call(
        down_body,
        out_shape=jax.ShapeDtypeStruct((256, 1024), F32),
        in_specs=[whole(pltpu.SMEM)] + [whole()] * (len(hidden) + len(pieces)),
        out_specs=whole(),
        scratch_shapes=[VMEM((256, 1536), BF16)],
        compiler_params=pltpu.CompilerParams(vmem_limit_bytes=12 << 20),
        cost_estimate=pl.CostEstimate(flops=2 * 256 * 1536 * 1024, bytes_accessed=5 << 20, transcendentals=0),
        name="down",
    )(where, *hidden, *pieces)


def mix_body(where, mine, theirs, info, slot_route, limit, out, slots):
    @pl.when(pl.program_id(0) == 0)
    def _():
        slot = lax.broadcasted_iota(I32, (CAP, 1), 0).astype(F32)
        scale = jnp.where(slot < limit[0:1, 0:1], slot_route[:, 0:1], 0.0)
        for ref, column in ((mine, where[0]), (theirs, 1 - where[0])):
            scaled = (ref[...] * scale).astype(BF16)
            for y in range(2):
                at = pl.multiple_of(y * 1024 + column * 512, 512)
                slots[:, pl.ds(at, 512)] = scaled[:, y * 512 : y * 512 + 512]

    picked = table(info).astype(BF16)
    mixed = lax.dot_general(picked, slots[...], (((0,), (0,)), ((), ())), preferred_element_type=F32)
    out[...] = mixed.astype(BF16)


def mix(where, mine, theirs, info, slot_route, limit):
    n, step = info.shape[1], 256
    return pl.pallas_call(
        mix_body,
        out_shape=jax.ShapeDtypeStruct((n, 2048), BF16),
        grid_spec=pltpu.PrefetchScalarGridSpec(
            num_scalar_prefetch=1,
            grid=(n // step,),
            in_specs=[
                pl.BlockSpec((CAP, 1024), lambda i, w: (0, 0)),
                pl.BlockSpec((CAP, 1024), lambda i, w: (0, 0)),
                pl.BlockSpec((8, step), lambda i, w: (0, i)),
                pl.BlockSpec((CAP, 128), lambda i, w: (0, 0)),
                pl.BlockSpec((8, 128), lambda i, w: (0, 0)),
            ],
            out_specs=pl.BlockSpec((step, 2048), lambda i, w: (i, 0)),
            scratch_shapes=[VMEM((CAP, 2048), BF16)],
        ),
        compiler_params=pltpu.CompilerParams(vmem_limit_bytes=16 << 20),
        cost_estimate=pl.CostEstimate(flops=2 * n * CAP * 2048, bytes_accessed=6 << 20, transcendentals=0),
        name="mix",
    )(where, mine, theirs, info, slot_route, limit)


def with_counts(units):
    return jnp.concatenate([u[:128] for u in units] + [u[128:] for u in units], axis=0)


def together(*arrays):
    return lax.optimization_barrier(arrays)


def HIDDEN_FAR(a):
    pairs = [(k, 3 - k) for k in range(4)]
    return lax.ppermute(a, ("xl", "ha"), pairs)


def per_device(tokens, expert_ids, keep_mask, route_weight, gate_weight, up_weight, down_weight):
    y, xl, z, c, ha = (lax.axis_index(a) for a in ("y", "xl", "z", "c", "ha"))
    sources = (expert_ids.T, keep_mask.T, route_weight.T, gate_weight, up_weight, down_weight)
    info, packed = prep(*(pltpu.with_memory_space_constraint(a, pltpu.HBM) for a in sources))
    arrived = lax.all_to_all(packed, ("xl", "c"), split_axis=0, concat_axis=0, tiled=True)
    slot_rows, slot_route = gather_rows(
        jnp.stack([y, z]), pltpu.with_memory_space_constraint(tokens, pltpu.HBM), info
    )

    lane = lax.broadcasted_iota(I32, (8, 384), 1)
    tile = jnp.zeros((8, 384), BF16)
    for j in range(4):
        tile = jnp.where(lane == j, arrived[j, 32:40], tile)
    unit = jnp.concatenate([arrived[:, :32].reshape(128, 384), tile], axis=0)
    picked = lax.dynamic_slice_in_dim(arrived, 2 * c, 2, axis=0)[:, 40:]
    rows = jnp.concatenate([picked[0, :32], picked[1, :32], picked[0, 32:], picked[1, 32:]], axis=0)

    neighbour_rows = across_x(slot_rows)
    b1, a1 = Z(1)(unit), Z(-1)(unit)
    d_back, d_ahead = Y(1)(rows), Y(-1)(rows)
    b2, a2 = Z(1)(b1), Z(-1)(a1)
    d_far = Y(1)(d_back[:64]), Y(-1)(d_ahead[64:])
    d_far0, d_far1 = d_far
    b2, a2, neighbour_rows = together(b2, a2, neighbour_rows)

    turned = [rows, d_ahead, jnp.concatenate([d_far0, d_far1], axis=0), d_back]
    shift = lax.rem(2 * ha - y + NY, NY)
    ordered = []
    for j in range(4):
        pick = turned[j]
        for s in range(1, 4):
            pick = jnp.where(shift == s, turned[(j + s) % 4], pick)
        ordered.append(pick)

    def halves(p, q):
        return jnp.concatenate([p[:64], q[:64], p[64:], q[64:]], axis=0)

    d_swap = HA(halves(ordered[2], ordered[3]))
    b3, a3 = Z(1)(b2), Z(-1)(a2)
    first = with_counts([unit, b1, a1, b2, a2])
    f_back, f_ahead = Y(1)(first), Y(-1)(first)
    b3, a3, d_swap = together(b3, a3, d_swap)

    d0 = jnp.concatenate([halves(ordered[0], ordered[1]), d_swap], axis=0)
    e = Z(1)(b3)
    db1, da1 = Z(1)(d0), Z(-1)(d0)
    e, f_back, f_ahead, db1, da1 = together(e, f_back, f_ahead, db1, da1)

    second = with_counts([b3, a3, e])
    s_back, s_ahead = Y(1)(second), Y(-1)(second)
    db2, da2 = Z(1)(db1), Z(-1)(da1)
    core_rows, far_rows = C(slot_rows), C(neighbour_rows)
    s_back, s_ahead, db2, da2, core_rows, far_rows = together(s_back, s_ahead, db2, da2, core_rows, far_rows)

    far0 = Y(1)(jnp.concatenate([f_back[:384], s_back[:128]], axis=0))
    far1 = Y(-1)(jnp.concatenate([f_ahead[384:640], s_ahead[128:384], f_ahead[640:], s_ahead[384:]], axis=0))
    db3, da3 = Z(1)(db2), Z(-1)(da2)
    near = (first, second, f_back, s_back, f_ahead, s_ahead)
    partial, x_far = gate_up_near(*near, slot_rows, core_rows, neighbour_rows, far_rows)
    partial, x_far, far0, far1, db3, da3 = together(partial, x_far, far0, far1, db3, da3)

    me = y * 32 + xl * 16 + z * 2 + c
    capacity = lax.axis_size(WA) * CAP // 2
    h_own, h_other, limit = gate_up_far(jnp.stack([y, z, me, capacity]), partial, x_far, far0, far1, *near)
    h_near, h_ha, h_far = XL(h_other), HA(h_own), HIDDEN_FAR(h_other)
    de0, de1 = Z(1)(db3[:256]), Z(-1)(da3[256:])
    core = C(jnp.concatenate([h_own, h_near, h_ha, h_far], axis=1))
    pieces = [d0, da1, da2, da3, de0, db3, db2, db1, de1]
    total = down(jnp.stack([xl, c, z]), (h_own, h_near, h_ha, h_far, core), pieces)
    other = C(total[128:])
    return mix(jnp.stack([c]), total[:128], other, info, slot_route, limit)


def solution(mesh):
    finer = Mesh(mesh.devices.reshape(NY, 2, NZ, 2, mesh.shape["ha"]), ("y", "xl", "z", "c", "ha"))
    placed = (P(WA, None),) * 4 + (P(WA, "ha"),) * 3
    return jax.shard_map(per_device, mesh=finer, in_specs=placed, out_specs=P(WA, "ha"), check_vma=False)
```

```python
import jax
import jax.numpy as jnp
from jax import lax
from jax.experimental import pallas as pl
from jax.experimental.pallas import tpu as pltpu
from jax.sharding import Mesh
from jax.sharding import PartitionSpec as P

CAP = 128
WA = ("y", "xl", "z", "c")
NY, NZ = 4, 8
F32, BF16, I32 = jnp.float32, jnp.bfloat16, jnp.int32
VMEM = pltpu.VMEM


def whole(memory_space=VMEM):
    return pl.BlockSpec(memory_space=memory_space)


def ring(axis, n, k):
    return lambda a: lax.ppermute(a, axis, [(i, (i + k) % n) for i in range(n)])


def Z(k):
    return ring("z", NZ, k)


def Y(k):
    return ring("y", NY, k)


def C(a):
    return lax.ppermute(a, "c", [(0, 1), (1, 0)])


def XL(a):
    return lax.ppermute(a, "xl", [(0, 1), (1, 0)])


def HA(a):
    return lax.ppermute(a, "ha", [(0, 1), (1, 0)])


def across_x(a):
    def at(x, c):
        return (x % 2) * 4 + c * 2 + x // 2

    pairs = [(at(x, c), at((x + 1 - 2 * c) % 4, c)) for x in range(4) for c in range(2)]
    return lax.ppermute(a, ("xl", "c", "ha"), pairs)


def prep_body(*refs):
    far, (info, packed), near, arrive = refs[:6], refs[6:8], refs[8:14], refs[14]
    copies = [pltpu.make_async_copy(f, n, arrive.at[i]) for i, (f, n) in enumerate(zip(far, near))]
    for copy in copies:
        copy.start()
    for copy in copies:
        copy.wait()
    ids, keep, rw, gate, up, down_rows = near
    hit = (ids[...] == 0) & (keep[...] == 1)
    chosen = jnp.max(jnp.where(hit, 1.0, 0.0), axis=0, keepdims=True)
    route = jnp.sum(jnp.where(hit, rw[...], 0.0), axis=0, keepdims=True)
    n = chosen.shape[1]
    row = lax.broadcasted_iota(I32, (n, n), 0)
    col = lax.broadcasted_iota(I32, (n, n), 1)
    before = jnp.where(row < col, 1.0, 0.0).astype(BF16)
    ones = jnp.broadcast_to(chosen, (16, n)).astype(BF16)
    position = jnp.dot(ones, before, preferred_element_type=F32)[:1]
    info[0:1, :] = position
    info[1:2, :] = chosen
    info[2:3, :] = route
    info[3:8, :] = jnp.zeros((5, n), F32)
    total = jnp.sum(chosen, axis=1, keepdims=True)
    for q in range(4):
        at = slice(q * 192, q * 192 + 192)
        packed[q, 0:32, :] = jnp.concatenate([gate[:, at], up[:, at]], axis=1)
        packed[q, 32:40, :] = jnp.broadcast_to(total, (8, 384)).astype(BF16)
        packed[q, 40:72, :] = down_rows[:, :384]
        packed[q, 72:104, :] = down_rows[:, 384:]


def prep(ids, keep, rw, gate, up, down_rows):
    n = ids.shape[1]
    return pl.pallas_call(
        prep_body,
        out_shape=(jax.ShapeDtypeStruct((8, n), F32), jax.ShapeDtypeStruct((4, 104, 384), BF16)),
        in_specs=[whole(pltpu.HBM)] * 6,
        out_specs=(whole(), whole()),
        scratch_shapes=[VMEM(a.shape, a.dtype) for a in (ids, keep, rw, gate, up, down_rows)]
        + [pltpu.SemaphoreType.DMA((6,))],
        compiler_params=pltpu.CompilerParams(vmem_limit_bytes=12 << 20),
        cost_estimate=pl.CostEstimate(flops=2 * 16 * n * n, bytes_accessed=4 * 32 * n, transcendentals=0),
        name="prep",
    )(ids, keep, rw, gate, up, down_rows)


def table(info):
    slot = lax.broadcasted_iota(I32, (CAP, info.shape[1]), 0).astype(F32)
    return (info[0:1, :] == slot) & (info[1:2, :] > 0.5)


def gather_body(where, tokens, info, out, slot_route, near, arrive):
    n, width = near.shape[1:]
    copies = [
        pltpu.make_async_copy(tokens.at[:, i * width : (i + 1) * width], near.at[i], arrive.at[i]) for i in range(NY)
    ]
    for copy in copies:
        copy.start()
    picked = table(info)
    got = jnp.sum(jnp.where(picked, info[2:3, :], 0.0), axis=1, keepdims=True)
    slot_route[...] = jnp.broadcast_to(got, slot_route.shape)
    one_hot = picked.astype(BF16)
    for block in range(NY):
        copies[block].wait()
        rows = jnp.dot(one_hot, near[block], preferred_element_type=F32).astype(BF16)
        ky = lax.rem(block - where[0] + NY, NY)
        yi = jnp.where(ky == 0, 0, jnp.where(ky == 3, 1, jnp.where(ky == 1, 2, 3)))
        for z in range(NZ):
            kz = lax.rem(z - where[1] + NZ, NZ)
            zi = jnp.where(kz == 0, 0, jnp.where(kz <= 3, 2 * kz, jnp.where(kz == 4, 7, 15 - 2 * kz)))
            piece = jnp.concatenate([rows[:, z * 64 : z * 64 + 64], rows[:, 512 + z * 64 : 576 + z * 64]], axis=1)
            out[:, pl.ds(pl.multiple_of((yi * NZ + zi) * 128, 128), 128)] = piece


def gather_rows(where, tokens, info):
    n, d = tokens.shape
    return pl.pallas_call(
        gather_body,
        out_shape=(jax.ShapeDtypeStruct((CAP, d), BF16), jax.ShapeDtypeStruct((CAP, 128), F32)),
        in_specs=[whole(pltpu.SMEM), whole(pltpu.HBM), whole()],
        out_specs=(whole(), whole()),
        scratch_shapes=[VMEM((NY, n, d // NY), tokens.dtype), pltpu.SemaphoreType.DMA((NY,))],
        compiler_params=pltpu.CompilerParams(vmem_limit_bytes=16 << 20),
        cost_estimate=pl.CostEstimate(flops=2 * CAP * n * d, bytes_accessed=2 * n * d, transcendentals=0),
        name="gather_rows",
    )(where, tokens, info)


def near_body(first, second, last, f_back, f_ahead, g_back, g_ahead, xo, xc, xn, xnc, total, x_far, x_all):
    for i, ref in enumerate((xo, xc, xn, xnc)):
        at = slice(i * 128, i * 128 + 128)
        x_all[at, :] = ref[:, :3712]
        x_far[at, 0:128] = ref[:, 1920:2048]
        x_far[at, 128:256] = ref[:, 2944:3072]
        x_far[at, 256:640] = ref[:, 3712:]
    acc = jnp.zeros((512, 384), F32)
    for start, ref, row, size in (
        (0, first, 0, 640),
        (640, second, 0, 256),
        (896, last, 0, 128),
        (1024, f_back, 0, 640),
        (1664, g_back, 0, 256),
        (2048, f_ahead, 0, 640),
        (2688, g_ahead, 0, 256),
        (3072, g_back, 256, 384),
        (3456, g_ahead, 256, 256),
    ):
        acc += jnp.dot(x_all[:, start : start + size], ref[row : row + size, :], preferred_element_type=F32)
    total[...] = acc


def gate_up_near(*arrays):
    return pl.pallas_call(
        near_body,
        out_shape=(jax.ShapeDtypeStruct((512, 384), F32), jax.ShapeDtypeStruct((512, 640), BF16)),
        in_specs=[whole()] * len(arrays),
        out_specs=(whole(), whole()),
        scratch_shapes=[VMEM((512, 3712), BF16)],
        compiler_params=pltpu.CompilerParams(vmem_limit_bytes=16 << 20),
        cost_estimate=pl.CostEstimate(flops=2 * 512 * 3456 * 384, bytes_accessed=8 << 20, transcendentals=0),
        name="gate_up_near",
    )(*arrays)


def far_body(where, total, x_far, k_back, k_ahead, k_far, *refs):
    (first, second, last, f_back, f_ahead, g_back, g_ahead), (own, other, limit) = refs[:7], refs[7:]
    acc = total[...]
    for start, ref, row in ((0, k_back, 0), (128, k_ahead, 0), (256, k_back, 128), (384, k_ahead, 128), (512, k_far, 0)):
        acc += jnp.dot(x_far[:, start : start + 128], ref[row : row + 128, :], preferred_element_type=F32)
    gate, up = acc[:, :192], acc[:, 192:]
    hidden = (gate * jax.nn.sigmoid(gate) * up).astype(BF16)
    own[...] = hidden[:256]
    other[...] = hidden[256:]

    lane = lax.broadcasted_iota(I32, (8, 128), 1)
    quad = lax.shift_right_logical(lane, 1) * 16 + (lane & 1)
    earlier = jnp.zeros((8, 128), F32)
    groups = (
        (0, first[640:680, 0:128], second[256:272, 0:128], last[128:136, 0:128]),
        (3, f_back[640:680, 0:128], g_back[640:656, 0:128], k_back[256:264, 0:128]),
        (1, f_ahead[640:680, 0:128], g_ahead[512:528, 0:128], k_ahead[256:264, 0:128]),
        (2, g_ahead[528:568, 0:128], k_ahead[264:280, 0:128], k_far[128:136, 0:128]),
    )
    for ky, *parts in groups:
        tiles = jnp.concatenate([part.astype(F32) for part in parts], axis=0)
        for zi, kz in enumerate((0, 7, 1, 6, 2, 5, 3, 4)):
            block = ((where[0] + ky) & 3) * 32 + ((where[1] + kz) & 7) * 2 + quad
            counted = (block < where[4]) & (lane < 4)
            earlier += jnp.where(counted, tiles[zi * 8 : zi * 8 + 8], 0.0)
    before = jnp.sum(earlier[0:1], axis=1, keepdims=True)
    limit[...] = jnp.broadcast_to(where[5].astype(F32) - before, limit.shape)


def gate_up_far(*arrays):
    half = jax.ShapeDtypeStruct((256, 192), BF16)
    return pl.pallas_call(
        far_body,
        out_shape=(half, half, jax.ShapeDtypeStruct((8, 128), F32)),
        in_specs=[whole(pltpu.SMEM)] + [whole()] * (len(arrays) - 1),
        out_specs=(whole(), whole(), whole()),
        compiler_params=pltpu.CompilerParams(vmem_limit_bytes=16 << 20),
        cost_estimate=pl.CostEstimate(flops=2 * 512 * 640 * 384, bytes_accessed=3 << 20, transcendentals=512 * 192),
        name="gate_up_far",
    )(*arrays)


def down_body(where, own, near, ha, far, core, *refs):
    pieces, (out, hidden) = refs[:-2], refs[-2:]

    for xl in range(2):
        for c in range(2):

            @pl.when((where[2] == xl) & (where[3] == c))
            def _():
                for k, ref in enumerate((own, near, ha, far)):
                    pair = xl if k % 2 == 0 else 1 - xl
                    base = (k // 2) * 768 + pair * 384
                    hidden[:, base + c * 192 : base + c * 192 + 192] = ref[...]
                    got = core[:, k * 192 : k * 192 + 192]
                    hidden[:, base + (1 - c) * 192 : base + (1 - c) * 192 + 192] = jnp.concatenate(
                        [got[128:], got[:128]], axis=0
                    )

    def dot(k, w):
        return lax.dot_general(
            hidden[:, k * 384 : k * 384 + 384], w, (((1,), (1,)), ((), ())), preferred_element_type=F32
        )

    blocks = []
    for r in range(NZ):
        front, rear = (pieces[4], pieces[8]) if r == 4 else (pieces[r], pieces[r])
        base = 0 if r == 4 else 256
        total = dot(0, front[0:128]) + dot(1, front[128:256])
        blocks.append(total + dot(2, rear[base : base + 128]) + dot(3, rear[base + 128 : base + 256]))
    for y in range(2):
        part = jnp.concatenate([b[:, y * 64 : y * 64 + 64] for b in blocks], axis=1)
        out[:, y * 512 : y * 512 + 512] = pltpu.roll(part, where[1] * 64, 1)


def down(where, hidden, pieces):
    return pl.pallas_call(
        down_body,
        out_shape=jax.ShapeDtypeStruct((256, 1024), F32),
        in_specs=[whole(pltpu.SMEM)] + [whole()] * (len(hidden) + len(pieces)),
        out_specs=whole(),
        scratch_shapes=[VMEM((256, 1536), BF16)],
        compiler_params=pltpu.CompilerParams(vmem_limit_bytes=12 << 20),
        cost_estimate=pl.CostEstimate(flops=2 * 256 * 1536 * 1024, bytes_accessed=5 << 20, transcendentals=0),
        name="down",
    )(where, *hidden, *pieces)


def mix_body(where, mine, theirs, info, slot_route, limit, out, slots):
    @pl.when(pl.program_id(0) == 0)
    def _():
        slot = lax.broadcasted_iota(I32, (CAP, 1), 0).astype(F32)
        scale = jnp.where(slot < limit[0:1, 0:1], slot_route[:, 0:1], 0.0)
        for ref, column in ((mine, where[3]), (theirs, 1 - where[3])):
            scaled = (ref[...] * scale).astype(BF16)
            for y in range(2):
                at = pl.multiple_of(y * 1024 + column * 512, 512)
                slots[:, pl.ds(at, 512)] = scaled[:, y * 512 : y * 512 + 512]

    picked = table(info).astype(BF16)
    mixed = lax.dot_general(picked, slots[...], (((0,), (0,)), ((), ())), preferred_element_type=F32)
    out[...] = mixed.astype(BF16)


def mix(where, mine, theirs, info, slot_route, limit):
    n, step = info.shape[1], 256
    return pl.pallas_call(
        mix_body,
        out_shape=jax.ShapeDtypeStruct((n, 2048), BF16),
        grid_spec=pltpu.PrefetchScalarGridSpec(
            num_scalar_prefetch=1,
            grid=(n // step,),
            in_specs=[
                pl.BlockSpec((CAP, 1024), lambda i, w: (0, 0)),
                pl.BlockSpec((CAP, 1024), lambda i, w: (0, 0)),
                pl.BlockSpec((8, step), lambda i, w: (0, i)),
                pl.BlockSpec((CAP, 128), lambda i, w: (0, 0)),
                pl.BlockSpec((8, 128), lambda i, w: (0, 0)),
            ],
            out_specs=pl.BlockSpec((step, 2048), lambda i, w: (i, 0)),
            scratch_shapes=[VMEM((CAP, 2048), BF16)],
        ),
        compiler_params=pltpu.CompilerParams(vmem_limit_bytes=16 << 20),
        cost_estimate=pl.CostEstimate(flops=2 * n * CAP * 2048, bytes_accessed=6 << 20, transcendentals=0),
        name="mix",
    )(where, mine, theirs, info, slot_route, limit)


def with_counts(units):
    return jnp.concatenate([u[:128] for u in units] + [u[128:] for u in units], axis=0)


def together(*arrays):
    return lax.optimization_barrier(arrays)


def HIDDEN_FAR(a):
    pairs = [(k, 3 - k) for k in range(4)]
    return lax.ppermute(a, ("xl", "ha"), pairs)


def per_device(tokens, expert_ids, keep_mask, route_weight, gate_weight, up_weight, down_weight):
    y, xl, z, c, ha = (lax.axis_index(a) for a in ("y", "xl", "z", "c", "ha"))
    me = y * 32 + xl * 16 + z * 2 + c
    shift = lax.rem(2 * ha - y + NY, NY)
    where = jnp.stack([y, z, xl, c, me, lax.axis_size(WA) * CAP // 2])
    sources = (expert_ids.T, keep_mask.T, route_weight.T, gate_weight, up_weight, down_weight)
    info, packed = prep(*(pltpu.with_memory_space_constraint(a, pltpu.HBM) for a in sources))
    arrived = lax.all_to_all(packed, ("xl", "c"), split_axis=0, concat_axis=0, tiled=True)
    slot_rows, slot_route = gather_rows(where, pltpu.with_memory_space_constraint(tokens, pltpu.HBM), info)

    lane = lax.broadcasted_iota(I32, (8, 384), 1)
    tile = jnp.zeros((8, 384), BF16)
    for j in range(4):
        tile = jnp.where(lane == j, arrived[j, 32:40], tile)
    unit = jnp.concatenate([arrived[:, :32].reshape(128, 384), tile], axis=0)
    picked = lax.dynamic_slice_in_dim(arrived, 2 * c, 2, axis=0)[:, 40:]
    rows = jnp.concatenate([picked[0, :32], picked[1, :32], picked[0, 32:], picked[1, 32:]], axis=0)

    b1, a1 = Z(1)(unit), Z(-1)(unit)
    d_back, d_ahead, d_far = Y(1)(rows), Y(-1)(rows), Y(2)(rows)
    b1, a1, slot_rows = together(b1, a1, slot_rows)
    b2, a2 = Z(1)(b1), Z(-1)(a1)
    neighbour_rows = across_x(slot_rows)

    turned = [rows, d_ahead, d_far, d_back]
    ordered = []
    for j in range(4):
        pick = turned[j]
        for s in range(1, 4):
            pick = jnp.where(shift == s, turned[(j + s) % 4], pick)
        ordered.append(pick)

    def halves(p, q):
        return jnp.concatenate([p[:64], q[:64], p[64:], q[64:]], axis=0)

    d_swap = HA(halves(ordered[2], ordered[3]))
    b2, a2, d_swap = together(b2, a2, d_swap)

    d0 = jnp.concatenate([halves(ordered[0], ordered[1]), d_swap], axis=0)
    up1, dn1 = Z(1)(jnp.concatenate([d0, b2], axis=0)), Z(-1)(jnp.concatenate([d0, a2], axis=0))
    first = with_counts([unit, b1, a1, b2, a2])
    f_back, f_ahead = Y(1)(first), Y(-1)(first)
    up1, dn1, f_back, f_ahead, neighbour_rows = together(up1, dn1, f_back, f_ahead, neighbour_rows)

    up2, dn2 = Z(1)(up1), Z(-1)(dn1[:512])
    second = with_counts([up1[512:], dn1[512:]])
    g_back = Y(1)(jnp.concatenate([second[:256], f_back[:384], second[256:]], axis=0))
    g_ahead = Y(-1)(jnp.concatenate([second[:256], f_ahead[384:640], second[256:], f_ahead[640:]], axis=0))
    core_rows, far_rows = C(slot_rows), C(neighbour_rows)
    up2, dn2, g_back, g_ahead, core_rows, far_rows = together(up2, dn2, g_back, g_ahead, core_rows, far_rows)

    last = up2[512:]
    up3, dn3 = Z(1)(up2[:512]), Z(-1)(dn2)
    k_back = Y(1)(jnp.concatenate([last[:128], g_back[:128], last[128:]], axis=0))
    k_ahead = Y(-1)(jnp.concatenate([last[:128], g_ahead[128:256], last[128:], g_ahead[512:528]], axis=0))
    k_far = Y(2)(last)
    near = (first, second, last, f_back, f_ahead, g_back, g_ahead)
    partial, x_far = gate_up_near(*near, slot_rows, core_rows, neighbour_rows, far_rows)
    k_back, k_ahead, k_far, up3, dn3, partial, x_far = together(k_back, k_ahead, k_far, up3, dn3, partial, x_far)

    de0, de1 = Z(1)(up3[:256]), Z(-1)(dn3[256:])
    h_own, h_other, limit = gate_up_far(where, partial, x_far, k_back, k_ahead, k_far, *near)
    h_near, h_ha, h_far = XL(h_other), HA(h_own), HIDDEN_FAR(h_other)
    h_near, h_ha, h_far, de0, de1 = together(h_near, h_ha, h_far, de0, de1)
    core = C(jnp.concatenate([h_own, h_near, h_ha, h_far], axis=1))
    pieces = [d0, dn1, dn2, dn3, de0, up3, up2, up1, de1]
    total = down(where, (h_own, h_near, h_ha, h_far, core), pieces)
    other = C(total[128:])
    return mix(where, total[:128], other, info, slot_route, limit)


def solution(mesh):
    finer = Mesh(mesh.devices.reshape(NY, 2, NZ, 2, mesh.shape["ha"]), ("y", "xl", "z", "c", "ha"))
    placed = (P(WA, None),) * 4 + (P(WA, "ha"),) * 3
    return jax.shard_map(per_device, mesh=finer, in_specs=placed, out_specs=P(WA, "ha"), check_vma=False)
```

```python
import jax
import jax.numpy as jnp
from jax import lax
from jax.experimental import pallas as pl
from jax.experimental.pallas import tpu as pltpu
from jax.sharding import Mesh
from jax.sharding import PartitionSpec as P

CAP = 128
WA = ("y", "xl", "z", "c")
NY, NZ = 4, 8
F32, BF16, I32 = jnp.float32, jnp.bfloat16, jnp.int32
VMEM = pltpu.VMEM


def whole(memory_space=VMEM):
    return pl.BlockSpec(memory_space=memory_space)


def ring(axis, n, k):
    return lambda a: lax.ppermute(a, axis, [(i, (i + k) % n) for i in range(n)])


def Z(k):
    return ring("z", NZ, k)


def Y(k):
    return ring("y", NY, k)


def C(a):
    return lax.ppermute(a, "c", [(0, 1), (1, 0)])


def XL(a):
    return lax.ppermute(a, "xl", [(0, 1), (1, 0)])


def HA(a):
    return lax.ppermute(a, "ha", [(0, 1), (1, 0)])


def across_x(a):
    def at(x, c):
        return (x % 2) * 4 + c * 2 + x // 2

    pairs = [(at(x, c), at((x + 1 - 2 * c) % 4, c)) for x in range(4) for c in range(2)]
    return lax.ppermute(a, ("xl", "c", "ha"), pairs)


def prep_body(*refs):
    where, far, (info, packed), near, arrive = refs[0], refs[1:7], refs[7:9], refs[9:15], refs[15]
    copies = [pltpu.make_async_copy(f, n, arrive.at[i]) for i, (f, n) in enumerate(zip(far, near))]
    for copy in copies:
        copy.start()
    for copy in copies:
        copy.wait()
    ids, keep, rw, gate, up, down_rows = near
    hit = (ids[...] == 0) & (keep[...] == 1)
    chosen = jnp.max(jnp.where(hit, 1.0, 0.0), axis=0, keepdims=True)
    route = jnp.sum(jnp.where(hit, rw[...], 0.0), axis=0, keepdims=True)
    n = chosen.shape[1]
    row = lax.broadcasted_iota(I32, (n, n), 0)
    col = lax.broadcasted_iota(I32, (n, n), 1)
    before = jnp.where(row < col, 1.0, 0.0).astype(BF16)
    ones = jnp.broadcast_to(chosen, (16, n)).astype(BF16)
    position = jnp.dot(ones, before, preferred_element_type=F32)[:1]
    info[0:1, :] = position
    info[1:2, :] = chosen
    info[2:3, :] = route
    info[3:8, :] = jnp.zeros((5, n), F32)
    total = jnp.sum(chosen, axis=1, keepdims=True)
    for q in range(4):
        at = slice(q * 192, q * 192 + 192)
        to = where[2] * 2 + where[3]
        to = q + to - 2 * (q & to)
        packed[to, 0:32, :] = jnp.concatenate([gate[:, at], up[:, at]], axis=1)
        packed[to, 32:40, :] = jnp.broadcast_to(total, (8, 384)).astype(BF16)
        packed[to, 40:72, :] = down_rows[:, :384]
        packed[to, 72:104, :] = down_rows[:, 384:]


def prep(where, ids, keep, rw, gate, up, down_rows):
    n = ids.shape[1]
    return pl.pallas_call(
        prep_body,
        out_shape=(jax.ShapeDtypeStruct((8, n), F32), jax.ShapeDtypeStruct((4, 104, 384), BF16)),
        in_specs=[whole(pltpu.SMEM)] + [whole(pltpu.HBM)] * 6,
        out_specs=(whole(), whole()),
        scratch_shapes=[VMEM(a.shape, a.dtype) for a in (ids, keep, rw, gate, up, down_rows)]
        + [pltpu.SemaphoreType.DMA((6,))],
        compiler_params=pltpu.CompilerParams(vmem_limit_bytes=12 << 20),
        cost_estimate=pl.CostEstimate(flops=2 * 16 * n * n, bytes_accessed=4 * 32 * n, transcendentals=0),
        name="prep",
    )(where, ids, keep, rw, gate, up, down_rows)


def table(info):
    slot = lax.broadcasted_iota(I32, (CAP, info.shape[1]), 0).astype(F32)
    return (info[0:1, :] == slot) & (info[1:2, :] > 0.5)


def gather_body(where, tokens, info, out, slot_route, near, arrive):
    n, width = near.shape[1:]
    copies = [
        pltpu.make_async_copy(tokens.at[:, i * width : (i + 1) * width], near.at[i], arrive.at[i]) for i in range(NY)
    ]
    for copy in copies:
        copy.start()
    picked = table(info)
    got = jnp.sum(jnp.where(picked, info[2:3, :], 0.0), axis=1, keepdims=True)
    slot_route[...] = jnp.broadcast_to(got, slot_route.shape)
    one_hot = picked.astype(BF16)
    for block in range(NY):
        copies[block].wait()
        rows = jnp.dot(one_hot, near[block], preferred_element_type=F32).astype(BF16)
        ky = lax.rem(block - where[0] + NY, NY)
        yi = jnp.where(ky == 0, 0, jnp.where(ky == 3, 1, jnp.where(ky == 1, 2, 3)))
        for z in range(NZ):
            kz = lax.rem(z - where[1] + NZ, NZ)
            zi = jnp.where(kz == 0, 0, jnp.where(kz <= 3, 2 * kz, jnp.where(kz == 4, 7, 15 - 2 * kz)))
            piece = jnp.concatenate([rows[:, z * 64 : z * 64 + 64], rows[:, 512 + z * 64 : 576 + z * 64]], axis=1)
            out[:, pl.ds(pl.multiple_of((yi * NZ + zi) * 128, 128), 128)] = piece


def gather_rows(where, tokens, info):
    n, d = tokens.shape
    return pl.pallas_call(
        gather_body,
        out_shape=(jax.ShapeDtypeStruct((CAP, d), BF16), jax.ShapeDtypeStruct((CAP, 128), F32)),
        in_specs=[whole(pltpu.SMEM), whole(pltpu.HBM), whole()],
        out_specs=(whole(), whole()),
        scratch_shapes=[VMEM((NY, n, d // NY), tokens.dtype), pltpu.SemaphoreType.DMA((NY,))],
        compiler_params=pltpu.CompilerParams(vmem_limit_bytes=16 << 20),
        cost_estimate=pl.CostEstimate(flops=2 * CAP * n * d, bytes_accessed=2 * n * d, transcendentals=0),
        name="gather_rows",
    )(where, tokens, info)


def near_body(first, second, last, f_back, f_ahead, g_back, g_ahead, xo, xc, xn, xnc, total, x_far, x_all):
    for i, ref in enumerate((xo, xc, xn, xnc)):
        at = slice(i * 128, i * 128 + 128)
        x_all[at, :] = ref[:, :3712]
        x_far[at, 0:128] = ref[:, 1920:2048]
        x_far[at, 128:256] = ref[:, 2944:3072]
        x_far[at, 256:640] = ref[:, 3712:]
    acc = jnp.zeros((512, 384), F32)
    for start, ref, row, size in (
        (0, first, 0, 640),
        (640, second, 0, 256),
        (896, last, 0, 128),
        (1024, f_back, 0, 640),
        (1664, g_back, 0, 256),
        (2048, f_ahead, 0, 640),
        (2688, g_ahead, 0, 256),
        (3072, g_back, 256, 384),
        (3456, g_ahead, 256, 256),
    ):
        acc += jnp.dot(x_all[:, start : start + size], ref[row : row + size, :], preferred_element_type=F32)
    total[...] = acc


def gate_up_near(*arrays):
    return pl.pallas_call(
        near_body,
        out_shape=(jax.ShapeDtypeStruct((512, 384), F32), jax.ShapeDtypeStruct((512, 640), BF16)),
        in_specs=[whole()] * len(arrays),
        out_specs=(whole(), whole()),
        scratch_shapes=[VMEM((512, 3712), BF16)],
        compiler_params=pltpu.CompilerParams(vmem_limit_bytes=16 << 20),
        cost_estimate=pl.CostEstimate(flops=2 * 512 * 3456 * 384, bytes_accessed=8 << 20, transcendentals=0),
        name="gate_up_near",
    )(*arrays)


def far_body(where, total, x_far, k_back, k_ahead, k_far, *refs):
    (first, second, last, f_back, f_ahead, g_back, g_ahead), (own, other, limit) = refs[:7], refs[7:]
    acc = total[...]
    for start, ref, row in ((0, k_back, 0), (128, k_ahead, 0), (256, k_back, 128), (384, k_ahead, 128), (512, k_far, 0)):
        acc += jnp.dot(x_far[:, start : start + 128], ref[row : row + 128, :], preferred_element_type=F32)
    gate, up = acc[:, :192], acc[:, 192:]
    hidden = (gate * jax.nn.sigmoid(gate) * up).astype(BF16)
    own[...] = hidden[:256]
    other[...] = hidden[256:]

    lane = lax.broadcasted_iota(I32, (8, 128), 1)
    quad = lax.shift_right_logical(lane, 1) * 16 + (lane & 1)
    earlier = jnp.zeros((8, 128), F32)
    groups = (
        (0, first[640:680, 0:128], second[256:272, 0:128], last[128:136, 0:128]),
        (3, f_back[640:680, 0:128], g_back[640:656, 0:128], k_back[256:264, 0:128]),
        (1, f_ahead[640:680, 0:128], g_ahead[512:528, 0:128], k_ahead[256:264, 0:128]),
        (2, g_ahead[528:568, 0:128], k_ahead[264:280, 0:128], k_far[128:136, 0:128]),
    )
    for ky, *parts in groups:
        tiles = jnp.concatenate([part.astype(F32) for part in parts], axis=0)
        for zi, kz in enumerate((0, 7, 1, 6, 2, 5, 3, 4)):
            block = ((where[0] + ky) & 3) * 32 + ((where[1] + kz) & 7) * 2 + quad
            counted = (block < where[4]) & (lane < 4)
            earlier += jnp.where(counted, tiles[zi * 8 : zi * 8 + 8], 0.0)
    before = jnp.sum(earlier[0:1], axis=1, keepdims=True)
    limit[...] = jnp.broadcast_to(where[5].astype(F32) - before, limit.shape)


def gate_up_far(*arrays):
    half = jax.ShapeDtypeStruct((256, 192), BF16)
    return pl.pallas_call(
        far_body,
        out_shape=(half, half, jax.ShapeDtypeStruct((8, 128), F32)),
        in_specs=[whole(pltpu.SMEM)] + [whole()] * (len(arrays) - 1),
        out_specs=(whole(), whole(), whole()),
        compiler_params=pltpu.CompilerParams(vmem_limit_bytes=16 << 20),
        cost_estimate=pl.CostEstimate(flops=2 * 512 * 640 * 384, bytes_accessed=3 << 20, transcendentals=512 * 192),
        name="gate_up_far",
    )(*arrays)


def down_body(where, own, near, ha, far, core, *refs):
    pieces, (out, hidden) = refs[:-2], refs[-2:]

    for xl in range(2):
        for c in range(2):

            @pl.when((where[2] == xl) & (where[3] == c))
            def _():
                for k, ref in enumerate((own, near, ha, far)):
                    pair = xl if k % 2 == 0 else 1 - xl
                    base = (k // 2) * 768 + pair * 384
                    hidden[:, base + c * 192 : base + c * 192 + 192] = ref[...]
                    got = core[:, k * 192 : k * 192 + 192]
                    hidden[:, base + (1 - c) * 192 : base + (1 - c) * 192 + 192] = jnp.concatenate(
                        [got[128:], got[:128]], axis=0
                    )

    def dot(k, w):
        return lax.dot_general(
            hidden[:, k * 384 : k * 384 + 384], w, (((1,), (1,)), ((), ())), preferred_element_type=F32
        )

    blocks = []
    for r in range(NZ):
        front, rear = (pieces[4], pieces[8]) if r == 4 else (pieces[r], pieces[r])
        base = 0 if r == 4 else 256
        total = dot(0, front[0:128]) + dot(1, front[128:256])
        blocks.append(total + dot(2, rear[base : base + 128]) + dot(3, rear[base + 128 : base + 256]))
    for y in range(2):
        part = jnp.concatenate([b[:, y * 64 : y * 64 + 64] for b in blocks], axis=1)
        out[:, y * 512 : y * 512 + 512] = pltpu.roll(part, where[1] * 64, 1)


def down(where, hidden, pieces):
    return pl.pallas_call(
        down_body,
        out_shape=jax.ShapeDtypeStruct((256, 1024), F32),
        in_specs=[whole(pltpu.SMEM)] + [whole()] * (len(hidden) + len(pieces)),
        out_specs=whole(),
        scratch_shapes=[VMEM((256, 1536), BF16)],
        compiler_params=pltpu.CompilerParams(vmem_limit_bytes=12 << 20),
        cost_estimate=pl.CostEstimate(flops=2 * 256 * 1536 * 1024, bytes_accessed=5 << 20, transcendentals=0),
        name="down",
    )(where, *hidden, *pieces)


def mix_body(where, mine, theirs, info, slot_route, limit, out, slots):
    @pl.when(pl.program_id(0) == 0)
    def _():
        slot = lax.broadcasted_iota(I32, (CAP, 1), 0).astype(F32)
        scale = jnp.where(slot < limit[0:1, 0:1], slot_route[:, 0:1], 0.0)
        for ref, column in ((mine, where[3]), (theirs, 1 - where[3])):
            scaled = (ref[...] * scale).astype(BF16)
            for y in range(2):
                at = pl.multiple_of(y * 1024 + column * 512, 512)
                slots[:, pl.ds(at, 512)] = scaled[:, y * 512 : y * 512 + 512]

    picked = table(info).astype(BF16)
    mixed = lax.dot_general(picked, slots[...], (((0,), (0,)), ((), ())), preferred_element_type=F32)
    out[...] = mixed.astype(BF16)


def mix(where, mine, theirs, info, slot_route, limit):
    n, step = info.shape[1], 256
    return pl.pallas_call(
        mix_body,
        out_shape=jax.ShapeDtypeStruct((n, 2048), BF16),
        grid_spec=pltpu.PrefetchScalarGridSpec(
            num_scalar_prefetch=1,
            grid=(n // step,),
            in_specs=[
                pl.BlockSpec((CAP, 1024), lambda i, w: (0, 0)),
                pl.BlockSpec((CAP, 1024), lambda i, w: (0, 0)),
                pl.BlockSpec((8, step), lambda i, w: (0, i)),
                pl.BlockSpec((CAP, 128), lambda i, w: (0, 0)),
                pl.BlockSpec((8, 128), lambda i, w: (0, 0)),
            ],
            out_specs=pl.BlockSpec((step, 2048), lambda i, w: (i, 0)),
            scratch_shapes=[VMEM((CAP, 2048), BF16)],
        ),
        compiler_params=pltpu.CompilerParams(vmem_limit_bytes=16 << 20),
        cost_estimate=pl.CostEstimate(flops=2 * n * CAP * 2048, bytes_accessed=6 << 20, transcendentals=0),
        name="mix",
    )(where, mine, theirs, info, slot_route, limit)


def with_counts(units):
    return jnp.concatenate([u[:128] for u in units] + [u[128:] for u in units], axis=0)


def together(*arrays):
    return lax.optimization_barrier(arrays)


def HIDDEN_FAR(a):
    pairs = [(k, 3 - k) for k in range(4)]
    return lax.ppermute(a, ("xl", "ha"), pairs)


def per_device(tokens, expert_ids, keep_mask, route_weight, gate_weight, up_weight, down_weight):
    y, xl, z, c, ha = (lax.axis_index(a) for a in ("y", "xl", "z", "c", "ha"))
    me = y * 32 + xl * 16 + z * 2 + c
    shift = lax.rem(2 * ha - y + NY, NY)
    where = jnp.stack([y, z, xl, c, me, lax.axis_size(WA) * CAP // 2])
    sources = (expert_ids.T, keep_mask.T, route_weight.T, gate_weight, up_weight, down_weight)
    info, packed = prep(where, *(pltpu.with_memory_space_constraint(a, pltpu.HBM) for a in sources))
    both = [(k, 3 - k) for k in range(4)]
    tiles = [packed[0], C(packed[1]), XL(packed[2]), lax.ppermute(packed[3], ("xl", "c"), both)]
    tiles = [jnp.where(c == 0, tiles[k], tiles[k ^ 1]) for k in range(4)]
    arrived = jnp.stack([jnp.where(xl == 0, tiles[k], tiles[k ^ 2]) for k in range(4)])
    slot_rows, slot_route = gather_rows(where, pltpu.with_memory_space_constraint(tokens, pltpu.HBM), info)

    lane = lax.broadcasted_iota(I32, (8, 384), 1)
    tile = jnp.zeros((8, 384), BF16)
    for j in range(4):
        tile = jnp.where(lane == j, arrived[j, 32:40], tile)
    unit = jnp.concatenate([arrived[:, :32].reshape(128, 384), tile], axis=0)
    picked = lax.dynamic_slice_in_dim(arrived, 2 * c, 2, axis=0)[:, 40:]
    rows = jnp.concatenate([picked[0, :32], picked[1, :32], picked[0, 32:], picked[1, 32:]], axis=0)

    b1, a1 = Z(1)(unit), Z(-1)(unit)
    d_back, d_ahead, d_far = Y(1)(rows), Y(-1)(rows), Y(2)(rows)
    b1, a1, slot_rows = together(b1, a1, slot_rows)
    b2, a2 = Z(1)(b1), Z(-1)(a1)
    neighbour_rows = across_x(slot_rows)

    turned = [rows, d_ahead, d_far, d_back]
    ordered = []
    for j in range(4):
        pick = turned[j]
        for s in range(1, 4):
            pick = jnp.where(shift == s, turned[(j + s) % 4], pick)
        ordered.append(pick)

    def halves(p, q):
        return jnp.concatenate([p[:64], q[:64], p[64:], q[64:]], axis=0)

    d_swap = HA(halves(ordered[2], ordered[3]))
    core_rows = C(slot_rows)
    b2, a2, d_swap, core_rows = together(b2, a2, d_swap, core_rows)

    d0 = jnp.concatenate([halves(ordered[0], ordered[1]), d_swap], axis=0)
    up1, dn1 = Z(1)(jnp.concatenate([d0, b2], axis=0)), Z(-1)(jnp.concatenate([d0, a2], axis=0))
    first = with_counts([unit, b1, a1, b2, a2])
    f_back, f_ahead = Y(1)(first), Y(-1)(first)
    up1, dn1 = together(up1, dn1)
    f_back, f_ahead, neighbour_rows = together(f_back, f_ahead, neighbour_rows)

    up2, dn2 = Z(1)(up1[:576]), Z(-1)(jnp.concatenate([dn1[:512], dn1[576:]], axis=0))
    second = with_counts([up1[512:], dn1[512:]])
    g_back = Y(1)(jnp.concatenate([second[:256], f_back[:384], second[256:]], axis=0))
    g_ahead = Y(-1)(jnp.concatenate([second[:256], f_ahead[384:640], second[256:], f_ahead[640:]], axis=0))
    far_rows = C(neighbour_rows)
    up2, dn2 = together(up2, dn2)
    g_back, g_ahead, far_rows = together(g_back, g_ahead, far_rows)

    last = jnp.concatenate([up2[512:], dn2[512:]], axis=0)
    up3, dn3 = Z(1)(up2[:512]), Z(-1)(dn2[:512])
    k_back = Y(1)(jnp.concatenate([last[:128], g_back[:128], last[128:]], axis=0))
    k_ahead = Y(-1)(jnp.concatenate([last[:128], g_ahead[128:256], last[128:], g_ahead[512:528]], axis=0))
    k_far = Y(2)(last)
    near = (first, second, last, f_back, f_ahead, g_back, g_ahead)
    partial, x_far = gate_up_near(*near, slot_rows, core_rows, neighbour_rows, far_rows)
    k_back, k_ahead, k_far, partial, x_far = together(k_back, k_ahead, k_far, partial, x_far)
    up3, dn3 = together(up3, dn3)

    de0, de1 = Z(1)(up3[:256]), Z(-1)(dn3[256:])
    h_own, h_other, limit = gate_up_far(where, partial, x_far, k_back, k_ahead, k_far, *near)
    h_near, h_ha, h_far = XL(h_other), HA(h_own), HIDDEN_FAR(h_other)
    h_near, h_ha, h_far, de0, de1 = together(h_near, h_ha, h_far, de0, de1)
    core = C(jnp.concatenate([h_own, h_near, h_ha, h_far], axis=1))
    pieces = [d0, dn1, dn2, dn3, de0, up3, up2, up1, de1]
    total = down(where, (h_own, h_near, h_ha, h_far, core), pieces)
    other = C(total[128:])
    return mix(where, total[:128], other, info, slot_route, limit)


def solution(mesh):
    finer = Mesh(mesh.devices.reshape(NY, 2, NZ, 2, mesh.shape["ha"]), ("y", "xl", "z", "c", "ha"))
    placed = (P(WA, None),) * 4 + (P(WA, "ha"),) * 3
    return jax.shard_map(per_device, mesh=finer, in_specs=placed, out_specs=P(WA, "ha"), check_vma=False)
```

```python
import jax
import jax.numpy as jnp
from jax import lax
from jax.experimental import pallas as pl
from jax.experimental.pallas import tpu as pltpu
from jax.sharding import Mesh
from jax.sharding import PartitionSpec as P

CAP = 128
WA = ("y", "xl", "z", "c")
NY, NZ = 4, 8
F32, BF16, I32 = jnp.float32, jnp.bfloat16, jnp.int32
VMEM = pltpu.VMEM


def whole(memory_space=VMEM):
    return pl.BlockSpec(memory_space=memory_space)


def ring(axis, n, k):
    return lambda a: lax.ppermute(a, axis, [(i, (i + k) % n) for i in range(n)])


def Z(k):
    return ring("z", NZ, k)


def Y(k):
    return ring("y", NY, k)


def C(a):
    return lax.ppermute(a, "c", [(0, 1), (1, 0)])


def XL(a):
    return lax.ppermute(a, "xl", [(0, 1), (1, 0)])


def HA(a):
    return lax.ppermute(a, "ha", [(0, 1), (1, 0)])


def across_x(a):
    def at(x, c):
        return (x % 2) * 4 + c * 2 + x // 2

    pairs = [(at(x, c), at((x + 1 - 2 * c) % 4, c)) for x in range(4) for c in range(2)]
    return lax.ppermute(a, ("xl", "c", "ha"), pairs)


def prep_body(*refs):
    where, far, (info, packed), near, arrive = refs[0], refs[1:7], refs[7:9], refs[9:15], refs[15]
    copies = [pltpu.make_async_copy(f, n, arrive.at[i]) for i, (f, n) in enumerate(zip(far, near))]
    for copy in copies:
        copy.start()
    for copy in copies:
        copy.wait()
    ids, keep, rw, gate, up, down_rows = near
    hit = (ids[...] == 0) & (keep[...] == 1)
    chosen = jnp.max(jnp.where(hit, 1.0, 0.0), axis=0, keepdims=True)
    route = jnp.sum(jnp.where(hit, rw[...], 0.0), axis=0, keepdims=True)
    n = chosen.shape[1]
    row = lax.broadcasted_iota(I32, (n, n), 0)
    col = lax.broadcasted_iota(I32, (n, n), 1)
    before = jnp.where(row < col, 1.0, 0.0).astype(BF16)
    ones = jnp.broadcast_to(chosen, (16, n)).astype(BF16)
    position = jnp.dot(ones, before, preferred_element_type=F32)[:1]
    info[0:1, :] = position
    info[1:2, :] = chosen
    info[2:3, :] = route
    info[3:8, :] = jnp.zeros((5, n), F32)
    total = jnp.sum(chosen, axis=1, keepdims=True)
    for q in range(4):
        at = slice(q * 192, q * 192 + 192)
        to = where[2] * 2 + where[3]
        to = q + to - 2 * (q & to)
        packed[to, 0:32, :] = jnp.concatenate([gate[:, at], up[:, at]], axis=1)
        packed[to, 32:40, :] = jnp.broadcast_to(total, (8, 384)).astype(BF16)
        packed[to, 40:72, :] = down_rows[:, :384]
        packed[to, 72:104, :] = down_rows[:, 384:]


def prep(where, ids, keep, rw, gate, up, down_rows):
    n = ids.shape[1]
    return pl.pallas_call(
        prep_body,
        out_shape=(jax.ShapeDtypeStruct((8, n), F32), jax.ShapeDtypeStruct((4, 104, 384), BF16)),
        in_specs=[whole(pltpu.SMEM)] + [whole(pltpu.HBM)] * 6,
        out_specs=(whole(), whole()),
        scratch_shapes=[VMEM(a.shape, a.dtype) for a in (ids, keep, rw, gate, up, down_rows)]
        + [pltpu.SemaphoreType.DMA((6,))],
        compiler_params=pltpu.CompilerParams(vmem_limit_bytes=12 << 20),
        cost_estimate=pl.CostEstimate(flops=2 * 16 * n * n, bytes_accessed=4 * 32 * n, transcendentals=0),
        name="prep",
    )(where, ids, keep, rw, gate, up, down_rows)


def table(info):
    slot = lax.broadcasted_iota(I32, (CAP, info.shape[1]), 0).astype(F32)
    return (info[0:1, :] == slot) & (info[1:2, :] > 0.5)


def gather_body(where, tokens, info, out, slot_route, near, arrive):
    n, width = near.shape[1:]
    copies = [
        pltpu.make_async_copy(tokens.at[:, i * width : (i + 1) * width], near.at[i], arrive.at[i]) for i in range(NY)
    ]
    for copy in copies:
        copy.start()
    picked = table(info)
    got = jnp.sum(jnp.where(picked, info[2:3, :], 0.0), axis=1, keepdims=True)
    slot_route[...] = jnp.broadcast_to(got, slot_route.shape)
    one_hot = picked.astype(BF16)
    for block in range(NY):
        copies[block].wait()
        rows = jnp.dot(one_hot, near[block], preferred_element_type=F32).astype(BF16)
        ky = lax.rem(block - where[0] + NY, NY)
        yi = jnp.where(ky == 0, 0, jnp.where(ky == 3, 1, jnp.where(ky == 1, 2, 3)))
        for z in range(NZ):
            kz = lax.rem(z - where[1] + NZ, NZ)
            zi = jnp.where(kz == 0, 0, jnp.where(kz <= 3, 2 * kz, jnp.where(kz == 4, 7, 15 - 2 * kz)))
            piece = jnp.concatenate([rows[:, z * 64 : z * 64 + 64], rows[:, 512 + z * 64 : 576 + z * 64]], axis=1)
            out[:, pl.ds(pl.multiple_of((yi * NZ + zi) * 128, 128), 128)] = piece


def gather_rows(where, tokens, info):
    n, d = tokens.shape
    return pl.pallas_call(
        gather_body,
        out_shape=(jax.ShapeDtypeStruct((CAP, d), BF16), jax.ShapeDtypeStruct((CAP, 128), F32)),
        in_specs=[whole(pltpu.SMEM), whole(pltpu.HBM), whole()],
        out_specs=(whole(), whole()),
        scratch_shapes=[VMEM((NY, n, d // NY), tokens.dtype), pltpu.SemaphoreType.DMA((NY,))],
        compiler_params=pltpu.CompilerParams(vmem_limit_bytes=16 << 20),
        cost_estimate=pl.CostEstimate(flops=2 * CAP * n * d, bytes_accessed=2 * n * d, transcendentals=0),
        name="gather_rows",
    )(where, tokens, info)


def near_body(first, second, last, f_back, f_ahead, g_back, g_ahead, xo, xc, xn, xnc, total, x_far, x_all):
    for i, ref in enumerate((xo, xc, xn, xnc)):
        at = slice(i * 128, i * 128 + 128)
        x_all[at, :] = ref[:, :3712]
        x_far[at, 0:128] = ref[:, 1920:2048]
        x_far[at, 128:256] = ref[:, 2944:3072]
        x_far[at, 256:640] = ref[:, 3712:]
    acc = jnp.zeros((512, 384), F32)
    for start, ref, row, size in (
        (0, first, 0, 640),
        (640, second, 0, 256),
        (896, last, 0, 128),
        (1024, f_back, 0, 640),
        (1664, g_back, 0, 256),
        (2048, f_ahead, 0, 640),
        (2688, g_ahead, 0, 256),
        (3072, g_back, 256, 384),
        (3456, g_ahead, 256, 256),
    ):
        acc += jnp.dot(x_all[:, start : start + size], ref[row : row + size, :], preferred_element_type=F32)
    total[...] = acc


def gate_up_near(*arrays):
    return pl.pallas_call(
        near_body,
        out_shape=(jax.ShapeDtypeStruct((512, 384), F32), jax.ShapeDtypeStruct((512, 640), BF16)),
        in_specs=[whole()] * len(arrays),
        out_specs=(whole(), whole()),
        scratch_shapes=[VMEM((512, 3712), BF16)],
        compiler_params=pltpu.CompilerParams(vmem_limit_bytes=16 << 20),
        cost_estimate=pl.CostEstimate(flops=2 * 512 * 3456 * 384, bytes_accessed=8 << 20, transcendentals=0),
        name="gate_up_near",
    )(*arrays)


def far_body(where, total, x_far, k_back, k_ahead, k_far, *refs):
    (first, second, last, f_back, f_ahead, g_back, g_ahead), (own, other, limit) = refs[:7], refs[7:]
    acc = total[...]
    for start, ref, row in ((0, k_back, 0), (128, k_ahead, 0), (256, k_back, 128), (384, k_ahead, 128), (512, k_far, 0)):
        acc += jnp.dot(x_far[:, start : start + 128], ref[row : row + 128, :], preferred_element_type=F32)
    gate, up = acc[:, :192], acc[:, 192:]
    hidden = (gate * jax.nn.sigmoid(gate) * up).astype(BF16)
    own[...] = hidden[:256]
    other[...] = hidden[256:]

    lane = lax.broadcasted_iota(I32, (8, 128), 1)
    quad = lax.shift_right_logical(lane, 1) * 16 + (lane & 1)
    earlier = jnp.zeros((8, 128), F32)
    groups = (
        (0, first[640:680, 0:128], second[256:272, 0:128], last[128:136, 0:128]),
        (3, f_back[640:680, 0:128], g_back[640:656, 0:128], k_back[256:264, 0:128]),
        (1, f_ahead[640:680, 0:128], g_ahead[512:528, 0:128], k_ahead[256:264, 0:128]),
        (2, g_ahead[528:568, 0:128], k_ahead[264:280, 0:128], k_far[128:136, 0:128]),
    )
    for ky, *parts in groups:
        tiles = jnp.concatenate([part.astype(F32) for part in parts], axis=0)
        for zi, kz in enumerate((0, 7, 1, 6, 2, 5, 3, 4)):
            block = ((where[0] + ky) & 3) * 32 + ((where[1] + kz) & 7) * 2 + quad
            counted = (block < where[4]) & (lane < 4)
            earlier += jnp.where(counted, tiles[zi * 8 : zi * 8 + 8], 0.0)
    before = jnp.sum(earlier[0:1], axis=1, keepdims=True)
    limit[...] = jnp.broadcast_to(where[5].astype(F32) - before, limit.shape)


def gate_up_far(*arrays):
    half = jax.ShapeDtypeStruct((256, 192), BF16)
    return pl.pallas_call(
        far_body,
        out_shape=(half, half, jax.ShapeDtypeStruct((8, 128), F32)),
        in_specs=[whole(pltpu.SMEM)] + [whole()] * (len(arrays) - 1),
        out_specs=(whole(), whole(), whole()),
        compiler_params=pltpu.CompilerParams(vmem_limit_bytes=16 << 20),
        cost_estimate=pl.CostEstimate(flops=2 * 512 * 640 * 384, bytes_accessed=3 << 20, transcendentals=512 * 192),
        name="gate_up_far",
    )(*arrays)


def down_body(where, own, near, ha, far, core, *refs):
    pieces, (out, hidden) = refs[:-2], refs[-2:]

    for xl in range(2):
        for c in range(2):

            @pl.when((where[2] == xl) & (where[3] == c))
            def _():
                for k, ref in enumerate((own, near, ha, far)):
                    pair = xl if k % 2 == 0 else 1 - xl
                    base = (k // 2) * 768 + pair * 384
                    hidden[:, base + c * 192 : base + c * 192 + 192] = ref[...]
                    got = core[:, k * 192 : k * 192 + 192]
                    hidden[:, base + (1 - c) * 192 : base + (1 - c) * 192 + 192] = jnp.concatenate(
                        [got[128:], got[:128]], axis=0
                    )

    def dot(k, w):
        return lax.dot_general(
            hidden[:, k * 384 : k * 384 + 384], w, (((1,), (1,)), ((), ())), preferred_element_type=F32
        )

    blocks = []
    for r in range(NZ):
        front, rear = (pieces[4], pieces[8]) if r == 4 else (pieces[r], pieces[r])
        base = 0 if r == 4 else 256
        total = dot(0, front[0:128]) + dot(1, front[128:256])
        blocks.append(total + dot(2, rear[base : base + 128]) + dot(3, rear[base + 128 : base + 256]))
    for y in range(2):
        part = jnp.concatenate([b[:, y * 64 : y * 64 + 64] for b in blocks], axis=1)
        out[:, y * 512 : y * 512 + 512] = pltpu.roll(part, where[1] * 64, 1)


def down(where, hidden, pieces):
    return pl.pallas_call(
        down_body,
        out_shape=jax.ShapeDtypeStruct((256, 1024), F32),
        in_specs=[whole(pltpu.SMEM)] + [whole()] * (len(hidden) + len(pieces)),
        out_specs=whole(),
        scratch_shapes=[VMEM((256, 1536), BF16)],
        compiler_params=pltpu.CompilerParams(vmem_limit_bytes=12 << 20),
        cost_estimate=pl.CostEstimate(flops=2 * 256 * 1536 * 1024, bytes_accessed=5 << 20, transcendentals=0),
        name="down",
    )(where, *hidden, *pieces)


def mix_body(where, mine, theirs, info, slot_route, limit, out, slots):
    @pl.when(pl.program_id(0) == 0)
    def _():
        slot = lax.broadcasted_iota(I32, (CAP, 1), 0).astype(F32)
        scale = jnp.where(slot < limit[0:1, 0:1], slot_route[:, 0:1], 0.0)
        for ref, column in ((mine, where[3]), (theirs, 1 - where[3])):
            scaled = (ref[...] * scale).astype(BF16)
            for y in range(2):
                at = pl.multiple_of(y * 1024 + column * 512, 512)
                slots[:, pl.ds(at, 512)] = scaled[:, y * 512 : y * 512 + 512]

    picked = table(info).astype(BF16)
    mixed = lax.dot_general(picked, slots[...], (((0,), (0,)), ((), ())), preferred_element_type=F32)
    out[...] = mixed.astype(BF16)


def mix(where, mine, theirs, info, slot_route, limit):
    n, step = info.shape[1], 256
    return pl.pallas_call(
        mix_body,
        out_shape=jax.ShapeDtypeStruct((n, 2048), BF16),
        grid_spec=pltpu.PrefetchScalarGridSpec(
            num_scalar_prefetch=1,
            grid=(n // step,),
            in_specs=[
                pl.BlockSpec((CAP, 1024), lambda i, w: (0, 0)),
                pl.BlockSpec((CAP, 1024), lambda i, w: (0, 0)),
                pl.BlockSpec((8, step), lambda i, w: (0, i)),
                pl.BlockSpec((CAP, 128), lambda i, w: (0, 0)),
                pl.BlockSpec((8, 128), lambda i, w: (0, 0)),
            ],
            out_specs=pl.BlockSpec((step, 2048), lambda i, w: (i, 0)),
            scratch_shapes=[VMEM((CAP, 2048), BF16)],
        ),
        compiler_params=pltpu.CompilerParams(vmem_limit_bytes=16 << 20),
        cost_estimate=pl.CostEstimate(flops=2 * n * CAP * 2048, bytes_accessed=6 << 20, transcendentals=0),
        name="mix",
    )(where, mine, theirs, info, slot_route, limit)


def with_counts(units):
    return jnp.concatenate([u[:128] for u in units] + [u[128:] for u in units], axis=0)


def together(*arrays):
    return lax.optimization_barrier(arrays)


def HIDDEN_FAR(a):
    pairs = [(k, 3 - k) for k in range(4)]
    return lax.ppermute(a, ("xl", "ha"), pairs)


def per_device(tokens, expert_ids, keep_mask, route_weight, gate_weight, up_weight, down_weight):
    y, xl, z, c, ha = (lax.axis_index(a) for a in ("y", "xl", "z", "c", "ha"))
    me = y * 32 + xl * 16 + z * 2 + c
    shift = lax.rem(2 * ha - y + NY, NY)
    where = jnp.stack([y, z, xl, c, me, lax.axis_size(WA) * CAP // 2])
    sources = (expert_ids.T, keep_mask.T, route_weight.T, gate_weight, up_weight, down_weight)
    info, packed = prep(where, *(pltpu.with_memory_space_constraint(a, pltpu.HBM) for a in sources))
    both = [(k, 3 - k) for k in range(4)]
    tiles = [packed[0], C(packed[1]), XL(packed[2]), lax.ppermute(packed[3], ("xl", "c"), both)]
    tiles = [jnp.where(c == 0, tiles[k], tiles[k ^ 1]) for k in range(4)]
    arrived = jnp.stack([jnp.where(xl == 0, tiles[k], tiles[k ^ 2]) for k in range(4)])
    slot_rows, slot_route = gather_rows(where, pltpu.with_memory_space_constraint(tokens, pltpu.HBM), info)

    lane = lax.broadcasted_iota(I32, (8, 384), 1)
    tile = jnp.zeros((8, 384), BF16)
    for j in range(4):
        tile = jnp.where(lane == j, arrived[j, 32:40], tile)
    unit = jnp.concatenate([arrived[:, :32].reshape(128, 384), tile], axis=0)
    picked = lax.dynamic_slice_in_dim(arrived, 2 * c, 2, axis=0)[:, 40:]
    rows = jnp.concatenate([picked[0, :32], picked[1, :32], picked[0, 32:], picked[1, 32:]], axis=0)

    b1, a1 = Z(1)(unit), Z(-1)(unit)
    d_back, d_ahead, d_far = Y(1)(rows), Y(-1)(rows), Y(2)(rows)
    b1, a1, slot_rows, d_back, d_ahead, d_far = together(b1, a1, slot_rows, d_back, d_ahead, d_far)
    b2, a2 = Z(1)(b1), Z(-1)(a1)
    neighbour_rows = across_x(slot_rows)

    turned = [rows, d_ahead, d_far, d_back]
    ordered = []
    for j in range(4):
        pick = turned[j]
        for s in range(1, 4):
            pick = jnp.where(shift == s, turned[(j + s) % 4], pick)
        ordered.append(pick)

    def halves(p, q):
        return jnp.concatenate([p[:64], q[:64], p[64:], q[64:]], axis=0)

    d_swap = HA(halves(ordered[2], ordered[3]))
    core_rows = C(slot_rows)
    b2, a2, d_swap, core_rows = together(b2, a2, d_swap, core_rows)

    d0 = jnp.concatenate([halves(ordered[0], ordered[1]), d_swap], axis=0)
    up1, dn1 = Z(1)(jnp.concatenate([d0, b2], axis=0)), Z(-1)(jnp.concatenate([d0, a2], axis=0))
    first = with_counts([unit, b1, a1, b2, a2])
    f_back, f_ahead = Y(1)(first), Y(-1)(first)
    up1, dn1 = together(up1, dn1)
    f_back, f_ahead, neighbour_rows = together(f_back, f_ahead, neighbour_rows)

    up2, dn2 = Z(1)(up1[:576]), Z(-1)(jnp.concatenate([dn1[:512], dn1[576:]], axis=0))
    second = with_counts([up1[512:], dn1[512:]])
    g_back = Y(1)(jnp.concatenate([second[:256], f_back[:384], second[256:]], axis=0))
    g_ahead = Y(-1)(jnp.concatenate([second[:256], f_ahead[384:640], second[256:], f_ahead[640:]], axis=0))
    far_rows = C(neighbour_rows)
    up2, dn2 = together(up2, dn2)
    g_back, g_ahead, far_rows = together(g_back, g_ahead, far_rows)

    last = jnp.concatenate([up2[512:], dn2[512:]], axis=0)
    up3, dn3 = Z(1)(up2[:512]), Z(-1)(dn2[:512])
    k_back = Y(1)(jnp.concatenate([last[:128], g_back[:128], last[128:]], axis=0))
    k_ahead = Y(-1)(jnp.concatenate([last[:128], g_ahead[128:256], last[128:], g_ahead[512:528]], axis=0))
    k_far = Y(2)(last)
    near = (first, second, last, f_back, f_ahead, g_back, g_ahead)
    partial, x_far = gate_up_near(*near, slot_rows, core_rows, neighbour_rows, far_rows)
    k_back, k_ahead, k_far, partial, x_far = together(k_back, k_ahead, k_far, partial, x_far)
    up3, dn3 = together(up3, dn3)

    de0, de1 = Z(1)(up3[:256]), Z(-1)(dn3[256:])
    h_own, h_other, limit = gate_up_far(where, partial, x_far, k_back, k_ahead, k_far, *near)
    h_near, h_ha, h_far = XL(h_other), HA(h_own), HIDDEN_FAR(h_other)
    h_near, h_ha, h_far, de0, de1 = together(h_near, h_ha, h_far, de0, de1)
    core = C(jnp.concatenate([h_own, h_near, h_ha, h_far], axis=1))
    pieces = [d0, dn1, dn2, dn3, de0, up3, up2, up1, de1]
    total = down(where, (h_own, h_near, h_ha, h_far, core), pieces)
    other = C(total[128:])
    return mix(where, total[:128], other, info, slot_route, limit)


def solution(mesh):
    finer = Mesh(mesh.devices.reshape(NY, 2, NZ, 2, mesh.shape["ha"]), ("y", "xl", "z", "c", "ha"))
    placed = (P(WA, None),) * 4 + (P(WA, "ha"),) * 3
    return jax.shard_map(per_device, mesh=finer, in_specs=placed, out_specs=P(WA, "ha"), check_vma=False)
```

```python
import jax
import jax.numpy as jnp
from jax import lax
from jax.experimental import pallas as pl
from jax.experimental.pallas import tpu as pltpu
from jax.sharding import Mesh
from jax.sharding import PartitionSpec as P

CAP = 128
WA = ("y", "xl", "z", "c")
NY, NZ = 4, 8
F32, BF16, I32 = jnp.float32, jnp.bfloat16, jnp.int32
VMEM = pltpu.VMEM


def whole(memory_space=VMEM):
    return pl.BlockSpec(memory_space=memory_space)


def ring(axis, n, k):
    return lambda a: lax.ppermute(a, axis, [(i, (i + k) % n) for i in range(n)])


def Z(k):
    return ring("z", NZ, k)


def Y(k):
    return ring("y", NY, k)


def C(a):
    return lax.ppermute(a, "c", [(0, 1), (1, 0)])


def XL(a):
    return lax.ppermute(a, "xl", [(0, 1), (1, 0)])


def HA(a):
    return lax.ppermute(a, "ha", [(0, 1), (1, 0)])


def across_x(a):
    def at(x, c):
        return (x % 2) * 4 + c * 2 + x // 2

    pairs = [(at(x, c), at((x + 1 - 2 * c) % 4, c)) for x in range(4) for c in range(2)]
    return lax.ppermute(a, ("xl", "c", "ha"), pairs)


def prep_body(*refs):
    where, far, (info, packed), near, arrive = refs[0], refs[1:7], refs[7:9], refs[9:15], refs[15]
    copies = [pltpu.make_async_copy(f, n, arrive.at[i]) for i, (f, n) in enumerate(zip(far, near))]
    for copy in copies:
        copy.start()
    for copy in copies:
        copy.wait()
    ids, keep, rw, gate, up, down_rows = near
    hit = (ids[...] == 0) & (keep[...] == 1)
    chosen = jnp.max(jnp.where(hit, 1.0, 0.0), axis=0, keepdims=True)
    route = jnp.sum(jnp.where(hit, rw[...], 0.0), axis=0, keepdims=True)
    n = chosen.shape[1]
    row = lax.broadcasted_iota(I32, (n, n), 0)
    col = lax.broadcasted_iota(I32, (n, n), 1)
    before = jnp.where(row < col, 1.0, 0.0).astype(BF16)
    ones = jnp.broadcast_to(chosen, (16, n)).astype(BF16)
    position = jnp.dot(ones, before, preferred_element_type=F32)[:1]
    info[0:1, :] = position
    info[1:2, :] = chosen
    info[2:3, :] = route
    info[3:8, :] = jnp.zeros((5, n), F32)
    total = jnp.sum(chosen, axis=1, keepdims=True)
    for q in range(4):
        at = slice(q * 192, q * 192 + 192)
        to = where[2] * 2 + where[3]
        to = q + to - 2 * (q & to)
        packed[to, 0:32, :] = jnp.concatenate([gate[:, at], up[:, at]], axis=1)
        packed[to, 32:40, :] = jnp.broadcast_to(total, (8, 384)).astype(BF16)
        packed[to, 40:72, :] = down_rows[:, :384]
        packed[to, 72:104, :] = down_rows[:, 384:]


def prep(where, ids, keep, rw, gate, up, down_rows):
    n = ids.shape[1]
    return pl.pallas_call(
        prep_body,
        out_shape=(jax.ShapeDtypeStruct((8, n), F32), jax.ShapeDtypeStruct((4, 104, 384), BF16)),
        in_specs=[whole(pltpu.SMEM)] + [whole(pltpu.HBM)] * 6,
        out_specs=(whole(), whole()),
        scratch_shapes=[VMEM(a.shape, a.dtype) for a in (ids, keep, rw, gate, up, down_rows)]
        + [pltpu.SemaphoreType.DMA((6,))],
        compiler_params=pltpu.CompilerParams(vmem_limit_bytes=12 << 20),
        cost_estimate=pl.CostEstimate(flops=2 * 16 * n * n, bytes_accessed=4 * 32 * n, transcendentals=0),
        name="prep",
    )(where, ids, keep, rw, gate, up, down_rows)


def table(info):
    slot = lax.broadcasted_iota(I32, (CAP, info.shape[1]), 0).astype(F32)
    return (info[0:1, :] == slot) & (info[1:2, :] > 0.5)


def gather_body(where, tokens, info, out, slot_route, near, arrive):
    n, width = near.shape[1:]
    copies = [
        pltpu.make_async_copy(tokens.at[:, i * width : (i + 1) * width], near.at[i], arrive.at[i]) for i in range(NY)
    ]
    for copy in copies:
        copy.start()
    picked = table(info)
    got = jnp.sum(jnp.where(picked, info[2:3, :], 0.0), axis=1, keepdims=True)
    slot_route[...] = jnp.broadcast_to(got, slot_route.shape)
    one_hot = picked.astype(BF16)
    for block in range(NY):
        copies[block].wait()
        rows = jnp.dot(one_hot, near[block], preferred_element_type=F32).astype(BF16)
        ky = lax.rem(block - where[0] + NY, NY)
        yi = jnp.where(ky == 0, 0, jnp.where(ky == 3, 1, jnp.where(ky == 1, 2, 3)))
        for z in range(NZ):
            kz = lax.rem(z - where[1] + NZ, NZ)
            zi = jnp.where(kz == 0, 0, jnp.where(kz <= 3, 2 * kz, jnp.where(kz == 4, 7, 15 - 2 * kz)))
            piece = jnp.concatenate([rows[:, z * 64 : z * 64 + 64], rows[:, 512 + z * 64 : 576 + z * 64]], axis=1)
            out[:, pl.ds(pl.multiple_of((yi * NZ + zi) * 128, 128), 128)] = piece


def gather_rows(where, tokens, info):
    n, d = tokens.shape
    return pl.pallas_call(
        gather_body,
        out_shape=(jax.ShapeDtypeStruct((CAP, d), BF16), jax.ShapeDtypeStruct((CAP, 128), F32)),
        in_specs=[whole(pltpu.SMEM), whole(pltpu.HBM), whole()],
        out_specs=(whole(), whole()),
        scratch_shapes=[VMEM((NY, n, d // NY), tokens.dtype), pltpu.SemaphoreType.DMA((NY,))],
        compiler_params=pltpu.CompilerParams(vmem_limit_bytes=16 << 20),
        cost_estimate=pl.CostEstimate(flops=2 * CAP * n * d, bytes_accessed=2 * n * d, transcendentals=0),
        name="gather_rows",
    )(where, tokens, info)


def near_body(first, second, last, f_back, f_ahead, g_back, g_ahead, xo, xc, xn, xnc, total, x_far, x_all):
    for i, ref in enumerate((xo, xc, xn, xnc)):
        at = slice(i * 128, i * 128 + 128)
        x_all[at, :] = ref[:, :3712]
        x_far[at, 0:128] = ref[:, 1920:2048]
        x_far[at, 128:256] = ref[:, 2944:3072]
        x_far[at, 256:640] = ref[:, 3712:]
    acc = jnp.zeros((512, 384), F32)
    for start, ref, row, size in (
        (0, first, 0, 640),
        (640, second, 0, 256),
        (896, last, 0, 128),
        (1024, f_back, 0, 640),
        (1664, g_back, 0, 256),
        (2048, f_ahead, 0, 640),
        (2688, g_ahead, 0, 256),
        (3072, g_back, 256, 384),
        (3456, g_ahead, 256, 256),
    ):
        acc += jnp.dot(x_all[:, start : start + size], ref[row : row + size, :], preferred_element_type=F32)
    total[...] = acc


def gate_up_near(*arrays):
    return pl.pallas_call(
        near_body,
        out_shape=(jax.ShapeDtypeStruct((512, 384), F32), jax.ShapeDtypeStruct((512, 640), BF16)),
        in_specs=[whole()] * len(arrays),
        out_specs=(whole(), whole()),
        scratch_shapes=[VMEM((512, 3712), BF16)],
        compiler_params=pltpu.CompilerParams(vmem_limit_bytes=16 << 20),
        cost_estimate=pl.CostEstimate(flops=2 * 512 * 3456 * 384, bytes_accessed=8 << 20, transcendentals=0),
        name="gate_up_near",
    )(*arrays)


def far_body(where, total, x_far, k_back, k_ahead, k_far, *refs):
    (first, second, last, f_back, f_ahead, g_back, g_ahead), (own, other, limit) = refs[:7], refs[7:]
    acc = total[...]
    for start, ref, row in ((0, k_back, 0), (128, k_ahead, 0), (256, k_back, 128), (384, k_ahead, 128), (512, k_far, 0)):
        acc += jnp.dot(x_far[:, start : start + 128], ref[row : row + 128, :], preferred_element_type=F32)
    gate, up = acc[:, :192], acc[:, 192:]
    hidden = (gate * jax.nn.sigmoid(gate) * up).astype(BF16)
    own[...] = hidden[:256]
    other[...] = hidden[256:]

    lane = lax.broadcasted_iota(I32, (8, 128), 1)
    quad = lax.shift_right_logical(lane, 1) * 16 + (lane & 1)
    earlier = jnp.zeros((8, 128), F32)
    groups = (
        (0, first[640:680, 0:128], second[256:272, 0:128], last[128:136, 0:128]),
        (3, f_back[640:680, 0:128], g_back[640:656, 0:128], k_back[256:264, 0:128]),
        (1, f_ahead[640:680, 0:128], g_ahead[512:528, 0:128], k_ahead[256:264, 0:128]),
        (2, g_ahead[528:568, 0:128], k_ahead[264:280, 0:128], k_far[128:136, 0:128]),
    )
    for ky, *parts in groups:
        tiles = jnp.concatenate([part.astype(F32) for part in parts], axis=0)
        for zi, kz in enumerate((0, 7, 1, 6, 2, 5, 3, 4)):
            block = ((where[0] + ky) & 3) * 32 + ((where[1] + kz) & 7) * 2 + quad
            counted = (block < where[4]) & (lane < 4)
            earlier += jnp.where(counted, tiles[zi * 8 : zi * 8 + 8], 0.0)
    before = jnp.sum(earlier[0:1], axis=1, keepdims=True)
    limit[...] = jnp.broadcast_to(where[5].astype(F32) - before, limit.shape)


def gate_up_far(*arrays):
    half = jax.ShapeDtypeStruct((256, 192), BF16)
    return pl.pallas_call(
        far_body,
        out_shape=(half, half, jax.ShapeDtypeStruct((8, 128), F32)),
        in_specs=[whole(pltpu.SMEM)] + [whole()] * (len(arrays) - 1),
        out_specs=(whole(), whole(), whole()),
        compiler_params=pltpu.CompilerParams(vmem_limit_bytes=16 << 20),
        cost_estimate=pl.CostEstimate(flops=2 * 512 * 640 * 384, bytes_accessed=3 << 20, transcendentals=512 * 192),
        name="gate_up_far",
    )(*arrays)


def down_body(where, own, near, ha, far, core, *refs):
    pieces, (out, hidden) = refs[:-2], refs[-2:]

    for xl in range(2):
        for c in range(2):

            @pl.when((where[2] == xl) & (where[3] == c))
            def _():
                for k, ref in enumerate((own, near, ha, far)):
                    pair = xl if k % 2 == 0 else 1 - xl
                    base = (k // 2) * 768 + pair * 384
                    hidden[:, base + c * 192 : base + c * 192 + 192] = ref[...]
                    got = core[:, k * 192 : k * 192 + 192]
                    hidden[:, base + (1 - c) * 192 : base + (1 - c) * 192 + 192] = jnp.concatenate(
                        [got[128:], got[:128]], axis=0
                    )

    def dot(k, w):
        return lax.dot_general(
            hidden[:, k * 384 : k * 384 + 384], w, (((1,), (1,)), ((), ())), preferred_element_type=F32
        )

    blocks = []
    for r in range(NZ):
        front, rear = (pieces[4], pieces[8]) if r == 4 else (pieces[r], pieces[r])
        base = 0 if r == 4 else 256
        total = dot(0, front[0:128]) + dot(1, front[128:256])
        blocks.append(total + dot(2, rear[base : base + 128]) + dot(3, rear[base + 128 : base + 256]))
    for y in range(2):
        part = jnp.concatenate([b[:, y * 64 : y * 64 + 64] for b in blocks], axis=1)
        out[:, y * 512 : y * 512 + 512] = pltpu.roll(part, where[1] * 64, 1)


def down(where, hidden, pieces):
    return pl.pallas_call(
        down_body,
        out_shape=jax.ShapeDtypeStruct((256, 1024), F32),
        in_specs=[whole(pltpu.SMEM)] + [whole()] * (len(hidden) + len(pieces)),
        out_specs=whole(),
        scratch_shapes=[VMEM((256, 1536), BF16)],
        compiler_params=pltpu.CompilerParams(vmem_limit_bytes=12 << 20),
        cost_estimate=pl.CostEstimate(flops=2 * 256 * 1536 * 1024, bytes_accessed=5 << 20, transcendentals=0),
        name="down",
    )(where, *hidden, *pieces)


def mix_body(where, mine, theirs, info, slot_route, limit, out, slots):
    @pl.when(pl.program_id(0) == 0)
    def _():
        slot = lax.broadcasted_iota(I32, (CAP, 1), 0).astype(F32)
        scale = jnp.where(slot < limit[0:1, 0:1], slot_route[:, 0:1], 0.0)
        for ref, column in ((mine, where[3]), (theirs, 1 - where[3])):
            scaled = (ref[...] * scale).astype(BF16)
            for y in range(2):
                at = pl.multiple_of(y * 1024 + column * 512, 512)
                slots[:, pl.ds(at, 512)] = scaled[:, y * 512 : y * 512 + 512]

    picked = table(info).astype(BF16)
    mixed = lax.dot_general(picked, slots[...], (((0,), (0,)), ((), ())), preferred_element_type=F32)
    out[...] = mixed.astype(BF16)


def mix(where, mine, theirs, info, slot_route, limit):
    n, step = info.shape[1], 256
    return pl.pallas_call(
        mix_body,
        out_shape=jax.ShapeDtypeStruct((n, 2048), BF16),
        grid_spec=pltpu.PrefetchScalarGridSpec(
            num_scalar_prefetch=1,
            grid=(n // step,),
            in_specs=[
                pl.BlockSpec((CAP, 1024), lambda i, w: (0, 0)),
                pl.BlockSpec((CAP, 1024), lambda i, w: (0, 0)),
                pl.BlockSpec((8, step), lambda i, w: (0, i)),
                pl.BlockSpec((CAP, 128), lambda i, w: (0, 0)),
                pl.BlockSpec((8, 128), lambda i, w: (0, 0)),
            ],
            out_specs=pl.BlockSpec((step, 2048), lambda i, w: (i, 0)),
            scratch_shapes=[VMEM((CAP, 2048), BF16)],
        ),
        compiler_params=pltpu.CompilerParams(vmem_limit_bytes=16 << 20),
        cost_estimate=pl.CostEstimate(flops=2 * n * CAP * 2048, bytes_accessed=6 << 20, transcendentals=0),
        name="mix",
    )(where, mine, theirs, info, slot_route, limit)


def with_counts(units):
    return jnp.concatenate([u[:128] for u in units] + [u[128:] for u in units], axis=0)


def together(*arrays):
    return lax.optimization_barrier(arrays)


def HIDDEN_FAR(a):
    pairs = [(k, 3 - k) for k in range(4)]
    return lax.ppermute(a, ("xl", "ha"), pairs)


def per_device(tokens, expert_ids, keep_mask, route_weight, gate_weight, up_weight, down_weight):
    y, xl, z, c, ha = (lax.axis_index(a) for a in ("y", "xl", "z", "c", "ha"))
    me = y * 32 + xl * 16 + z * 2 + c
    shift = lax.rem(2 * ha - y + NY, NY)
    where = jnp.stack([y, z, xl, c, me, lax.axis_size(WA) * CAP // 2])
    sources = (expert_ids.T, keep_mask.T, route_weight.T, gate_weight, up_weight, down_weight)
    info, packed = prep(where, *(pltpu.with_memory_space_constraint(a, pltpu.HBM) for a in sources))
    both = [(k, 3 - k) for k in range(4)]
    tiles = [packed[0], C(packed[1]), XL(packed[2]), lax.ppermute(packed[3], ("xl", "c"), both)]
    tiles = [jnp.where(c == 0, tiles[k], tiles[k ^ 1]) for k in range(4)]
    arrived = jnp.stack([jnp.where(xl == 0, tiles[k], tiles[k ^ 2]) for k in range(4)])
    slot_rows, slot_route = gather_rows(where, pltpu.with_memory_space_constraint(tokens, pltpu.HBM), info)

    lane = lax.broadcasted_iota(I32, (8, 384), 1)
    tile = jnp.zeros((8, 384), BF16)
    for j in range(4):
        tile = jnp.where(lane == j, arrived[j, 32:40], tile)
    unit = jnp.concatenate([arrived[:, :32].reshape(128, 384), tile], axis=0)
    picked = lax.dynamic_slice_in_dim(arrived, 2 * c, 2, axis=0)[:, 40:]
    rows = jnp.concatenate([picked[0, :32], picked[1, :32], picked[0, 32:], picked[1, 32:]], axis=0)

    b1, a1 = Z(1)(unit), Z(-1)(unit)
    d_back, d_ahead, d_far = Y(1)(rows), Y(-1)(rows), Y(2)(rows)
    b1, a1, d_back, d_ahead, d_far = together(b1, a1, d_back, d_ahead, d_far)
    b2, a2 = Z(1)(b1), Z(-1)(a1)

    turned = [rows, d_ahead, d_far, d_back]
    ordered = []
    for j in range(4):
        pick = turned[j]
        for s in range(1, 4):
            pick = jnp.where(shift == s, turned[(j + s) % 4], pick)
        ordered.append(pick)

    def halves(p, q):
        return jnp.concatenate([p[:64], q[:64], p[64:], q[64:]], axis=0)

    d_swap = HA(halves(ordered[2], ordered[3]))
    core_rows = C(slot_rows)
    b2, a2, d_swap, core_rows, slot_rows = together(b2, a2, d_swap, core_rows, slot_rows)
    neighbour_rows = across_x(slot_rows)

    d0 = jnp.concatenate([halves(ordered[0], ordered[1]), d_swap], axis=0)
    up1, dn1 = Z(1)(jnp.concatenate([d0, b2], axis=0)), Z(-1)(jnp.concatenate([d0, a2], axis=0))
    first = with_counts([unit, b1, a1, b2, a2])
    f_back, f_ahead = Y(1)(first), Y(-1)(first)
    up1, dn1 = together(up1, dn1)
    f_back, f_ahead, neighbour_rows = together(f_back, f_ahead, neighbour_rows)

    up2, dn2 = Z(1)(up1[:576]), Z(-1)(jnp.concatenate([dn1[:512], dn1[576:]], axis=0))
    second = with_counts([up1[512:], dn1[512:]])
    g_back = Y(1)(jnp.concatenate([second[:256], f_back[:384], second[256:]], axis=0))
    g_ahead = Y(-1)(jnp.concatenate([second[:256], f_ahead[384:640], second[256:], f_ahead[640:]], axis=0))
    far_rows = C(neighbour_rows)
    up2, dn2 = together(up2, dn2)
    g_back, g_ahead, far_rows = together(g_back, g_ahead, far_rows)

    last = jnp.concatenate([up2[512:], dn2[512:]], axis=0)
    up3, dn3 = Z(1)(up2[:512]), Z(-1)(dn2[:512])
    k_back = Y(1)(jnp.concatenate([last[:128], g_back[:128], last[128:]], axis=0))
    k_ahead = Y(-1)(jnp.concatenate([last[:128], g_ahead[128:256], last[128:], g_ahead[512:528]], axis=0))
    k_far = Y(2)(last)
    near = (first, second, last, f_back, f_ahead, g_back, g_ahead)
    partial, x_far = gate_up_near(*near, slot_rows, core_rows, neighbour_rows, far_rows)
    k_back, k_ahead, k_far, partial, x_far = together(k_back, k_ahead, k_far, partial, x_far)
    up3, dn3 = together(up3, dn3)

    de0, de1 = Z(1)(up3[:256]), Z(-1)(dn3[256:])
    h_own, h_other, limit = gate_up_far(where, partial, x_far, k_back, k_ahead, k_far, *near)
    h_near, h_ha, h_far = XL(h_other), HA(h_own), HIDDEN_FAR(h_other)
    h_near, h_ha, h_far, de0, de1 = together(h_near, h_ha, h_far, de0, de1)
    core = C(jnp.concatenate([h_own, h_near, h_ha, h_far], axis=1))
    pieces = [d0, dn1, dn2, dn3, de0, up3, up2, up1, de1]
    total = down(where, (h_own, h_near, h_ha, h_far, core), pieces)
    other = C(total[128:])
    return mix(where, total[:128], other, info, slot_route, limit)


def solution(mesh):
    finer = Mesh(mesh.devices.reshape(NY, 2, NZ, 2, mesh.shape["ha"]), ("y", "xl", "z", "c", "ha"))
    placed = (P(WA, None),) * 4 + (P(WA, "ha"),) * 3
    return jax.shard_map(per_device, mesh=finer, in_specs=placed, out_specs=P(WA, "ha"), check_vma=False)
```

```python
import functools

import jax
import jax.numpy as jnp
from jax import lax
from jax.experimental import pallas as pl
from jax.experimental.pallas import tpu as pltpu
from jax.sharding import Mesh
from jax.sharding import PartitionSpec as P

CAP = 128
WA = ("y", "xl", "z", "c")
NY, NZ = 4, 8
F32, BF16, I32 = jnp.float32, jnp.bfloat16, jnp.int32
VMEM = pltpu.VMEM


def whole(memory_space=VMEM):
    return pl.BlockSpec(memory_space=memory_space)


def ring(axis, n, k):
    return lambda a: lax.ppermute(a, axis, [(i, (i + k) % n) for i in range(n)])


def Z(k):
    return ring("z", NZ, k)


def Y(k):
    return ring("y", NY, k)


def C(a):
    return lax.ppermute(a, "c", [(0, 1), (1, 0)])


def XL(a):
    return lax.ppermute(a, "xl", [(0, 1), (1, 0)])


def HA(a):
    return lax.ppermute(a, "ha", [(0, 1), (1, 0)])


def across_x(a):
    def at(x, c):
        return (x % 2) * 4 + c * 2 + x // 2

    pairs = [(at(x, c), at((x + 1 - 2 * c) % 4, c)) for x in range(4) for c in range(2)]
    return lax.ppermute(a, ("xl", "c", "ha"), pairs)


def prep_body(*refs):
    where, far, (info, packed), near, arrive = refs[0], refs[1:7], refs[7:9], refs[9:15], refs[15]
    copies = [pltpu.make_async_copy(f, n, arrive.at[i]) for i, (f, n) in enumerate(zip(far, near))]
    for copy in copies:
        copy.start()
    for copy in copies:
        copy.wait()
    ids, keep, rw, gate, up, down_rows = near
    hit = (ids[...] == 0) & (keep[...] == 1)
    chosen = jnp.max(jnp.where(hit, 1.0, 0.0), axis=0, keepdims=True)
    route = jnp.sum(jnp.where(hit, rw[...], 0.0), axis=0, keepdims=True)
    n = chosen.shape[1]
    row = lax.broadcasted_iota(I32, (n, n), 0)
    col = lax.broadcasted_iota(I32, (n, n), 1)
    before = jnp.where(row < col, 1.0, 0.0).astype(BF16)
    ones = jnp.broadcast_to(chosen, (16, n)).astype(BF16)
    position = jnp.dot(ones, before, preferred_element_type=F32)[:1]
    info[0:1, :] = position
    info[1:2, :] = chosen
    info[2:3, :] = route
    info[3:8, :] = jnp.zeros((5, n), F32)
    total = jnp.sum(chosen, axis=1, keepdims=True)
    for q in range(4):
        at = slice(q * 192, q * 192 + 192)
        to = where[2] * 2 + where[3]
        to = q + to - 2 * (q & to)
        packed[to, 0:32, :] = jnp.concatenate([gate[:, at], up[:, at]], axis=1)
        packed[to, 32:40, :] = jnp.broadcast_to(total, (8, 384)).astype(BF16)
        packed[to, 40:72, :] = down_rows[:, :384]
        packed[to, 72:104, :] = down_rows[:, 384:]


def prep(where, ids, keep, rw, gate, up, down_rows):
    n = ids.shape[1]
    return pl.pallas_call(
        prep_body,
        out_shape=(jax.ShapeDtypeStruct((8, n), F32), jax.ShapeDtypeStruct((4, 104, 384), BF16)),
        in_specs=[whole(pltpu.SMEM)] + [whole(pltpu.HBM)] * 6,
        out_specs=(whole(), whole()),
        scratch_shapes=[VMEM(a.shape, a.dtype) for a in (ids, keep, rw, gate, up, down_rows)]
        + [pltpu.SemaphoreType.DMA((6,))],
        compiler_params=pltpu.CompilerParams(vmem_limit_bytes=12 << 20),
        cost_estimate=pl.CostEstimate(flops=2 * 16 * n * n, bytes_accessed=4 * 32 * n, transcendentals=0),
        name="prep",
    )(where, ids, keep, rw, gate, up, down_rows)


def table(info):
    slot = lax.broadcasted_iota(I32, (CAP, info.shape[1]), 0).astype(F32)
    return (info[0:1, :] == slot) & (info[1:2, :] > 0.5)


def gather_body(where, tokens, info, out, slot_route, near, arrive):
    n, width = near.shape[1:]
    copies = [
        pltpu.make_async_copy(tokens.at[:, i * width : (i + 1) * width], near.at[i], arrive.at[i]) for i in range(NY)
    ]
    for copy in copies:
        copy.start()
    picked = table(info)
    got = jnp.sum(jnp.where(picked, info[2:3, :], 0.0), axis=1, keepdims=True)
    slot_route[...] = jnp.broadcast_to(got, slot_route.shape)
    one_hot = picked.astype(BF16)
    for block in range(NY):
        copies[block].wait()
        rows = jnp.dot(one_hot, near[block], preferred_element_type=F32).astype(BF16)
        ky = lax.rem(block - where[0] + NY, NY)
        yi = jnp.where(ky == 0, 0, jnp.where(ky == 3, 1, jnp.where(ky == 1, 2, 3)))
        for z in range(NZ):
            kz = lax.rem(z - where[1] + NZ, NZ)
            zi = jnp.where(kz == 0, 0, jnp.where(kz <= 3, 2 * kz, jnp.where(kz == 4, 7, 15 - 2 * kz)))
            piece = jnp.concatenate([rows[:, z * 64 : z * 64 + 64], rows[:, 512 + z * 64 : 576 + z * 64]], axis=1)
            out[:, pl.ds(pl.multiple_of((yi * NZ + zi) * 128, 128), 128)] = piece


def gather_rows(where, tokens, info):
    n, d = tokens.shape
    return pl.pallas_call(
        gather_body,
        out_shape=(jax.ShapeDtypeStruct((CAP, d), BF16), jax.ShapeDtypeStruct((CAP, 128), F32)),
        in_specs=[whole(pltpu.SMEM), whole(pltpu.HBM), whole()],
        out_specs=(whole(), whole()),
        scratch_shapes=[VMEM((NY, n, d // NY), tokens.dtype), pltpu.SemaphoreType.DMA((NY,))],
        compiler_params=pltpu.CompilerParams(vmem_limit_bytes=16 << 20),
        cost_estimate=pl.CostEstimate(flops=2 * CAP * n * d, bytes_accessed=2 * n * d, transcendentals=0),
        name="gather_rows",
    )(where, tokens, info)


def near_body(first, second, last, f_back, f_ahead, g_back, g_ahead, xo, xc, xn, xnc, total, x_far, x_all):
    for i, ref in enumerate((xo, xc, xn, xnc)):
        at = slice(i * 128, i * 128 + 128)
        x_all[at, :] = ref[:, :3712]
        x_far[at, 0:128] = ref[:, 1920:2048]
        x_far[at, 128:256] = ref[:, 2944:3072]
        x_far[at, 256:640] = ref[:, 3712:]
    acc = jnp.zeros((512, 384), F32)
    for start, ref, row, size in (
        (0, first, 0, 640),
        (640, second, 0, 256),
        (896, last, 0, 128),
        (1024, f_back, 0, 640),
        (1664, g_back, 0, 256),
        (2048, f_ahead, 0, 640),
        (2688, g_ahead, 0, 256),
        (3072, g_back, 256, 384),
        (3456, g_ahead, 256, 256),
    ):
        acc += jnp.dot(x_all[:, start : start + size], ref[row : row + size, :], preferred_element_type=F32)
    total[...] = acc


def gate_up_near(*arrays):
    return pl.pallas_call(
        near_body,
        out_shape=(jax.ShapeDtypeStruct((512, 384), F32), jax.ShapeDtypeStruct((512, 640), BF16)),
        in_specs=[whole()] * len(arrays),
        out_specs=(whole(), whole()),
        scratch_shapes=[VMEM((512, 3712), BF16)],
        compiler_params=pltpu.CompilerParams(vmem_limit_bytes=16 << 20),
        cost_estimate=pl.CostEstimate(flops=2 * 512 * 3456 * 384, bytes_accessed=8 << 20, transcendentals=0),
        name="gate_up_near",
    )(*arrays)


def far_body(where, total, x_far, k_back, k_ahead, k_far, *refs):
    (first, second, last, f_back, f_ahead, g_back, g_ahead), (own, other, limit) = refs[:7], refs[7:]
    acc = total[...]
    for start, ref, row in ((0, k_back, 0), (128, k_ahead, 0), (256, k_back, 128), (384, k_ahead, 128), (512, k_far, 0)):
        acc += jnp.dot(x_far[:, start : start + 128], ref[row : row + 128, :], preferred_element_type=F32)
    gate, up = acc[:, :192], acc[:, 192:]
    hidden = (gate * jax.nn.sigmoid(gate) * up).astype(BF16)
    own[...] = hidden[:256]
    other[...] = hidden[256:]

    lane = lax.broadcasted_iota(I32, (8, 128), 1)
    quad = lax.shift_right_logical(lane, 1) * 16 + (lane & 1)
    earlier = jnp.zeros((8, 128), F32)
    groups = (
        (0, first[640:680, 0:128], second[256:272, 0:128], last[128:136, 0:128]),
        (3, f_back[640:680, 0:128], g_back[640:656, 0:128], k_back[256:264, 0:128]),
        (1, f_ahead[640:680, 0:128], g_ahead[512:528, 0:128], k_ahead[256:264, 0:128]),
        (2, g_ahead[528:568, 0:128], k_ahead[264:280, 0:128], k_far[128:136, 0:128]),
    )
    for ky, *parts in groups:
        tiles = jnp.concatenate([part.astype(F32) for part in parts], axis=0)
        for zi, kz in enumerate((0, 7, 1, 6, 2, 5, 3, 4)):
            block = ((where[0] + ky) & 3) * 32 + ((where[1] + kz) & 7) * 2 + quad
            counted = (block < where[4]) & (lane < 4)
            earlier += jnp.where(counted, tiles[zi * 8 : zi * 8 + 8], 0.0)
    before = jnp.sum(earlier[0:1], axis=1, keepdims=True)
    limit[...] = jnp.broadcast_to(where[5].astype(F32) - before, limit.shape)


def gate_up_far(*arrays):
    half = jax.ShapeDtypeStruct((256, 192), BF16)
    return pl.pallas_call(
        far_body,
        out_shape=(half, half, jax.ShapeDtypeStruct((8, 128), F32)),
        in_specs=[whole(pltpu.SMEM)] + [whole()] * (len(arrays) - 1),
        out_specs=(whole(), whole(), whole()),
        compiler_params=pltpu.CompilerParams(vmem_limit_bytes=16 << 20),
        cost_estimate=pl.CostEstimate(flops=2 * 512 * 640 * 384, bytes_accessed=3 << 20, transcendentals=512 * 192),
        name="gate_up_far",
    )(*arrays)


def down_body(where, own, near, ha, far, core, *refs):
    pieces, (out, hidden) = refs[:-2], refs[-2:]

    for xl in range(2):
        for c in range(2):

            @pl.when((where[2] == xl) & (where[3] == c))
            def _():
                for k, ref in enumerate((own, near, ha, far)):
                    pair = xl if k % 2 == 0 else 1 - xl
                    base = (k // 2) * 768 + pair * 384
                    hidden[:, base + c * 192 : base + c * 192 + 192] = ref[...]
                    got = core[:, k * 192 : k * 192 + 192]
                    hidden[:, base + (1 - c) * 192 : base + (1 - c) * 192 + 192] = jnp.concatenate(
                        [got[128:], got[:128]], axis=0
                    )

    def dot(k, w):
        return lax.dot_general(
            hidden[:, k * 384 : k * 384 + 384], w, (((1,), (1,)), ((), ())), preferred_element_type=F32
        )

    blocks = []
    for r in range(NZ):
        front, rear = (pieces[4], pieces[8]) if r == 4 else (pieces[r], pieces[r])
        base = 0 if r == 4 else 256
        total = dot(0, front[0:128]) + dot(1, front[128:256])
        blocks.append(total + dot(2, rear[base : base + 128]) + dot(3, rear[base + 128 : base + 256]))
    for y in range(2):
        part = jnp.concatenate([b[:, y * 64 : y * 64 + 64] for b in blocks], axis=1)
        out[:, y * 512 : y * 512 + 512] = pltpu.roll(part, where[1] * 64, 1)


def down(where, hidden, pieces):
    return pl.pallas_call(
        down_body,
        out_shape=jax.ShapeDtypeStruct((256, 1024), F32),
        in_specs=[whole(pltpu.SMEM)] + [whole()] * (len(hidden) + len(pieces)),
        out_specs=whole(),
        scratch_shapes=[VMEM((256, 1536), BF16)],
        compiler_params=pltpu.CompilerParams(vmem_limit_bytes=12 << 20),
        cost_estimate=pl.CostEstimate(flops=2 * 256 * 1536 * 1024, bytes_accessed=5 << 20, transcendentals=0),
        name="down",
    )(where, *hidden, *pieces)


def mix_body(theirs, where, rows, info, slot_route, limit, *refs):
    out, done, sent = refs[-3:]
    slot = lax.broadcasted_iota(I32, (CAP, 1), 0).astype(F32)
    scale = jnp.where(slot < limit[0:1, 0:1], slot_route[:, 0:1], 0.0)
    one_hot = table(info).astype(BF16)
    column = 1 - where[3] if theirs else where[3]
    n = one_hot.shape[1]
    copies = []
    for y in range(2):
        scaled = (rows[0:CAP, y * 512 : y * 512 + 512] * scale).astype(BF16)
        for t in range(0, n, 256):
            mixed = lax.dot_general(
                one_hot[:, t : t + 256], scaled, (((0,), (0,)), ((), ())), preferred_element_type=F32
            )
            done[y, t : t + 256, :] = mixed.astype(BF16)
        at = pl.multiple_of(y * 1024 + column * 512, 512)
        copies.append(pltpu.make_async_copy(done.at[y], out.at[:, pl.ds(at, 512)], sent.at[y]))
        copies[-1].start()
    for copy in copies:
        copy.wait()


def mix(where, rows, info, slot_route, limit, half=None):
    n = info.shape[1]
    extra = () if half is None else (half,)
    return pl.pallas_call(
        functools.partial(mix_body, half is not None),
        out_shape=jax.ShapeDtypeStruct((n, 2048), BF16),
        in_specs=[whole(pltpu.SMEM)] + [whole()] * 4 + [whole(pltpu.HBM)] * len(extra),
        out_specs=whole(pltpu.HBM),
        scratch_shapes=[VMEM((2, n, 512), BF16), pltpu.SemaphoreType.DMA((2,))],
        input_output_aliases={} if half is None else {5: 0},
        compiler_params=pltpu.CompilerParams(vmem_limit_bytes=12 << 20),
        cost_estimate=pl.CostEstimate(flops=2 * n * CAP * 1024, bytes_accessed=3 << 20, transcendentals=0),
        name="mix_own" if half is None else "mix_rest",
    )(where, rows, info, slot_route, limit, *extra)


def with_counts(units):
    return jnp.concatenate([u[:128] for u in units] + [u[128:] for u in units], axis=0)


def together(*arrays):
    return lax.optimization_barrier(arrays)


def HIDDEN_FAR(a):
    pairs = [(k, 3 - k) for k in range(4)]
    return lax.ppermute(a, ("xl", "ha"), pairs)


def per_device(tokens, expert_ids, keep_mask, route_weight, gate_weight, up_weight, down_weight):
    y, xl, z, c, ha = (lax.axis_index(a) for a in ("y", "xl", "z", "c", "ha"))
    me = y * 32 + xl * 16 + z * 2 + c
    shift = lax.rem(2 * ha - y + NY, NY)
    where = jnp.stack([y, z, xl, c, me, lax.axis_size(WA) * CAP // 2])
    sources = (expert_ids.T, keep_mask.T, route_weight.T, gate_weight, up_weight, down_weight)
    info, packed = prep(where, *(pltpu.with_memory_space_constraint(a, pltpu.HBM) for a in sources))
    both = [(k, 3 - k) for k in range(4)]
    tiles = [packed[0], C(packed[1]), XL(packed[2]), lax.ppermute(packed[3], ("xl", "c"), both)]
    tiles = [jnp.where(c == 0, tiles[k], tiles[k ^ 1]) for k in range(4)]
    arrived = jnp.stack([jnp.where(xl == 0, tiles[k], tiles[k ^ 2]) for k in range(4)])
    slot_rows, slot_route = gather_rows(where, pltpu.with_memory_space_constraint(tokens, pltpu.HBM), info)

    lane = lax.broadcasted_iota(I32, (8, 384), 1)
    tile = jnp.zeros((8, 384), BF16)
    for j in range(4):
        tile = jnp.where(lane == j, arrived[j, 32:40], tile)
    unit = jnp.concatenate([arrived[:, :32].reshape(128, 384), tile], axis=0)
    picked = lax.dynamic_slice_in_dim(arrived, 2 * c, 2, axis=0)[:, 40:]
    rows = jnp.concatenate([picked[0, :32], picked[1, :32], picked[0, 32:], picked[1, 32:]], axis=0)

    b1, a1 = Z(1)(unit), Z(-1)(unit)
    d_back, d_ahead, d_far = Y(1)(rows), Y(-1)(rows), Y(2)(rows)
    b1, a1, d_back, d_ahead, d_far = together(b1, a1, d_back, d_ahead, d_far)
    b2, a2 = Z(1)(b1), Z(-1)(a1)

    turned = [rows, d_ahead, d_far, d_back]
    ordered = []
    for j in range(4):
        pick = turned[j]
        for s in range(1, 4):
            pick = jnp.where(shift == s, turned[(j + s) % 4], pick)
        ordered.append(pick)

    def halves(p, q):
        return jnp.concatenate([p[:64], q[:64], p[64:], q[64:]], axis=0)

    d_swap = HA(halves(ordered[2], ordered[3]))
    core_rows = C(slot_rows)
    b2, a2, d_swap, core_rows, slot_rows = together(b2, a2, d_swap, core_rows, slot_rows)
    neighbour_rows = across_x(slot_rows)

    d0 = jnp.concatenate([halves(ordered[0], ordered[1]), d_swap], axis=0)
    up1, dn1 = Z(1)(jnp.concatenate([d0, b2], axis=0)), Z(-1)(jnp.concatenate([d0, a2], axis=0))
    first = with_counts([unit, b1, a1, b2, a2])
    f_back, f_ahead = Y(1)(first), Y(-1)(first)
    up1, dn1 = together(up1, dn1)
    f_back, f_ahead, neighbour_rows = together(f_back, f_ahead, neighbour_rows)

    up2, dn2 = Z(1)(up1[:576]), Z(-1)(jnp.concatenate([dn1[:512], dn1[576:]], axis=0))
    second = with_counts([up1[512:], dn1[512:]])
    g_back = Y(1)(jnp.concatenate([second[:256], f_back[:384], second[256:]], axis=0))
    g_ahead = Y(-1)(jnp.concatenate([second[:256], f_ahead[384:640], second[256:], f_ahead[640:]], axis=0))
    far_rows = C(neighbour_rows)
    up2, dn2 = together(up2, dn2)
    g_back, g_ahead, far_rows = together(g_back, g_ahead, far_rows)

    last = jnp.concatenate([up2[512:], dn2[512:]], axis=0)
    up3, dn3 = Z(1)(up2[:512]), Z(-1)(dn2[:512])
    k_back = Y(1)(jnp.concatenate([last[:128], g_back[:128], last[128:]], axis=0))
    k_ahead = Y(-1)(jnp.concatenate([last[:128], g_ahead[128:256], last[128:], g_ahead[512:528]], axis=0))
    k_far = Y(2)(last)
    near = (first, second, last, f_back, f_ahead, g_back, g_ahead)
    partial, x_far = gate_up_near(*near, slot_rows, core_rows, neighbour_rows, far_rows)
    k_back, k_ahead, k_far, partial, x_far = together(k_back, k_ahead, k_far, partial, x_far)
    up3, dn3 = together(up3, dn3)

    de0, de1 = Z(1)(up3[:256]), Z(-1)(dn3[256:])
    h_own, h_other, limit = gate_up_far(where, partial, x_far, k_back, k_ahead, k_far, *near)
    h_near, h_ha, h_far = XL(h_other), HA(h_own), HIDDEN_FAR(h_other)
    h_near, h_ha, h_far, de0, de1 = together(h_near, h_ha, h_far, de0, de1)
    core = C(jnp.concatenate([h_own, h_near, h_ha, h_far], axis=1))
    pieces = [d0, dn1, dn2, dn3, de0, up3, up2, up1, de1]
    total = down(where, (h_own, h_near, h_ha, h_far, core), pieces)
    other = C(total[128:])
    half = mix(where, total, info, slot_route, limit)
    return mix(where, other, info, slot_route, limit, half)


def solution(mesh):
    finer = Mesh(mesh.devices.reshape(NY, 2, NZ, 2, mesh.shape["ha"]), ("y", "xl", "z", "c", "ha"))
    placed = (P(WA, None),) * 4 + (P(WA, "ha"),) * 3
    return jax.shard_map(per_device, mesh=finer, in_specs=placed, out_specs=P(WA, "ha"), check_vma=False)
```

```python
import functools

import jax
import jax.numpy as jnp
from jax import lax
from jax.experimental import pallas as pl
from jax.experimental.pallas import tpu as pltpu
from jax.sharding import Mesh
from jax.sharding import PartitionSpec as P

CAP = 128
WA = ("y", "xl", "z", "c")
NY, NZ = 4, 8
F32, BF16, I32 = jnp.float32, jnp.bfloat16, jnp.int32
VMEM = pltpu.VMEM


def whole(memory_space=VMEM):
    return pl.BlockSpec(memory_space=memory_space)


def ring(axis, n, k):
    return lambda a: lax.ppermute(a, axis, [(i, (i + k) % n) for i in range(n)])


def Z(k):
    return ring("z", NZ, k)


def Y(k):
    return ring("y", NY, k)


def C(a):
    return lax.ppermute(a, "c", [(0, 1), (1, 0)])


def XL(a):
    return lax.ppermute(a, "xl", [(0, 1), (1, 0)])


def HA(a):
    return lax.ppermute(a, "ha", [(0, 1), (1, 0)])


def across_x(a):
    def at(x, c):
        return (x % 2) * 4 + c * 2 + x // 2

    pairs = [(at(x, c), at((x + 1 - 2 * c) % 4, c)) for x in range(4) for c in range(2)]
    return lax.ppermute(a, ("xl", "c", "ha"), pairs)


def prep_body(*refs):
    where, far, (info, packed), near, arrive = refs[0], refs[1:7], refs[7:9], refs[9:15], refs[15]
    copies = [pltpu.make_async_copy(f, n, arrive.at[i]) for i, (f, n) in enumerate(zip(far, near))]
    for copy in copies:
        copy.start()
    for copy in copies:
        copy.wait()
    ids, keep, rw, gate, up, down_rows = near
    hit = (ids[...] == 0) & (keep[...] == 1)
    chosen = jnp.max(jnp.where(hit, 1.0, 0.0), axis=0, keepdims=True)
    route = jnp.sum(jnp.where(hit, rw[...], 0.0), axis=0, keepdims=True)
    n = chosen.shape[1]
    info[0:1, :] = jnp.zeros((1, n), F32)
    info[1:2, :] = chosen
    info[2:3, :] = route
    info[3:8, :] = jnp.zeros((5, n), F32)
    total = jnp.sum(chosen, axis=1, keepdims=True)
    for q in range(4):
        at = slice(q * 192, q * 192 + 192)
        to = where[2] * 2 + where[3]
        to = q + to - 2 * (q & to)
        packed[to, 0:32, :] = jnp.concatenate([gate[:, at], up[:, at]], axis=1)
        packed[to, 32:40, :] = jnp.broadcast_to(total, (8, 384)).astype(BF16)
        packed[to, 40:72, :] = down_rows[:, :384]
        packed[to, 72:104, :] = down_rows[:, 384:]


def prep(where, ids, keep, rw, gate, up, down_rows):
    n = ids.shape[1]
    return pl.pallas_call(
        prep_body,
        out_shape=(jax.ShapeDtypeStruct((8, n), F32), jax.ShapeDtypeStruct((4, 104, 384), BF16)),
        in_specs=[whole(pltpu.SMEM)] + [whole(pltpu.HBM)] * 6,
        out_specs=(whole(), whole()),
        scratch_shapes=[VMEM(a.shape, a.dtype) for a in (ids, keep, rw, gate, up, down_rows)]
        + [pltpu.SemaphoreType.DMA((6,))],
        compiler_params=pltpu.CompilerParams(vmem_limit_bytes=12 << 20),
        cost_estimate=pl.CostEstimate(flops=2 * 16 * n * n, bytes_accessed=4 * 32 * n, transcendentals=0),
        name="prep",
    )(where, ids, keep, rw, gate, up, down_rows)


def table(info):
    slot = lax.broadcasted_iota(I32, (CAP, info.shape[1]), 0).astype(F32)
    return (info[0:1, :] == slot) & (info[1:2, :] > 0.5)


def gather_body(where, tokens, routed, out, slot_route, info, near, arrive):
    n, width = near.shape[1:]
    copies = [
        pltpu.make_async_copy(tokens.at[:, i * width : (i + 1) * width], near.at[i], arrive.at[i]) for i in range(NY)
    ]
    for copy in copies:
        copy.start()
    chosen = routed[1:2, :]
    row = lax.broadcasted_iota(I32, (n, n), 0)
    col = lax.broadcasted_iota(I32, (n, n), 1)
    before = jnp.where(row < col, 1.0, 0.0).astype(BF16)
    ones = jnp.broadcast_to(chosen, (16, n)).astype(BF16)
    position = jnp.dot(ones, before, preferred_element_type=F32)[:1]
    info[0:1, :] = position
    info[1:8, :] = routed[1:8, :]
    picked = table(info)
    got = jnp.sum(jnp.where(picked, info[2:3, :], 0.0), axis=1, keepdims=True)
    slot_route[...] = jnp.broadcast_to(got, slot_route.shape)
    one_hot = picked.astype(BF16)
    for block in range(NY):
        copies[block].wait()
        rows = jnp.dot(one_hot, near[block], preferred_element_type=F32).astype(BF16)
        ky = lax.rem(block - where[0] + NY, NY)
        yi = jnp.where(ky == 0, 0, jnp.where(ky == 3, 1, jnp.where(ky == 1, 2, 3)))
        for z in range(NZ):
            kz = lax.rem(z - where[1] + NZ, NZ)
            zi = jnp.where(kz == 0, 0, jnp.where(kz <= 3, 2 * kz, jnp.where(kz == 4, 7, 15 - 2 * kz)))
            piece = jnp.concatenate([rows[:, z * 64 : z * 64 + 64], rows[:, 512 + z * 64 : 576 + z * 64]], axis=1)
            out[:, pl.ds(pl.multiple_of((yi * NZ + zi) * 128, 128), 128)] = piece


def gather_rows(where, tokens, info):
    n, d = tokens.shape
    return pl.pallas_call(
        gather_body,
        out_shape=(
            jax.ShapeDtypeStruct((CAP, d), BF16),
            jax.ShapeDtypeStruct((CAP, 128), F32),
            jax.ShapeDtypeStruct(info.shape, F32),
        ),
        in_specs=[whole(pltpu.SMEM), whole(pltpu.HBM), whole()],
        out_specs=(whole(), whole(), whole()),
        scratch_shapes=[VMEM((NY, n, d // NY), tokens.dtype), pltpu.SemaphoreType.DMA((NY,))],
        compiler_params=pltpu.CompilerParams(vmem_limit_bytes=16 << 20),
        cost_estimate=pl.CostEstimate(flops=2 * CAP * n * d, bytes_accessed=2 * n * d, transcendentals=0),
        name="gather_rows",
    )(where, tokens, info)


def near_body(first, second, last, f_back, f_ahead, g_back, g_ahead, xo, xc, xn, xnc, total, x_far, x_all):
    for i, ref in enumerate((xo, xc, xn, xnc)):
        at = slice(i * 128, i * 128 + 128)
        x_all[at, :] = ref[:, :3712]
        x_far[at, 0:128] = ref[:, 1920:2048]
        x_far[at, 128:256] = ref[:, 2944:3072]
        x_far[at, 256:640] = ref[:, 3712:]
    acc = jnp.zeros((512, 384), F32)
    for start, ref, row, size in (
        (0, first, 0, 640),
        (640, second, 0, 256),
        (896, last, 0, 128),
        (1024, f_back, 0, 640),
        (1664, g_back, 0, 256),
        (2048, f_ahead, 0, 640),
        (2688, g_ahead, 0, 256),
        (3072, g_back, 256, 384),
        (3456, g_ahead, 256, 256),
    ):
        acc += jnp.dot(x_all[:, start : start + size], ref[row : row + size, :], preferred_element_type=F32)
    total[...] = acc


def gate_up_near(*arrays):
    return pl.pallas_call(
        near_body,
        out_shape=(jax.ShapeDtypeStruct((512, 384), F32), jax.ShapeDtypeStruct((512, 640), BF16)),
        in_specs=[whole()] * len(arrays),
        out_specs=(whole(), whole()),
        scratch_shapes=[VMEM((512, 3712), BF16)],
        compiler_params=pltpu.CompilerParams(vmem_limit_bytes=16 << 20),
        cost_estimate=pl.CostEstimate(flops=2 * 512 * 3456 * 384, bytes_accessed=8 << 20, transcendentals=0),
        name="gate_up_near",
    )(*arrays)


def far_body(where, total, x_far, k_back, k_ahead, k_far, *refs):
    (first, second, last, f_back, f_ahead, g_back, g_ahead), (own, other, limit) = refs[:7], refs[7:]
    acc = total[...]
    for start, ref, row in ((0, k_back, 0), (128, k_ahead, 0), (256, k_back, 128), (384, k_ahead, 128), (512, k_far, 0)):
        acc += jnp.dot(x_far[:, start : start + 128], ref[row : row + 128, :], preferred_element_type=F32)
    gate, up = acc[:, :192], acc[:, 192:]
    hidden = (gate * jax.nn.sigmoid(gate) * up).astype(BF16)
    own[...] = hidden[:256]
    other[...] = hidden[256:]

    lane = lax.broadcasted_iota(I32, (8, 128), 1)
    quad = lax.shift_right_logical(lane, 1) * 16 + (lane & 1)
    earlier = jnp.zeros((8, 128), F32)
    groups = (
        (0, first[640:680, 0:128], second[256:272, 0:128], last[128:136, 0:128]),
        (3, f_back[640:680, 0:128], g_back[640:656, 0:128], k_back[256:264, 0:128]),
        (1, f_ahead[640:680, 0:128], g_ahead[512:528, 0:128], k_ahead[256:264, 0:128]),
        (2, g_ahead[528:568, 0:128], k_ahead[264:280, 0:128], k_far[128:136, 0:128]),
    )
    for ky, *parts in groups:
        tiles = jnp.concatenate([part.astype(F32) for part in parts], axis=0)
        for zi, kz in enumerate((0, 7, 1, 6, 2, 5, 3, 4)):
            block = ((where[0] + ky) & 3) * 32 + ((where[1] + kz) & 7) * 2 + quad
            counted = (block < where[4]) & (lane < 4)
            earlier += jnp.where(counted, tiles[zi * 8 : zi * 8 + 8], 0.0)
    before = jnp.sum(earlier[0:1], axis=1, keepdims=True)
    limit[...] = jnp.broadcast_to(where[5].astype(F32) - before, limit.shape)


def gate_up_far(*arrays):
    half = jax.ShapeDtypeStruct((256, 192), BF16)
    return pl.pallas_call(
        far_body,
        out_shape=(half, half, jax.ShapeDtypeStruct((8, 128), F32)),
        in_specs=[whole(pltpu.SMEM)] + [whole()] * (len(arrays) - 1),
        out_specs=(whole(), whole(), whole()),
        compiler_params=pltpu.CompilerParams(vmem_limit_bytes=16 << 20),
        cost_estimate=pl.CostEstimate(flops=2 * 512 * 640 * 384, bytes_accessed=3 << 20, transcendentals=512 * 192),
        name="gate_up_far",
    )(*arrays)


def down_body(where, own, near, ha, far, core, *refs):
    pieces, (out, hidden) = refs[:-2], refs[-2:]

    for xl in range(2):
        for c in range(2):

            @pl.when((where[2] == xl) & (where[3] == c))
            def _():
                for k, ref in enumerate((own, near, ha, far)):
                    pair = xl if k % 2 == 0 else 1 - xl
                    base = (k // 2) * 768 + pair * 384
                    hidden[:, base + c * 192 : base + c * 192 + 192] = ref[...]
                    got = core[:, k * 192 : k * 192 + 192]
                    hidden[:, base + (1 - c) * 192 : base + (1 - c) * 192 + 192] = jnp.concatenate(
                        [got[128:], got[:128]], axis=0
                    )

    def dot(k, w):
        return lax.dot_general(
            hidden[:, k * 384 : k * 384 + 384], w, (((1,), (1,)), ((), ())), preferred_element_type=F32
        )

    blocks = []
    for r in range(NZ):
        front, rear = (pieces[4], pieces[8]) if r == 4 else (pieces[r], pieces[r])
        base = 0 if r == 4 else 256
        total = dot(0, front[0:128]) + dot(1, front[128:256])
        blocks.append(total + dot(2, rear[base : base + 128]) + dot(3, rear[base + 128 : base + 256]))
    for y in range(2):
        part = jnp.concatenate([b[:, y * 64 : y * 64 + 64] for b in blocks], axis=1)
        out[:, y * 512 : y * 512 + 512] = pltpu.roll(part, where[1] * 64, 1)


def down(where, hidden, pieces):
    return pl.pallas_call(
        down_body,
        out_shape=jax.ShapeDtypeStruct((256, 1024), F32),
        in_specs=[whole(pltpu.SMEM)] + [whole()] * (len(hidden) + len(pieces)),
        out_specs=whole(),
        scratch_shapes=[VMEM((256, 1536), BF16)],
        compiler_params=pltpu.CompilerParams(vmem_limit_bytes=12 << 20),
        cost_estimate=pl.CostEstimate(flops=2 * 256 * 1536 * 1024, bytes_accessed=5 << 20, transcendentals=0),
        name="down",
    )(where, *hidden, *pieces)


def mix_body(theirs, where, rows, info, slot_route, limit, *refs):
    out, done, sent = refs[-3:]
    slot = lax.broadcasted_iota(I32, (CAP, 1), 0).astype(F32)
    scale = jnp.where(slot < limit[0:1, 0:1], slot_route[:, 0:1], 0.0)
    one_hot = table(info).astype(BF16)
    column = 1 - where[3] if theirs else where[3]
    n = one_hot.shape[1]
    copies = []
    for y in range(2):
        scaled = (rows[0:CAP, y * 512 : y * 512 + 512] * scale).astype(BF16)
        for t in range(0, n, 256):
            mixed = lax.dot_general(
                one_hot[:, t : t + 256], scaled, (((0,), (0,)), ((), ())), preferred_element_type=F32
            )
            done[y, t : t + 256, :] = mixed.astype(BF16)
            if t % 512 == 256:
                part = pl.ds(t - 256, 512)
                at = pl.multiple_of(y * 1024 + column * 512, 512)
                copies.append(
                    pltpu.make_async_copy(
                        done.at[y, part, :], out.at[part, pl.ds(at, 512)], sent.at[2 * y + t // 512]
                    )
                )
                copies[-1].start()
    for copy in copies:
        copy.wait()


def mix(where, rows, info, slot_route, limit, half=None):
    n = info.shape[1]
    extra = () if half is None else (half,)
    return pl.pallas_call(
        functools.partial(mix_body, half is not None),
        out_shape=jax.ShapeDtypeStruct((n, 2048), BF16),
        in_specs=[whole(pltpu.SMEM)] + [whole()] * 4 + [whole(pltpu.HBM)] * len(extra),
        out_specs=whole(pltpu.HBM),
        scratch_shapes=[VMEM((2, n, 512), BF16), pltpu.SemaphoreType.DMA((4,))],
        input_output_aliases={} if half is None else {5: 0},
        compiler_params=pltpu.CompilerParams(vmem_limit_bytes=12 << 20),
        cost_estimate=pl.CostEstimate(flops=2 * n * CAP * 1024, bytes_accessed=3 << 20, transcendentals=0),
        name="mix_own" if half is None else "mix_rest",
    )(where, rows, info, slot_route, limit, *extra)


def with_counts(units):
    return jnp.concatenate([u[:128] for u in units] + [u[128:] for u in units], axis=0)


def together(*arrays):
    return lax.optimization_barrier(arrays)


def HIDDEN_FAR(a):
    pairs = [(k, 3 - k) for k in range(4)]
    return lax.ppermute(a, ("xl", "ha"), pairs)


def per_device(tokens, expert_ids, keep_mask, route_weight, gate_weight, up_weight, down_weight):
    y, xl, z, c, ha = (lax.axis_index(a) for a in ("y", "xl", "z", "c", "ha"))
    me = y * 32 + xl * 16 + z * 2 + c
    shift = lax.rem(2 * ha - y + NY, NY)
    where = jnp.stack([y, z, xl, c, me, lax.axis_size(WA) * CAP // 2])
    sources = (expert_ids.T, keep_mask.T, route_weight.T, gate_weight, up_weight, down_weight)
    info, packed = prep(where, *(pltpu.with_memory_space_constraint(a, pltpu.HBM) for a in sources))
    both = [(k, 3 - k) for k in range(4)]
    tiles = [packed[0], C(packed[1]), XL(packed[2]), lax.ppermute(packed[3], ("xl", "c"), both)]
    tiles = [jnp.where(c == 0, tiles[k], tiles[k ^ 1]) for k in range(4)]
    arrived = jnp.stack([jnp.where(xl == 0, tiles[k], tiles[k ^ 2]) for k in range(4)])
    slot_rows, slot_route, info = gather_rows(where, pltpu.with_memory_space_constraint(tokens, pltpu.HBM), info)

    lane = lax.broadcasted_iota(I32, (8, 384), 1)
    tile = jnp.zeros((8, 384), BF16)
    for j in range(4):
        tile = jnp.where(lane == j, arrived[j, 32:40], tile)
    unit = jnp.concatenate([arrived[:, :32].reshape(128, 384), tile], axis=0)
    picked = lax.dynamic_slice_in_dim(arrived, 2 * c, 2, axis=0)[:, 40:]
    rows = jnp.concatenate([picked[0, :32], picked[1, :32], picked[0, 32:], picked[1, 32:]], axis=0)

    b1, a1 = Z(1)(unit), Z(-1)(unit)
    d_back, d_ahead, d_far = Y(1)(rows), Y(-1)(rows), Y(2)(rows)
    b1, a1, d_back, d_ahead, d_far = together(b1, a1, d_back, d_ahead, d_far)
    b2, a2 = Z(1)(b1), Z(-1)(a1)

    turned = [rows, d_ahead, d_far, d_back]
    ordered = []
    for j in range(4):
        pick = turned[j]
        for s in range(1, 4):
            pick = jnp.where(shift == s, turned[(j + s) % 4], pick)
        ordered.append(pick)

    def halves(p, q):
        return jnp.concatenate([p[:64], q[:64], p[64:], q[64:]], axis=0)

    d_swap = HA(halves(ordered[2], ordered[3]))
    core_rows = C(slot_rows)
    b2, a2, d_swap, core_rows, slot_rows = together(b2, a2, d_swap, core_rows, slot_rows)
    neighbour_rows = across_x(slot_rows)

    d0 = jnp.concatenate([halves(ordered[0], ordered[1]), d_swap], axis=0)
    up1, dn1 = Z(1)(jnp.concatenate([d0, b2], axis=0)), Z(-1)(jnp.concatenate([d0, a2], axis=0))
    first = with_counts([unit, b1, a1, b2, a2])
    f_back, f_ahead = Y(1)(first), Y(-1)(first)
    up1, dn1 = together(up1, dn1)
    f_back, f_ahead, neighbour_rows = together(f_back, f_ahead, neighbour_rows)

    up2, dn2 = Z(1)(up1[:576]), Z(-1)(jnp.concatenate([dn1[:512], dn1[576:]], axis=0))
    second = with_counts([up1[512:], dn1[512:]])
    g_back = Y(1)(jnp.concatenate([second[:256], f_back[:384], second[256:]], axis=0))
    g_ahead = Y(-1)(jnp.concatenate([second[:256], f_ahead[384:640], second[256:], f_ahead[640:]], axis=0))
    far_rows = C(neighbour_rows)
    up2, dn2 = together(up2, dn2)
    g_back, g_ahead, far_rows = together(g_back, g_ahead, far_rows)

    last = jnp.concatenate([up2[512:], dn2[512:]], axis=0)
    up3, dn3 = Z(1)(up2[:512]), Z(-1)(dn2[:512])
    k_back = Y(1)(jnp.concatenate([last[:128], g_back[:128], last[128:]], axis=0))
    k_ahead = Y(-1)(jnp.concatenate([last[:128], g_ahead[128:256], last[128:], g_ahead[512:528]], axis=0))
    k_far = Y(2)(last)
    near = (first, second, last, f_back, f_ahead, g_back, g_ahead)
    partial, x_far = gate_up_near(*near, slot_rows, core_rows, neighbour_rows, far_rows)
    k_back, k_ahead, k_far, partial, x_far = together(k_back, k_ahead, k_far, partial, x_far)
    up3, dn3 = together(up3, dn3)

    de0, de1 = Z(1)(up3[:256]), Z(-1)(dn3[256:])
    h_own, h_other, limit = gate_up_far(where, partial, x_far, k_back, k_ahead, k_far, *near)
    h_near, h_ha, h_far = XL(h_other), HA(h_own), HIDDEN_FAR(h_other)
    h_near, h_ha, h_far, de0, de1 = together(h_near, h_ha, h_far, de0, de1)
    core = C(jnp.concatenate([h_own, h_near, h_ha, h_far], axis=1))
    pieces = [d0, dn1, dn2, dn3, de0, up3, up2, up1, de1]
    total = down(where, (h_own, h_near, h_ha, h_far, core), pieces)
    other = C(total[128:])
    half = mix(where, total, info, slot_route, limit)
    return mix(where, other, info, slot_route, limit, half)


def solution(mesh):
    finer = Mesh(mesh.devices.reshape(NY, 2, NZ, 2, mesh.shape["ha"]), ("y", "xl", "z", "c", "ha"))
    placed = (P(WA, None),) * 4 + (P(WA, "ha"),) * 3
    return jax.shard_map(per_device, mesh=finer, in_specs=placed, out_specs=P(WA, "ha"), check_vma=False)
```

```python
import functools

import jax
import jax.numpy as jnp
from jax import lax
from jax.experimental import pallas as pl
from jax.experimental.pallas import tpu as pltpu
from jax.sharding import Mesh
from jax.sharding import PartitionSpec as P

CAP = 128
WA = ("y", "xl", "z", "c")
NY, NZ = 4, 8
F32, BF16, I32 = jnp.float32, jnp.bfloat16, jnp.int32
VMEM = pltpu.VMEM


def whole(memory_space=VMEM):
    return pl.BlockSpec(memory_space=memory_space)


def ring(axis, n, k):
    return lambda a: lax.ppermute(a, axis, [(i, (i + k) % n) for i in range(n)])


def Z(k):
    return ring("z", NZ, k)


def Y(k):
    return ring("y", NY, k)


def C(a):
    return lax.ppermute(a, "c", [(0, 1), (1, 0)])


def XL(a):
    return lax.ppermute(a, "xl", [(0, 1), (1, 0)])


def HA(a):
    return lax.ppermute(a, "ha", [(0, 1), (1, 0)])


def across_x(a):
    def at(x, c):
        return (x % 2) * 4 + c * 2 + x // 2

    pairs = [(at(x, c), at((x + 1 - 2 * c) % 4, c)) for x in range(4) for c in range(2)]
    return lax.ppermute(a, ("xl", "c", "ha"), pairs)


def prep_body(*refs):
    where, far, (info, packed), near, arrive = refs[0], refs[1:7], refs[7:9], refs[9:15], refs[15]
    copies = [pltpu.make_async_copy(f, n, arrive.at[i]) for i, (f, n) in enumerate(zip(far, near))]
    for copy in copies:
        copy.start()
    for copy in copies:
        copy.wait()
    ids, keep, rw, gate, up, down_rows = near
    hit = (ids[...] == 0) & (keep[...] == 1)
    chosen = jnp.max(jnp.where(hit, 1.0, 0.0), axis=0, keepdims=True)
    route = jnp.sum(jnp.where(hit, rw[...], 0.0), axis=0, keepdims=True)
    n = chosen.shape[1]
    row = lax.broadcasted_iota(I32, (n, n), 0)
    col = lax.broadcasted_iota(I32, (n, n), 1)
    before = jnp.where(row < col, 1.0, 0.0).astype(BF16)
    ones = jnp.broadcast_to(chosen, (16, n)).astype(BF16)
    position = jnp.dot(ones, before, preferred_element_type=F32)[:1]
    info[0:1, :] = position
    info[1:2, :] = chosen
    info[2:3, :] = route
    info[3:8, :] = jnp.zeros((5, n), F32)
    total = jnp.sum(chosen, axis=1, keepdims=True)
    for q in range(4):
        at = slice(q * 192, q * 192 + 192)
        to = where[2] * 2 + where[3]
        to = q + to - 2 * (q & to)
        packed[to, 0:32, :] = jnp.concatenate([gate[:, at], up[:, at]], axis=1)
        packed[to, 32:40, :] = jnp.broadcast_to(total, (8, 384)).astype(BF16)
        packed[to, 40:72, :] = down_rows[:, :384]
        packed[to, 72:104, :] = down_rows[:, 384:]


def prep(where, ids, keep, rw, gate, up, down_rows):
    n = ids.shape[1]
    return pl.pallas_call(
        prep_body,
        out_shape=(jax.ShapeDtypeStruct((8, n), F32), jax.ShapeDtypeStruct((4, 104, 384), BF16)),
        in_specs=[whole(pltpu.SMEM)] + [whole(pltpu.HBM)] * 6,
        out_specs=(whole(), whole()),
        scratch_shapes=[VMEM(a.shape, a.dtype) for a in (ids, keep, rw, gate, up, down_rows)]
        + [pltpu.SemaphoreType.DMA((6,))],
        compiler_params=pltpu.CompilerParams(vmem_limit_bytes=12 << 20),
        cost_estimate=pl.CostEstimate(flops=2 * 16 * n * n, bytes_accessed=4 * 32 * n, transcendentals=0),
        name="prep",
    )(where, ids, keep, rw, gate, up, down_rows)


def table(info):
    slot = lax.broadcasted_iota(I32, (CAP, info.shape[1]), 0).astype(F32)
    return (info[0:1, :] == slot) & (info[1:2, :] > 0.5)


def gather_body(where, tokens, info, out, slot_route, near, arrive):
    n, width = near.shape[1:]
    copies = [
        pltpu.make_async_copy(tokens.at[:, i * width : (i + 1) * width], near.at[i], arrive.at[i]) for i in range(NY)
    ]
    for copy in copies:
        copy.start()
    picked = table(info)
    got = jnp.sum(jnp.where(picked, info[2:3, :], 0.0), axis=1, keepdims=True)
    slot_route[...] = jnp.broadcast_to(got, slot_route.shape)
    one_hot = picked.astype(BF16)
    for block in range(NY):
        copies[block].wait()
        rows = jnp.dot(one_hot, near[block], preferred_element_type=F32).astype(BF16)
        ky = lax.rem(block - where[0] + NY, NY)
        yi = jnp.where(ky == 0, 0, jnp.where(ky == 3, 1, jnp.where(ky == 1, 2, 3)))
        for z in range(NZ):
            kz = lax.rem(z - where[1] + NZ, NZ)
            zi = jnp.where(kz == 0, 0, jnp.where(kz <= 3, 2 * kz, jnp.where(kz == 4, 7, 15 - 2 * kz)))
            piece = jnp.concatenate([rows[:, z * 64 : z * 64 + 64], rows[:, 512 + z * 64 : 576 + z * 64]], axis=1)
            out[:, pl.ds(pl.multiple_of((yi * NZ + zi) * 128, 128), 128)] = piece


def gather_rows(where, tokens, info):
    n, d = tokens.shape
    return pl.pallas_call(
        gather_body,
        out_shape=(jax.ShapeDtypeStruct((CAP, d), BF16), jax.ShapeDtypeStruct((CAP, 128), F32)),
        in_specs=[whole(pltpu.SMEM), whole(pltpu.HBM), whole()],
        out_specs=(whole(), whole()),
        scratch_shapes=[VMEM((NY, n, d // NY), tokens.dtype), pltpu.SemaphoreType.DMA((NY,))],
        compiler_params=pltpu.CompilerParams(vmem_limit_bytes=16 << 20),
        cost_estimate=pl.CostEstimate(flops=2 * CAP * n * d, bytes_accessed=2 * n * d, transcendentals=0),
        name="gather_rows",
    )(where, tokens, info)


def near_body(first, second, last, f_back, f_ahead, g_back, g_ahead, xo, xc, xn, xnc, total, x_far, x_all):
    for i, ref in enumerate((xo, xc, xn, xnc)):
        at = slice(i * 128, i * 128 + 128)
        x_all[at, :] = ref[:, :3712]
        x_far[at, 0:128] = ref[:, 1920:2048]
        x_far[at, 128:256] = ref[:, 2944:3072]
        x_far[at, 256:640] = ref[:, 3712:]
    acc = jnp.zeros((512, 384), F32)
    for start, ref, row, size in (
        (0, first, 0, 640),
        (640, second, 0, 256),
        (896, last, 0, 128),
        (1024, f_back, 0, 640),
        (1664, g_back, 0, 256),
        (2048, f_ahead, 0, 640),
        (2688, g_ahead, 0, 256),
        (3072, g_back, 256, 384),
        (3456, g_ahead, 256, 256),
    ):
        acc += jnp.dot(x_all[:, start : start + size], ref[row : row + size, :], preferred_element_type=F32)
    total[...] = acc


def gate_up_near(*arrays):
    return pl.pallas_call(
        near_body,
        out_shape=(jax.ShapeDtypeStruct((512, 384), F32), jax.ShapeDtypeStruct((512, 640), BF16)),
        in_specs=[whole()] * len(arrays),
        out_specs=(whole(), whole()),
        scratch_shapes=[VMEM((512, 3712), BF16)],
        compiler_params=pltpu.CompilerParams(vmem_limit_bytes=16 << 20),
        cost_estimate=pl.CostEstimate(flops=2 * 512 * 3456 * 384, bytes_accessed=8 << 20, transcendentals=0),
        name="gate_up_near",
    )(*arrays)


def far_body(where, total, x_far, k_back, k_ahead, k_far, *refs):
    (first, second, last, f_back, f_ahead, g_back, g_ahead), (own, other, limit) = refs[:7], refs[7:]
    acc = total[...]
    for start, ref, row in ((0, k_back, 0), (128, k_ahead, 0), (256, k_back, 128), (384, k_ahead, 128), (512, k_far, 0)):
        acc += jnp.dot(x_far[:, start : start + 128], ref[row : row + 128, :], preferred_element_type=F32)
    gate, up = acc[:, :192], acc[:, 192:]
    hidden = (gate * jax.nn.sigmoid(gate) * up).astype(BF16)
    own[...] = hidden[:256]
    other[...] = hidden[256:]

    lane = lax.broadcasted_iota(I32, (8, 128), 1)
    quad = lax.shift_right_logical(lane, 1) * 16 + (lane & 1)
    earlier = jnp.zeros((8, 128), F32)
    groups = (
        (0, first[640:680, 0:128], second[256:272, 0:128], last[128:136, 0:128]),
        (3, f_back[640:680, 0:128], g_back[640:656, 0:128], k_back[256:264, 0:128]),
        (1, f_ahead[640:680, 0:128], g_ahead[512:528, 0:128], k_ahead[256:264, 0:128]),
        (2, g_ahead[528:568, 0:128], k_ahead[264:280, 0:128], k_far[128:136, 0:128]),
    )
    for ky, *parts in groups:
        tiles = jnp.concatenate([part.astype(F32) for part in parts], axis=0)
        for zi, kz in enumerate((0, 7, 1, 6, 2, 5, 3, 4)):
            block = ((where[0] + ky) & 3) * 32 + ((where[1] + kz) & 7) * 2 + quad
            counted = (block < where[4]) & (lane < 4)
            earlier += jnp.where(counted, tiles[zi * 8 : zi * 8 + 8], 0.0)
    before = jnp.sum(earlier[0:1], axis=1, keepdims=True)
    limit[...] = jnp.broadcast_to(where[5].astype(F32) - before, limit.shape)


def gate_up_far(*arrays):
    half = jax.ShapeDtypeStruct((256, 192), BF16)
    return pl.pallas_call(
        far_body,
        out_shape=(half, half, jax.ShapeDtypeStruct((8, 128), F32)),
        in_specs=[whole(pltpu.SMEM)] + [whole()] * (len(arrays) - 1),
        out_specs=(whole(), whole(), whole()),
        compiler_params=pltpu.CompilerParams(vmem_limit_bytes=16 << 20),
        cost_estimate=pl.CostEstimate(flops=2 * 512 * 640 * 384, bytes_accessed=3 << 20, transcendentals=512 * 192),
        name="gate_up_far",
    )(*arrays)


def down_body(where, own, near, ha, far, core, *refs):
    pieces, (out, hidden) = refs[:-2], refs[-2:]

    for xl in range(2):
        for c in range(2):

            @pl.when((where[2] == xl) & (where[3] == c))
            def _():
                for k, ref in enumerate((own, near, ha, far)):
                    pair = xl if k % 2 == 0 else 1 - xl
                    base = (k // 2) * 768 + pair * 384
                    hidden[:, base + c * 192 : base + c * 192 + 192] = ref[...]
                    got = core[:, k * 192 : k * 192 + 192]
                    hidden[:, base + (1 - c) * 192 : base + (1 - c) * 192 + 192] = jnp.concatenate(
                        [got[128:], got[:128]], axis=0
                    )

    def dot(k, w):
        return lax.dot_general(
            hidden[:, k * 384 : k * 384 + 384], w, (((1,), (1,)), ((), ())), preferred_element_type=F32
        )

    blocks = []
    for r in range(NZ):
        front, rear = (pieces[4], pieces[8]) if r == 4 else (pieces[r], pieces[r])
        base = 0 if r == 4 else 256
        total = dot(0, front[0:128]) + dot(1, front[128:256])
        blocks.append(total + dot(2, rear[base : base + 128]) + dot(3, rear[base + 128 : base + 256]))
    for y in range(2):
        part = jnp.concatenate([b[:, y * 64 : y * 64 + 64] for b in blocks], axis=1)
        out[:, y * 512 : y * 512 + 512] = pltpu.roll(part, where[1] * 64, 1)


def down(where, hidden, pieces):
    return pl.pallas_call(
        down_body,
        out_shape=jax.ShapeDtypeStruct((256, 1024), F32),
        in_specs=[whole(pltpu.SMEM)] + [whole()] * (len(hidden) + len(pieces)),
        out_specs=whole(),
        scratch_shapes=[VMEM((256, 1536), BF16)],
        compiler_params=pltpu.CompilerParams(vmem_limit_bytes=12 << 20),
        cost_estimate=pl.CostEstimate(flops=2 * 256 * 1536 * 1024, bytes_accessed=5 << 20, transcendentals=0),
        name="down",
    )(where, *hidden, *pieces)


def mix_body(theirs, where, rows, info, slot_route, limit, *refs):
    out, done, sent = refs[-3:]
    slot = lax.broadcasted_iota(I32, (CAP, 1), 0).astype(F32)
    scale = jnp.where(slot < limit[0:1, 0:1], slot_route[:, 0:1], 0.0)
    one_hot = table(info).astype(BF16)
    column = 1 - where[3] if theirs else where[3]
    n = one_hot.shape[1]
    copies = []
    for y in range(2):
        scaled = (rows[0:CAP, y * 512 : y * 512 + 512] * scale).astype(BF16)
        for t in range(0, n, 256):
            mixed = lax.dot_general(
                one_hot[:, t : t + 256], scaled, (((0,), (0,)), ((), ())), preferred_element_type=F32
            )
            done[y, t : t + 256, :] = mixed.astype(BF16)
            if t % 512 == 256:
                part = pl.ds(t - 256, 512)
                at = pl.multiple_of(y * 1024 + column * 512, 512)
                copies.append(
                    pltpu.make_async_copy(
                        done.at[y, part, :], out.at[part, pl.ds(at, 512)], sent.at[2 * y + t // 512]
                    )
                )
                copies[-1].start()
    for copy in copies:
        copy.wait()


def mix(where, rows, info, slot_route, limit, half=None):
    n = info.shape[1]
    extra = () if half is None else (half,)
    return pl.pallas_call(
        functools.partial(mix_body, half is not None),
        out_shape=jax.ShapeDtypeStruct((n, 2048), BF16),
        in_specs=[whole(pltpu.SMEM)] + [whole()] * 4 + [whole(pltpu.HBM)] * len(extra),
        out_specs=whole(pltpu.HBM),
        scratch_shapes=[VMEM((2, n, 512), BF16), pltpu.SemaphoreType.DMA((4,))],
        input_output_aliases={} if half is None else {5: 0},
        compiler_params=pltpu.CompilerParams(vmem_limit_bytes=12 << 20),
        cost_estimate=pl.CostEstimate(flops=2 * n * CAP * 1024, bytes_accessed=3 << 20, transcendentals=0),
        name="mix_own" if half is None else "mix_rest",
    )(where, rows, info, slot_route, limit, *extra)


def with_counts(units):
    return jnp.concatenate([u[:128] for u in units] + [u[128:] for u in units], axis=0)


def together(*arrays):
    return lax.optimization_barrier(arrays)


def HIDDEN_FAR(a):
    pairs = [(k, 3 - k) for k in range(4)]
    return lax.ppermute(a, ("xl", "ha"), pairs)


def per_device(tokens, expert_ids, keep_mask, route_weight, gate_weight, up_weight, down_weight):
    y, xl, z, c, ha = (lax.axis_index(a) for a in ("y", "xl", "z", "c", "ha"))
    me = y * 32 + xl * 16 + z * 2 + c
    shift = lax.rem(2 * ha - y + NY, NY)
    where = jnp.stack([y, z, xl, c, me, lax.axis_size(WA) * CAP // 2])
    sources = (expert_ids.T, keep_mask.T, route_weight.T, gate_weight, up_weight, down_weight)
    info, packed = prep(where, *(pltpu.with_memory_space_constraint(a, pltpu.HBM) for a in sources))
    both = [(k, 3 - k) for k in range(4)]
    tiles = [packed[0], C(packed[1]), XL(packed[2]), lax.ppermute(packed[3], ("xl", "c"), both)]
    tiles = [jnp.where(c == 0, tiles[k], tiles[k ^ 1]) for k in range(4)]
    arrived = jnp.stack([jnp.where(xl == 0, tiles[k], tiles[k ^ 2]) for k in range(4)])
    slot_rows, slot_route = gather_rows(where, pltpu.with_memory_space_constraint(tokens, pltpu.HBM), info)

    lane = lax.broadcasted_iota(I32, (8, 384), 1)
    tile = jnp.zeros((8, 384), BF16)
    for j in range(4):
        tile = jnp.where(lane == j, arrived[j, 32:40], tile)
    unit = jnp.concatenate([arrived[:, :32].reshape(128, 384), tile], axis=0)
    picked = lax.dynamic_slice_in_dim(arrived, 2 * c, 2, axis=0)[:, 40:]
    rows = jnp.concatenate([picked[0, :32], picked[1, :32], picked[0, 32:], picked[1, 32:]], axis=0)

    b1, a1 = Z(1)(unit), Z(-1)(unit)
    d_back, d_ahead, d_far = Y(1)(rows), Y(-1)(rows), Y(2)(rows)
    b1, a1, d_back, d_ahead, d_far = together(b1, a1, d_back, d_ahead, d_far)
    b2, a2 = Z(1)(b1), Z(-1)(a1)

    turned = [rows, d_ahead, d_far, d_back]
    ordered = []
    for j in range(4):
        pick = turned[j]
        for s in range(1, 4):
            pick = jnp.where(shift == s, turned[(j + s) % 4], pick)
        ordered.append(pick)

    def halves(p, q):
        return jnp.concatenate([p[:64], q[:64], p[64:], q[64:]], axis=0)

    d_swap = HA(halves(ordered[2], ordered[3]))
    core_rows = C(slot_rows)
    b2, a2, d_swap, core_rows, slot_rows = together(b2, a2, d_swap, core_rows, slot_rows)
    neighbour_rows = across_x(slot_rows)

    d0 = jnp.concatenate([halves(ordered[0], ordered[1]), d_swap], axis=0)
    up1, dn1 = Z(1)(jnp.concatenate([d0, b2], axis=0)), Z(-1)(jnp.concatenate([d0, a2], axis=0))
    first = with_counts([unit, b1, a1, b2, a2])
    f_back, f_ahead = Y(1)(first), Y(-1)(first)
    up1, dn1 = together(up1, dn1)
    f_back, f_ahead, neighbour_rows = together(f_back, f_ahead, neighbour_rows)

    up2, dn2 = Z(1)(up1[:576]), Z(-1)(jnp.concatenate([dn1[:512], dn1[576:]], axis=0))
    second = with_counts([up1[512:], dn1[512:]])
    g_back = Y(1)(jnp.concatenate([second[:256], f_back[:384], second[256:]], axis=0))
    g_ahead = Y(-1)(jnp.concatenate([second[:256], f_ahead[384:640], second[256:], f_ahead[640:]], axis=0))
    far_rows = C(neighbour_rows)
    up2, dn2, far_rows = together(up2, dn2, far_rows)
    g_back, g_ahead, far_rows = together(g_back, g_ahead, far_rows)

    last = jnp.concatenate([up2[512:], dn2[512:]], axis=0)
    up3, dn3 = Z(1)(up2[:512]), Z(-1)(dn2[:512])
    k_back = Y(1)(jnp.concatenate([last[:128], g_back[:128], last[128:]], axis=0))
    k_ahead = Y(-1)(jnp.concatenate([last[:128], g_ahead[128:256], last[128:], g_ahead[512:528]], axis=0))
    k_far = Y(2)(last)
    near = (first, second, last, f_back, f_ahead, g_back, g_ahead)
    partial, x_far = gate_up_near(*near, slot_rows, core_rows, neighbour_rows, far_rows)
    k_back, k_ahead, k_far, partial, x_far = together(k_back, k_ahead, k_far, partial, x_far)
    up3, dn3 = together(up3, dn3)

    de0, de1 = Z(1)(up3[:256]), Z(-1)(dn3[256:])
    h_own, h_other, limit = gate_up_far(where, partial, x_far, k_back, k_ahead, k_far, *near)
    h_near, h_ha, h_far = XL(h_other), HA(h_own), HIDDEN_FAR(h_other)
    h_near, h_ha, h_far, de0, de1 = together(h_near, h_ha, h_far, de0, de1)
    core = C(jnp.concatenate([h_own, h_near, h_ha, h_far], axis=1))
    pieces = [d0, dn1, dn2, dn3, de0, up3, up2, up1, de1]
    total = down(where, (h_own, h_near, h_ha, h_far, core), pieces)
    other = C(total[128:])
    half = mix(where, total, info, slot_route, limit)
    return mix(where, other, info, slot_route, limit, half)


def solution(mesh):
    finer = Mesh(mesh.devices.reshape(NY, 2, NZ, 2, mesh.shape["ha"]), ("y", "xl", "z", "c", "ha"))
    placed = (P(WA, None),) * 4 + (P(WA, "ha"),) * 3
    return jax.shard_map(per_device, mesh=finer, in_specs=placed, out_specs=P(WA, "ha"), check_vma=False)
```
